256 devices in a mesh: table: 16 (over x, y), dp: 8 (over z), col: 2 (over core).
Axes of the slice: x: 4, y: 4, z: 8, core: 2. Of those that a mesh axis runs over, the one named last changes fastest.
Arguments:
- table_weights: float32 [32768, 512], P('table', 'col'), may hold values from -6 to 6
- moment_first: float32 [32768, 512], P('table', 'col'), may hold values from -3 to 3
- moment_second: float32 [32768], P('table'), may hold values from 0.1 to 2
- hot_slices: int32 [16, 2], replicated, may hold values from 0 to 31, as said below
- upstream_grad: bfloat16 [131072, 512], P(('table', 'dp'), 'col'), may hold values from -20 to 20
- dedup_map: int32 [131072, 32], P(('table', 'dp')), may hold values from 0 to 4095, as said below
- unique_rows: int32 [128, 16, 256], P(('table', 'dp')), may hold values from 0 to 32767, as said below
- row_counts: int32 [128, 16], P(('table', 'dp')), may hold values from 192 to 256, as said below
Outputs:
- new_weights: float32 [32768, 512], P('table', 'col')
- new_first: float32 [32768, 512], P('table', 'col')
- new_second: float32 [32768], P('table')
The draws below stay inside these ranges and needn't reach their ends.
Inputs may be any that keep to these rules, and one draw needn't show every extreme that they name: `hot_slices`: each row holds 2 different slice numbers below 32. `unique_rows`: for source device s and owner t, the first row_counts[s, t] entries are different rows r with physical(r) on table index t; the remaining entries are not used. `row_counts`: in every draw some owner receives 256 used slots from every source device. `dedup_map`: an entry in a row of source device s is a used slot t * 256 + k with k < row_counts[s, t].
All inputs are finite; a program needn't handle non-finite values.
Results may differ from the reference program's by a relative error of at most 0.0003.
Values sent between devices are 32-bit elements; how exact they have to be, the bound alone decides.
No kernel may reach another device: no remote copies, remote signals or barrier semaphores. Data moves between devices by JAX's collectives and lax.ppermute only.
A program may use at most 64 MiB of HBM per device.

```python
import math
import jax
import jax.numpy as jnp
from jax import lax

E = 512
R_DEV = 2048
SLICE = 64
HOTS = 2
CAP = 256
B_DEV = 1024
BAG = 32
ROWS = 32768
SLOTS = 4096
N_TABLE = 16
N_DP = 8


def int_layout(key):
    n_slices = R_DEV // SLICE
    hot_keys = jax.random.split(jax.random.fold_in(key, 101), N_TABLE)
    hot = jax.vmap(lambda row_key: jax.random.permutation(row_key, n_slices)[:HOTS])(hot_keys).astype(jnp.int32)
    first_row = jax.random.permutation(jax.random.fold_in(key, 107), n_slices - 1)[:HOTS - 1]
    first_row = jnp.concatenate([jnp.full((1,), n_slices - 1, jnp.int32), first_row.astype(jnp.int32)])
    hot = hot.at[0].set(first_row).astype(jnp.int32)
    sources = N_TABLE * N_DP
    counts = jax.random.randint(jax.random.fold_in(key, 102), (sources, N_TABLE), CAP - CAP // 4, CAP + 1)
    busiest = jax.random.randint(jax.random.fold_in(key, 103), (), 0, N_TABLE)
    counts = jnp.where(jnp.arange(N_TABLE)[None, :] == busiest, CAP, counts)
    counts = counts.at[0, N_TABLE - 1].set(CAP).astype(jnp.int32)
    place_keys = jax.random.split(jax.random.fold_in(key, 104), sources * N_TABLE)
    places = jax.vmap(lambda row_key: jax.random.permutation(row_key, R_DEV)[:CAP])(place_keys)
    places = places.reshape(sources, N_TABLE, CAP).astype(jnp.int32)
    last_piece = n_slices - 1
    last_match = hot[N_TABLE - 1] == last_piece
    last_partner = (N_TABLE - 1 + N_TABLE // 2) % N_TABLE
    last_partner_piece = jnp.sum(jnp.where(last_match, hot[last_partner], 0))
    is_moved = jnp.any(last_match)
    last_owner = jnp.where(is_moved, last_partner, N_TABLE - 1).astype(jnp.int32)
    last_place = jnp.where(is_moved, last_partner_piece * SLICE + SLICE - 1, R_DEV - 1).astype(jnp.int32)
    full_perm = jax.random.permutation(jax.random.fold_in(key, 108), R_DEV).astype(jnp.int32)
    where_last = jnp.argmax(full_perm == last_place).astype(jnp.int32)
    full_perm = full_perm.at[where_last].set(full_perm[0]).at[0].set(last_place)
    places = places.at[0, last_owner].set(full_perm[:CAP])
    row_owner = jnp.broadcast_to(jnp.arange(N_TABLE)[None, :, None], places.shape).astype(jnp.int32)
    row_piece = places // SLICE
    row_offset = places % SLICE
    matches = hot[row_owner] == row_piece[..., None]
    partner = (row_owner + N_TABLE // 2) % N_TABLE
    partner_piece = jnp.sum(jnp.where(matches, hot[partner], 0), axis=-1)
    logical = jnp.where(jnp.any(matches, axis=-1), partner * R_DEV + partner_piece * SLICE + row_offset, row_owner * R_DEV + places)
    dest = jax.random.randint(jax.random.fold_in(key, 105), (sources, B_DEV, BAG), 0, N_TABLE)
    limit = counts[jnp.arange(sources)[:, None, None], dest]
    slot = jax.random.randint(jax.random.fold_in(key, 106), (sources, B_DEV, BAG), 0, limit)
    dedup = dest * CAP + slot
    dedup = dedup.at[0, 0, 0].set(N_TABLE * CAP - 1)
    dedup = dedup.reshape(sources * B_DEV, BAG)
    return (hot, counts, logical.astype(jnp.int32), dedup.astype(jnp.int32))


def draw_hot_slices(key, part):
    return int_layout(key)[0]


def draw_row_counts(key, part):
    return int_layout(key)[1]


def draw_unique_rows(key, part):
    return int_layout(key)[2]


def draw_dedup_map(key, part):
    return int_layout(key)[3]


def draw_upstream_grad(key, part):
    batch = B_DEV * N_TABLE * N_DP
    base_key, col_key, row_key = jax.random.split(key, 3)
    columns = jnp.arange(E).astype(jnp.float32)
    ramp = jnp.sqrt(1.0 + 2.0 * columns / (E - 1))
    col_scale = jnp.exp(jax.random.uniform(col_key, (E,), jnp.float32, -1.2, 1.2))
    row_scale = jnp.exp(jax.random.uniform(row_key, (batch, 1), jnp.float32, -1.2, 1.2))
    base = jnp.clip(jax.random.normal(base_key, (batch, E), jnp.float32), -4.0, 4.0)
    return (0.25 * base * col_scale * row_scale * ramp).astype(jnp.bfloat16)


def steps_of(stream_key, extent, shards, low, high):
    def one(position, blocks):
        draws = jax.random.uniform(jax.random.fold_in(jax.random.fold_in(stream_key, 6), position), (blocks,), jnp.float32, low / len(shards), high / len(shards))
        return jnp.repeat(jnp.exp(draws), extent[position] // blocks).reshape((-1,) + (1,) * (len(extent) - position - 1))

    gain = one(*shards[0])
    for cut in shards[1:]:
        gain = gain * one(*cut)
    return gain


def normal_values(own_key, dims, deviation, bound, shards=(), kind=jnp.bfloat16):
    level = steps_of(own_key, dims, shards, -0.22, 0.18) if shards else 1.0
    values = jax.random.normal(own_key, dims, jnp.float32) * deviation * level
    return jnp.minimum(jnp.maximum(values, -bound), bound).astype(kind)


def setup_inputs(seed: int = 0) -> dict:
    keys = jax.random.split(jax.random.key(seed), 9)
    table_weights = normal_values(keys[0], (ROWS, E), 1.0, 6.0, ((0, 16), (1, 2)), jnp.float32)
    moment_first = normal_values(keys[1], (ROWS, E), 0.5, 3.0, ((0, 16), (1, 2)), jnp.float32)
    moment_second = jnp.clip(jnp.exp(math.log(2.0) - 2.9957323 * jax.random.uniform(keys[2], (ROWS,), jnp.float32) ** steps_of(keys[2], (ROWS,), ((0, 16),), -0.2, 0.2)), 0.1, 2.0)
    hot_slices = draw_hot_slices(jax.random.fold_in(keys[8], 71), 0)
    upstream_grad = draw_upstream_grad(jax.random.fold_in(keys[8], 71), 0)
    dedup_map = draw_dedup_map(jax.random.fold_in(keys[8], 71), 0)
    unique_rows = draw_unique_rows(jax.random.fold_in(keys[8], 71), 0)
    row_counts = draw_row_counts(jax.random.fold_in(keys[8], 71), 0)
    return {"table_weights": table_weights, "moment_first": moment_first, "moment_second": moment_second, "hot_slices": hot_slices, "upstream_grad": upstream_grad, "dedup_map": dedup_map, "unique_rows": unique_rows, "row_counts": row_counts}


beta_one = 0.9
beta_two = 0.99
learn_rate = 0.1
eps_value = 1e-08

def to_physical(rows, hot_slices):
    n_table = hot_slices.shape[0]
    row_owner = rows // R_DEV
    local_row = rows % R_DEV
    row_piece = local_row // SLICE
    row_offset = local_row % SLICE
    matches = hot_slices[row_owner] == row_piece[..., None]
    partner = (row_owner + n_table // 2) % n_table
    partner_piece = lax.optimization_barrier(jnp.sum(jnp.where(matches, hot_slices[partner], 0), axis=-1))
    moved = partner * R_DEV + partner_piece * SLICE + row_offset
    return jnp.where(jnp.any(matches, axis=-1), moved, rows).astype(jnp.int32)

def reference(table_weights, moment_first, moment_second, hot_slices, upstream_grad, dedup_map, unique_rows, row_counts):
    every_row = jnp.arange(ROWS).astype(jnp.int32)
    placed_at = to_physical(every_row, hot_slices)
    placed_weights = jnp.zeros_like(table_weights).at[placed_at].set(table_weights)
    placed_first = jnp.zeros_like(moment_first).at[placed_at].set(moment_first)
    placed_second = jnp.zeros_like(moment_second).at[placed_at].set(moment_second)
    sources = N_TABLE * N_DP
    valid = jnp.arange(CAP)[None, None, :] < row_counts[:, :, None]
    targets = jnp.where(valid, to_physical(unique_rows, hot_slices), ROWS)
    targets = targets.reshape(sources, SLOTS).astype(jnp.int32)
    grads = upstream_grad.reshape(sources, B_DEV, E)
    maps = dedup_map.reshape(sources, B_DEV, BAG)

    def one_source(total, inputs):
        grad_block, map_block, target_block = inputs
        spread = jnp.broadcast_to(grad_block.astype(jnp.float32)[:, None, :], (B_DEV, BAG, E))
        slot_grad = jax.ops.segment_sum(spread.reshape(B_DEV * BAG, E), map_block.reshape(B_DEV * BAG), num_segments=SLOTS)
        return (total.at[target_block].add(slot_grad), None)
    total, _ = lax.scan(one_source, jnp.zeros((ROWS + 1, E), jnp.float32), (grads, maps, targets))
    row_grad = total[:ROWS]
    new_second = beta_two * placed_second + (1.0 - beta_two) * lax.optimization_barrier(jnp.mean(row_grad * row_grad, axis=1))
    new_first = beta_one * placed_first + (1.0 - beta_one) * row_grad
    scaled = jnp.sqrt(new_second / (1.0 - beta_two ** 8)) + eps_value
    new_weights = placed_weights - learn_rate * (new_first / (1.0 - beta_one ** 8)) / scaled[:, None]
    return (new_weights, new_first, new_second)
```

```python
import functools
import jax
import jax.numpy as jnp
from jax import lax
from jax.experimental import pallas as pl
from jax.experimental.pallas import tpu as pltpu
from jax.sharding import PartitionSpec as P

SLICE = 64
LOW = 256
GROUP = 8
TARGET_ROWS = 8

beta_one = 0.9
beta_two = 0.99
learn_rate = 0.1
eps_value = 1e-08

NT = (((1,), (1,)), ((), ()))


def partner_2(block, axis, distance):
    count = lax.axis_size(axis)
    route = []
    for low in range(count):
        high = low | 1 << distance
        if high != low and high < count:
            route += [(low, high), (high, low)]
    return lax.ppermute(block, axis, route)


def one_hot(positions, wanted):
    return jnp.where(positions == wanted, 1.0, 0.0).astype(jnp.bfloat16)


def slot_kernel(map_ref, grad_ref, target_ref, out_ref, tally):
    groups, span = map_ref.shape
    highs = tally.shape[0]
    bag = span // GROUP
    sample = lax.broadcasted_iota(jnp.int32, (1, span), 1) // bag
    left_at = lax.broadcasted_iota(jnp.int32, (highs * GROUP, span), 0)
    right_at = lax.broadcasted_iota(jnp.int32, (LOW, span), 0)

    def count(step, carry):
        first = pl.multiple_of(step * 8, 8)
        slots = map_ref[pl.ds(first, 8), :]
        for pair in range(4):
            halves = []
            for which in range(2):
                at = 2 * pair + which
                row = slots[at : at + 1, :]
                left = one_hot(left_at, (row // LOW) * GROUP + sample)
                right = one_hot(right_at, row % LOW)
                part = lax.dot_general(left, right, NT, preferred_element_type=jnp.float32)
                halves.append(part.reshape(highs, GROUP, LOW))
            both = jnp.concatenate(halves, axis=1).astype(jnp.bfloat16)
            begin = pl.multiple_of(first * GROUP + pair * 2 * GROUP, 2 * GROUP)
            tally[:, pl.ds(begin, 2 * GROUP), :] = both
        return carry

    lax.fori_loop(0, groups // 8, count, 0)
    columns = grad_ref.shape[0]

    def total(owner, carry):
        out_ref[owner, :columns, :] = jnp.dot(
            grad_ref[...], tally[owner], preferred_element_type=jnp.float32
        )
        out_ref[owner, columns:, :] = jnp.broadcast_to(
            target_ref[pl.ds(owner, 1), :], (TARGET_ROWS, LOW)
        )
        return carry

    lax.fori_loop(0, highs, total, 0)


def slot_sums(slots, grad_t, targets):
    highs = targets.shape[0]
    columns, samples = grad_t.shape
    return pl.pallas_call(
        slot_kernel,
        out_shape=jax.ShapeDtypeStruct((highs, columns + TARGET_ROWS, LOW), jnp.float32),
        in_specs=[pl.BlockSpec(memory_space=pltpu.VMEM)] * 3,
        out_specs=pl.BlockSpec(memory_space=pltpu.VMEM),
        scratch_shapes=[pltpu.VMEM((highs, samples, LOW), jnp.bfloat16)],
        compiler_params=pltpu.CompilerParams(vmem_limit_bytes=40 << 20),
        name="slot_sums",
    )(slots, grad_t, targets)


def place_kernel(got_ref, out_ref, select, pieces):
    sources, height, cap = got_ref.shape
    columns = height - TARGET_ROWS
    rows = out_ref.shape[0]
    block = select.shape[0]
    for source in range(sources):
        value = got_ref[source, :columns, :]
        upper = value.astype(jnp.bfloat16)
        lower = (value - upper.astype(jnp.float32)).astype(jnp.bfloat16)
        at = source * cap
        pieces[0, :, at : at + cap] = upper
        pieces[1, :, at : at + cap] = lower
    place = lax.broadcasted_iota(jnp.int32, (block, cap), 0)

    def fill(step, carry):
        start = step * block
        for source in range(sources):
            target = got_ref[source, columns : columns + 1, :].astype(jnp.int32)
            at = source * cap
            select[:, at : at + cap] = one_hot(place, target - start)
        chosen = select[...]
        total = lax.dot_general(chosen, pieces[0], NT, preferred_element_type=jnp.float32)
        total += lax.dot_general(chosen, pieces[1], NT, preferred_element_type=jnp.float32)
        out_ref[pl.ds(pl.multiple_of(start, block), block), :] = total
        return carry

    lax.fori_loop(0, rows // block, fill, 0)


def place_sums(got, rows):
    sources, height, cap = got.shape
    columns = height - TARGET_ROWS
    return pl.pallas_call(
        place_kernel,
        out_shape=jax.ShapeDtypeStruct((rows, columns), jnp.float32),
        in_specs=[pl.BlockSpec(memory_space=pltpu.VMEM)],
        out_specs=pl.BlockSpec(memory_space=pltpu.VMEM),
        scratch_shapes=[
            pltpu.VMEM((512, sources * cap), jnp.bfloat16),
            pltpu.VMEM((2, columns, sources * cap), jnp.bfloat16),
        ],
        compiler_params=pltpu.CompilerParams(vmem_limit_bytes=40 << 20),
        name="place_sums",
    )(got)


def local_targets(unique_rows, row_counts, hot_slices, rows_dev):
    n_table, n_hots = hot_slices.shape
    cap = unique_rows.shape[1]
    partner = (jnp.arange(n_table) + n_table // 2) % n_table
    partner_hot = jnp.concatenate([hot_slices[n_table // 2 :], hot_slices[: n_table // 2]], axis=0)
    local_row = unique_rows % rows_dev
    from_partner = unique_rows // rows_dev == partner[:, None]
    target = local_row
    for k in range(n_hots):
        moved = from_partner & (local_row // SLICE == partner_hot[:, k : k + 1])
        target = jnp.where(moved, hot_slices[:, k : k + 1] * SLICE + local_row % SLICE, target)
    valid = jnp.arange(cap)[None, :] < row_counts[:, None]
    return jnp.where(valid, target, rows_dev)


def adam_rows(weights, first, second, gradient, squares, full_width):
    new_second = beta_two * second + (1.0 - beta_two) * (squares / full_width)
    new_first = beta_one * first + (1.0 - beta_one) * gradient
    scaled = jnp.sqrt(new_second / (1.0 - beta_two**8)) + eps_value
    new_weights = weights - learn_rate * (new_first / (1.0 - beta_one**8)) / scaled[:, None]
    return (new_weights, new_first, new_second)


def on_device(
    table_weights,
    moment_first,
    moment_second,
    hot_slices,
    upstream_grad,
    dedup_map,
    unique_rows,
    row_counts,
):
    n_table = lax.axis_size("table")
    position = lax.axis_index("table")
    rows_dev, col_width = table_weights.shape
    own_hot = hot_slices[position]
    n_hots = own_hot.shape[0]
    starts = [own_hot[k] * SLICE for k in range(n_hots)]
    out_weights = jnp.stack(
        [lax.dynamic_slice_in_dim(table_weights, starts[k], SLICE, 0) for k in range(n_hots)]
    )
    out_first = jnp.stack(
        [lax.dynamic_slice_in_dim(moment_first, starts[k], SLICE, 0) for k in range(n_hots)]
    )
    out_second = jnp.stack(
        [lax.dynamic_slice_in_dim(moment_second, starts[k], SLICE, 0) for k in range(n_hots)]
    )
    swap_bit = n_table.bit_length() - 2
    incoming = partner_2((out_weights, out_first, out_second), "table", swap_bit)
    placed_weights = table_weights
    placed_first = moment_first
    placed_second = moment_second
    for k in range(n_hots):
        placed_weights = lax.dynamic_update_slice_in_dim(
            placed_weights, incoming[0][k], starts[k], 0
        )
        placed_first = lax.dynamic_update_slice_in_dim(placed_first, incoming[1][k], starts[k], 0)
        placed_second = lax.dynamic_update_slice_in_dim(placed_second, incoming[2][k], starts[k], 0)
    targets = local_targets(unique_rows[0], row_counts[0], hot_slices, rows_dev)
    slots = dedup_map.reshape(-1, GROUP * dedup_map.shape[1])
    slot_grad = slot_sums(slots, upstream_grad.T, targets.astype(jnp.float32))
    got = lax.all_to_all(slot_grad, "table", split_axis=0, concat_axis=0, tiled=True)
    dense = place_sums(got, rows_dev)
    full_width = col_width * lax.axis_size("col")
    gradient = lax.psum(dense, "dp")
    squares = lax.psum(jnp.sum(gradient * gradient, axis=1), "col")
    new_weights, new_first, new_second = adam_rows(
        placed_weights, placed_first, placed_second, gradient, squares, full_width
    )
    return (new_weights, new_first, new_second)


def solution(mesh):
    placed = (
        P("table", "col"),
        P("table", "col"),
        P("table"),
        P(),
        P(("table", "dp"), "col"),
        P(("table", "dp"), None),
        P(("table", "dp"), None, None),
        P(("table", "dp"), None),
    )
    return jax.shard_map(
        on_device,
        mesh=mesh,
        in_specs=placed,
        out_specs=(P("table", "col"), P("table", "col"), P("table")),
        check_vma=False,
    )
```

```python
import jax
import jax.numpy as jnp
from jax import lax
from jax.experimental import pallas as pl
from jax.experimental.pallas import tpu as pltpu
from jax.sharding import PartitionSpec as P

SLICE = 64
LOW = 256
GROUP = 8
EXTRA = 8
LANES = 128

beta_one = 0.9
beta_two = 0.99
learn_rate = 0.1
eps_value = 1e-08

NT = (((1,), (1,)), ((), ()))
VMEM = pl.BlockSpec(memory_space=pltpu.VMEM)
SMEM = pl.BlockSpec(memory_space=pltpu.SMEM)
HBM = pl.BlockSpec(memory_space=pl.ANY)


def one_hot(positions, wanted):
    return jnp.where(positions == wanted, 1.0, 0.0).astype(jnp.bfloat16)


def slot_kernel(map_ref, grad_ref, target_ref, out_ref, tally):
    groups, span = map_ref.shape
    highs = tally.shape[0]
    bag = span // GROUP
    owner = pl.program_id(0)

    @pl.when(owner == 0)
    def _():
        sample = lax.broadcasted_iota(jnp.int32, (1, span), 1) // bag
        left_at = lax.broadcasted_iota(jnp.int32, (highs * GROUP, span), 0)
        right_at = lax.broadcasted_iota(jnp.int32, (LOW, span), 0)

        def count(step, carry):
            first = pl.multiple_of(step * 8, 8)
            slots = map_ref[pl.ds(first, 8), :]
            for pair in range(4):
                halves = []
                for which in range(2):
                    at = 2 * pair + which
                    row = slots[at : at + 1, :]
                    left = one_hot(left_at, (row // LOW) * GROUP + sample)
                    right = one_hot(right_at, row % LOW)
                    part = lax.dot_general(left, right, NT, preferred_element_type=jnp.float32)
                    halves.append(part.reshape(highs, GROUP, LOW))
                both = jnp.concatenate(halves, axis=1).astype(jnp.bfloat16)
                begin = pl.multiple_of(first * GROUP + pair * 2 * GROUP, 2 * GROUP)
                tally[:, pl.ds(begin, 2 * GROUP), :] = both
            return carry

        lax.fori_loop(0, groups // 8, count, 0)

    columns = grad_ref.shape[0]
    out_ref[0, :columns, :] = jnp.dot(
        grad_ref[...], tally[owner], preferred_element_type=jnp.float32
    )
    out_ref[0, columns:, :] = jnp.broadcast_to(target_ref[pl.ds(owner, 1), :], (EXTRA, LOW))


def slot_sums(slots, grad_t, targets):
    highs = targets.shape[0]
    columns, samples = grad_t.shape
    height = columns + EXTRA
    return pl.pallas_call(
        slot_kernel,
        grid=(highs,),
        out_shape=jax.ShapeDtypeStruct((highs, height, LOW), jnp.float32),
        in_specs=[VMEM] * 3,
        out_specs=pl.BlockSpec((1, height, LOW), lambda owner: (owner, 0, 0)),
        scratch_shapes=[pltpu.VMEM((highs, samples, LOW), jnp.bfloat16)],
        compiler_params=pltpu.CompilerParams(vmem_limit_bytes=58 << 20),
        name="slot_sums",
    )(slots, grad_t, targets)


def add_block(pieces, aims, start, out_ref, select):
    block, width = select.shape
    step = 256
    place = lax.broadcasted_iota(jnp.int32, (block, step), 0)
    for at in range(0, width, step):
        select[:, at : at + step] = one_hot(place, aims[:1, at : at + step] - start)
    chosen = select[...]
    total = lax.dot_general(chosen, pieces[0], NT, preferred_element_type=jnp.float32)
    total += lax.dot_general(chosen, pieces[1], NT, preferred_element_type=jnp.float32)
    out_ref[...] = total


def place_first_kernel(start_ref, got_ref, pieces, aims, out_ref, select):
    sources, height, cap = got_ref.shape
    columns = height - EXTRA
    for source in range(sources):
        value = got_ref[source, :columns, :]
        upper = value.astype(jnp.bfloat16)
        lower = (value - upper.astype(jnp.float32)).astype(jnp.bfloat16)
        at = source * cap
        pieces[0, :, at : at + cap] = upper
        pieces[1, :, at : at + cap] = lower
        aims[:, at : at + cap] = got_ref[source, columns:, :].astype(jnp.int32)
    add_block(pieces, aims, start_ref[0], out_ref, select)


def place_next_kernel(start_ref, pieces, aims, *refs):
    outs, select = refs[:-1], refs[-1]
    for k, out_ref in enumerate(outs):
        add_block(pieces, aims, start_ref[k], out_ref, select)


def place_first(got, start, block):
    sources, height, cap = got.shape
    columns = height - EXTRA
    width = sources * cap
    return pl.pallas_call(
        place_first_kernel,
        out_shape=(
            jax.ShapeDtypeStruct((2, columns, width), jnp.bfloat16),
            jax.ShapeDtypeStruct((EXTRA, width), jnp.int32),
            jax.ShapeDtypeStruct((block, columns), jnp.float32),
        ),
        in_specs=[SMEM, VMEM],
        out_specs=[VMEM] * 3,
        scratch_shapes=[pltpu.VMEM((block, width), jnp.bfloat16)],
        compiler_params=pltpu.CompilerParams(vmem_limit_bytes=16 << 20),
        cost_estimate=pl.CostEstimate(
            flops=4 * block * width * columns, bytes_accessed=12 << 20, transcendentals=0
        ),
        name="place_first",
    )(start, got)


def place_next(pieces, aims, starts, block):
    _, columns, width = pieces.shape
    count = starts.shape[0]
    return pl.pallas_call(
        place_next_kernel,
        out_shape=tuple(jax.ShapeDtypeStruct((block, columns), jnp.float32) for _ in range(count)),
        in_specs=[SMEM, VMEM, VMEM],
        out_specs=[VMEM] * count,
        scratch_shapes=[pltpu.VMEM((block, width), jnp.bfloat16)],
        compiler_params=pltpu.CompilerParams(vmem_limit_bytes=16 << 20),
        cost_estimate=pl.CostEstimate(
            flops=4 * count * block * width * columns, bytes_accessed=8 << 20, transcendentals=0
        ),
        name="place_next",
    )(starts, pieces, aims)


def adam_kernel(groups, aliased, *refs):
    count = len(groups)
    block_ref, hot_ref = refs[:2]
    parts = refs[2 : 2 + sum(groups)]
    swapped, table, first, second = refs[2 + sum(groups) : 6 + sum(groups)]
    rest = refs[6 + sum(groups) + aliased :]
    out_table, out_first, out_second, held, grad, in_sem, out_sem = rest
    rows = grad.shape[1]
    n_hots = hot_ref.shape[0]
    per_block = rows // SLICE
    full_width = 2 * grad.shape[2]

    def at_block(i):
        return pl.ds(pl.multiple_of(block_ref[i] * rows, rows), rows)

    def arrivals(i):
        at = at_block(i)
        return (
            pltpu.make_async_copy(table.at[at, :], held.at[0, i], in_sem.at[0, i]),
            pltpu.make_async_copy(first.at[at, :], held.at[1, i], in_sem.at[1, i]),
        )

    def returns(i):
        at = at_block(i)
        return (
            pltpu.make_async_copy(held.at[0, i], out_table.at[at, :], out_sem.at[0, i]),
            pltpu.make_async_copy(held.at[1, i], out_first.at[at, :], out_sem.at[1, i]),
        )

    for i in range(count):
        for copy in arrivals(i):
            copy.start()
    begin = 0
    for i in range(count):
        for copy in arrivals(i):
            copy.wait()
        block = block_ref[i]
        for k in range(n_hots):
            hot = hot_ref[k]

            @pl.when(hot // per_block == block)
            def _():
                at = pl.ds(pl.multiple_of((hot % per_block) * SLICE, SLICE), SLICE)
                held[0, i, at, :] = swapped[k * SLICE : (k + 1) * SLICE, :]
                begin_first = (n_hots + k) * SLICE
                held[1, i, at, :] = swapped[begin_first : begin_first + SLICE, :]

        mine = parts[begin : begin + groups[i]]
        begin += groups[i]
        top = 0
        for part in mine:
            height = part.shape[0] - (EXTRA if part is mine[-1] else 0)
            grad[0, top : top + height, :] = part[:height, :]
            top += height
        tail = mine[-1].shape[0] - EXTRA
        lines = rows // LANES
        old = second[pl.ds(block * lines, lines), :]
        for line in range(lines):
            squares = mine[-1][tail : tail + 1, line * LANES : (line + 1) * LANES]
            fresh = beta_two * old[line : line + 1, :] + (1.0 - beta_two) * (squares / full_width)
            out_second[i * lines + line : i * lines + line + 1, :] = fresh
            scaled = jnp.sqrt(fresh / (1.0 - beta_two**8)) + eps_value
            rate = (learn_rate / (1.0 - beta_one**8)) / scaled
            rate = jnp.broadcast_to(rate, (LANES, LANES)).T
            at = slice(line * LANES, (line + 1) * LANES)
            for side in range(grad.shape[2] // LANES):
                cut = slice(side * LANES, (side + 1) * LANES)
                moment = beta_one * held[1, i, at, cut] + (1.0 - beta_one) * grad[0, at, cut]
                held[1, i, at, cut] = moment
                held[0, i, at, cut] = held[0, i, at, cut] - moment * rate
        for copy in returns(i):
            copy.start()
    for i in range(count):
        for copy in returns(i):
            copy.wait()


def adam_blocks(blocks, parts, own_hot, swapped, table, first, second, held=None):
    groups = tuple(len(p) for p in parts)
    flat = [ref for p in parts for ref in p]
    rows, columns = table.shape
    count = len(groups)
    block = SLICE * 4
    lines = block // LANES
    aliased = 0 if held is None else 2
    n_in = 6 + len(flat)
    outs = pl.pallas_call(
        lambda *refs: adam_kernel(groups, aliased, *refs),
        out_shape=(
            jax.ShapeDtypeStruct((rows, columns), jnp.float32),
            jax.ShapeDtypeStruct((rows, columns), jnp.float32),
            jax.ShapeDtypeStruct((count * lines, LANES), jnp.float32),
        ),
        in_specs=[SMEM, SMEM] + [VMEM] * (len(flat) + 1) + [HBM, HBM, VMEM] + [HBM] * aliased,
        out_specs=[HBM, HBM, VMEM],
        scratch_shapes=[
            pltpu.VMEM((2, count, block, columns), jnp.float32),
            pltpu.VMEM((1, block, columns), jnp.float32),
            pltpu.SemaphoreType.DMA((2, count)),
            pltpu.SemaphoreType.DMA((2, count)),
        ],
        input_output_aliases={n_in: 0, n_in + 1: 1} if aliased else {},
        compiler_params=pltpu.CompilerParams(vmem_limit_bytes=16 << 20),
        cost_estimate=pl.CostEstimate(
            flops=8 * count * block * columns,
            bytes_accessed=20 * count * block * columns,
            transcendentals=0,
        ),
        name="adam_blocks",
    )(blocks, own_hot, *flat, swapped, table, first, second, *(held or ()))
    return outs


def local_targets(unique_rows, row_counts, hot_slices, rows_dev):
    n_table, n_hots = hot_slices.shape
    cap = unique_rows.shape[1]
    partner = (jnp.arange(n_table) + n_table // 2) % n_table
    partner_hot = jnp.concatenate([hot_slices[n_table // 2 :], hot_slices[: n_table // 2]], axis=0)
    local_row = unique_rows % rows_dev
    from_partner = unique_rows // rows_dev == partner[:, None]
    target = local_row
    for k in range(n_hots):
        moved = from_partner & (local_row // SLICE == partner_hot[:, k : k + 1])
        target = jnp.where(moved, hot_slices[:, k : k + 1] * SLICE + local_row % SLICE, target)
    valid = jnp.arange(cap)[None, :] < row_counts[:, None]
    return jnp.where(valid, target, rows_dev)


def on_device(
    table_weights,
    moment_first,
    moment_second,
    hot_slices,
    upstream_grad,
    dedup_map,
    unique_rows,
    row_counts,
):
    n_table = lax.axis_size("table")
    n_dp = lax.axis_size("dp")
    position = lax.axis_index("table")
    me = lax.axis_index("dp")
    rows_dev, col_width = table_weights.shape
    block = rows_dev // n_dp
    half = block // 2

    targets = local_targets(unique_rows[0], row_counts[0], hot_slices, rows_dev)
    slots = dedup_map.reshape(-1, GROUP * dedup_map.shape[1])
    slot_grad = slot_sums(slots, upstream_grad.T, targets.astype(jnp.float32))
    got = lax.all_to_all(slot_grad, "table", split_axis=0, concat_axis=0, tiled=True)

    own_hot = hot_slices[position]
    n_hots = own_hot.shape[0]
    starts = [own_hot[k] * SLICE for k in range(n_hots)]
    leaving = [lax.dynamic_slice_in_dim(table_weights, s, SLICE, 0) for s in starts]
    leaving += [lax.dynamic_slice_in_dim(moment_first, s, SLICE, 0) for s in starts]
    leaving_second = [lax.dynamic_slice_in_dim(moment_second, s, SLICE, 0) for s in starts]
    lead = jnp.concatenate(leaving_second)[None, :]
    lead = jnp.broadcast_to(jnp.pad(lead, ((0, 0), (0, col_width - n_hots * SLICE))), (EXTRA, col_width))
    swap = [(t, (t + n_table // 2) % n_table) for t in range(n_table)]
    parcel, slot_grad_seen = lax.optimization_barrier(
        (jnp.concatenate(leaving + [lead], axis=0), slot_grad[0, :8, :128])
    )
    swapped = lax.ppermute(parcel, "table", swap)
    got, swapped = lax.optimization_barrier((got, swapped))
    new_lead = swapped[2 * n_hots * SLICE, : n_hots * SLICE].reshape(n_hots, SLICE)
    slices = moment_second.reshape(-1, SLICE)
    for k in range(n_hots):
        here = jnp.arange(slices.shape[0])[:, None] == own_hot[k]
        slices = jnp.where(here, new_lead[k][None, :], slices)
    placed_second = slices.reshape(-1, LANES)

    up = [(i, (i + 1) % n_dp) for i in range(n_dp)]
    down = [(i, (i - 1) % n_dp) for i in range(n_dp)]

    def send(value, route):
        return lax.ppermute(value, "dp", route)

    def block_at(offset):
        return (me + offset + n_dp) % n_dp

    def begin_at(*offsets):
        return jnp.stack([block_at(o) * block for o in offsets]).astype(jnp.int32)

    pieces, aims, far = place_first(got, begin_at(4), block)
    rise = send(far[:half], up)
    fall = send(far[half:], down)
    plus, minus = place_next(pieces, aims, begin_at(3, -3), block)
    rise = jnp.concatenate([plus[:half] + rise, plus[half:]], axis=0)
    fall = jnp.concatenate([minus[:half], minus[half:] + fall], axis=0)
    for distance in (2, 1):
        rise, fall = send(rise, up), send(fall, down)
        plus, minus = place_next(pieces, aims, begin_at(distance, -distance), block)
        rise, fall = plus + rise, minus + fall
    rise, fall = send(rise, up), send(fall, down)
    (mine,) = place_next(pieces, aims, begin_at(0), block)
    mine = mine + rise + fall
    squares = lax.psum(jnp.sum(mine * mine, axis=1), "col")
    own = jnp.concatenate([mine, jnp.broadcast_to(squares[None, :], (EXTRA, block))], axis=0)

    order, parts = [0], [[own]]
    rise = fall = own
    for distance in (1, 2, 3):
        rise, fall = send(rise, up), send(fall, down)
        order += [-distance, distance]
        parts += [[rise], [fall]]
    rise, fall = send(rise[:half], up), send(fall[half:], down)
    near = jnp.stack([block_at(o) for o in order]).astype(jnp.int32)
    common = (own_hot, swapped, table_weights, moment_first, placed_second)
    weights, first, near_second = adam_blocks(near, parts, *common)
    last = block_at(4).reshape(1).astype(jnp.int32)
    weights, first, last_second = adam_blocks(
        last, [[rise, fall]], *common, held=(weights, first)
    )
    lines = block // LANES
    together = jnp.concatenate([near_second, last_second], axis=0).reshape(n_dp, block)
    arrived = jnp.concatenate([near, last])
    second = jnp.zeros_like(together)
    wanted = jnp.arange(n_dp)
    for i in range(n_dp):
        second = jnp.where((wanted == arrived[i])[:, None], together[i][None, :], second)
    return (weights, first, second.reshape(-1))


def solution(mesh):
    placed = (
        P("table", "col"),
        P("table", "col"),
        P("table"),
        P(),
        P(("table", "dp"), "col"),
        P(("table", "dp"), None),
        P(("table", "dp"), None, None),
        P(("table", "dp"), None),
    )
    return jax.shard_map(
        on_device,
        mesh=mesh,
        in_specs=placed,
        out_specs=(P("table", "col"), P("table", "col"), P("table")),
        check_vma=False,
    )
```

```python
import jax
import jax.numpy as jnp
from jax import lax
from jax.experimental import pallas as pl
from jax.experimental.pallas import tpu as pltpu
from jax.sharding import Mesh
from jax.sharding import PartitionSpec as P

SLICE = 64
CAP = 256
LOW = 128
GROUP = 8
EXTRA = 8
LANES = 128

beta_one = 0.9
beta_two = 0.99
learn_rate = 0.1
eps_value = 1e-08

NT = (((1,), (1,)), ((), ()))
VMEM = pl.BlockSpec(memory_space=pltpu.VMEM)
SMEM = pl.BlockSpec(memory_space=pltpu.SMEM)
HBM = pl.BlockSpec(memory_space=pltpu.HBM)
ANY = pl.BlockSpec(memory_space=pl.ANY)


def digits(values):
    return values.astype(jnp.float32).astype(jnp.bfloat16)


def counting(shape):
    return digits(lax.broadcasted_iota(jnp.int32, shape, 0))


def one_hot(positions, wanted):
    return jnp.where(positions == wanted, jnp.bfloat16(1), jnp.bfloat16(0))


def slot_kernel(map_ref, grad_ref, target_ref, out_ref, tally, held, sems):
    groups, span = map_ref.shape
    owners, _, cap = tally.shape
    per_owner = cap // LOW
    highs = owners * per_owner
    sample = lax.broadcasted_iota(jnp.int32, (1, span), 1) // (span // GROUP)
    left_at = counting((highs * GROUP, span))
    right_at = counting((LOW, span))
    batch = 16

    def count(step, carry):
        first = pl.multiple_of(step * batch, batch)
        slots = map_ref[pl.ds(first, batch), :]
        lefts = digits((slots // LOW) * GROUP + sample)
        rights = digits(slots % LOW)
        for pair in range(batch // 2):
            halves = []
            for at in (2 * pair, 2 * pair + 1):
                left = one_hot(left_at, lefts[at : at + 1, :])
                right = one_hot(right_at, rights[at : at + 1, :])
                part = lax.dot_general(left, right, NT, preferred_element_type=jnp.float32)
                halves.append(part.reshape(highs, GROUP, LOW))
            both = jnp.concatenate(halves, axis=1).astype(jnp.bfloat16)
            both = both.reshape(owners, per_owner, 2 * GROUP, LOW)
            begin = pl.multiple_of(first * GROUP + pair * 2 * GROUP, 2 * GROUP)
            for k in range(per_owner):
                tally[:, pl.ds(begin, 2 * GROUP), k * LOW : (k + 1) * LOW] = both[:, k]
        return carry

    lax.fori_loop(0, groups // batch, count, 0)
    depth, shares, height, _ = held.shape
    columns = height - EXTRA

    def leave(owner):
        slot = owner % depth
        at = pl.ds(owner * shares, shares)
        return pltpu.make_async_copy(held.at[slot], out_ref.at[at], sems.at[slot])

    for owner in range(owners):
        if owner >= depth:
            leave(owner - depth).wait()
        slot = owner % depth
        total = jnp.dot(grad_ref[...], tally[owner], preferred_element_type=jnp.float32)
        aim = jnp.broadcast_to(target_ref[owner : owner + 1, :], (EXTRA, cap))
        for share in range(shares):
            held[slot, share, :columns, :] = total[share * columns : (share + 1) * columns, :]
            held[slot, share, columns:, :] = aim
        leave(owner).start()
    for owner in range(owners - depth, owners):
        leave(owner).wait()


def slot_sums(slots, grad_t, targets, shares):
    owners, cap = targets.shape
    columns, samples = grad_t.shape
    height = columns // shares + EXTRA
    depth = 4
    return pl.pallas_call(
        slot_kernel,
        out_shape=jax.ShapeDtypeStruct((owners * shares, height, cap), jnp.float32),
        in_specs=[VMEM] * 3,
        out_specs=HBM,
        scratch_shapes=[
            pltpu.VMEM((owners, samples, cap), jnp.bfloat16),
            pltpu.VMEM((depth, shares, height, cap), jnp.float32),
            pltpu.SemaphoreType.DMA((depth,)),
        ],
        compiler_params=pltpu.CompilerParams(vmem_limit_bytes=50 << 20),
        name="slot_sums",
    )(slots, grad_t, targets)


def add_block(pieces, aims, start, out_ref, select):
    part, width = select.shape
    columns = out_ref.shape[1]
    place = counting((part, CAP))
    for top in range(0, out_ref.shape[0], part):
        for at in range(0, width, CAP):
            row = aims[:1, at : at + CAP] - (start + top)
            row = digits(jnp.where((row >= 0) & (row < part), row, -1))
            select[:, at : at + CAP] = one_hot(place, row)
        both = lax.dot_general(select[...], pieces[...], NT, preferred_element_type=jnp.float32)
        out_ref[top : top + part, :] = both[:, :columns] + both[:, columns:]


def place_first_kernel(start_ref, got_ref, pieces, aims, out_ref, select, held, sems):
    sources, height, cap = got_ref.shape
    columns = height - EXTRA
    batch = sources // sems.shape[0]

    def fetch(k):
        at = pl.ds(k * batch, batch)
        return pltpu.make_async_copy(got_ref.at[at], held.at[at], sems.at[k])

    for k in range(sems.shape[0]):
        fetch(k).start()
    for source in range(sources):
        if source % batch == 0:
            fetch(source // batch).wait()
        value = held[source, :columns, :]
        upper = value.astype(jnp.bfloat16)
        lower = (value - upper.astype(jnp.float32)).astype(jnp.bfloat16)
        at = source * cap
        pieces[:columns, at : at + cap] = upper
        pieces[columns:, at : at + cap] = lower
        aims[:, at : at + cap] = held[source, columns:, :].astype(jnp.int32)
    add_block(pieces, aims, start_ref[0], out_ref, select)


def place_next_kernel(start_ref, pieces, aims, *refs):
    outs, select = refs[:-1], refs[-1]
    for k, out_ref in enumerate(outs):
        add_block(pieces, aims, start_ref[k], out_ref, select)


def place_cost(blocks, block, width, columns):
    flops = 4 * blocks * block * width * columns
    return pl.CostEstimate(flops=flops, bytes_accessed=8 << 20, transcendentals=0)


def place_first(got, start, block):
    sources, height, cap = got.shape
    columns = height - EXTRA
    width = sources * cap
    return pl.pallas_call(
        place_first_kernel,
        out_shape=(
            jax.ShapeDtypeStruct((2 * columns, width), jnp.bfloat16),
            jax.ShapeDtypeStruct((EXTRA, width), jnp.int32),
            jax.ShapeDtypeStruct((block, columns), jnp.float32),
        ),
        in_specs=[SMEM, HBM],
        out_specs=[VMEM] * 3,
        scratch_shapes=[
            pltpu.VMEM((CAP, width), jnp.bfloat16),
            pltpu.VMEM(got.shape, jnp.float32),
            pltpu.SemaphoreType.DMA((8,)),
        ],
        compiler_params=pltpu.CompilerParams(vmem_limit_bytes=24 << 20),
        cost_estimate=place_cost(1, block, width, columns),
        name="place_first",
    )(start, got)


def place_next(pieces, aims, starts, block):
    columns, width = pieces.shape[0] // 2, pieces.shape[1]
    count = starts.shape[0]
    return pl.pallas_call(
        place_next_kernel,
        out_shape=tuple(jax.ShapeDtypeStruct((block, columns), jnp.float32) for _ in range(count)),
        in_specs=[SMEM, VMEM, VMEM],
        out_specs=[VMEM] * count,
        scratch_shapes=[pltpu.VMEM((CAP, width), jnp.bfloat16)],
        compiler_params=pltpu.CompilerParams(vmem_limit_bytes=18 << 20),
        cost_estimate=place_cost(count, block, width, columns),
        name="place_next",
    )(starts, pieces, aims)


def adam_kernel(groups, full_width, aliased, *refs):
    count = len(groups)
    row_ref, column_ref = refs[:2]
    parts = refs[2 : 2 + sum(groups)]
    table, first, second, before = refs[2 + sum(groups) : 6 + sum(groups)]
    rest = refs[6 + sum(groups) + aliased :]
    out_table, out_first, out_second, held, in_sem, out_sem = rest
    rows, columns = held.shape[2:]
    lines = rows // LANES

    def place_of(i):
        at = pl.ds(pl.multiple_of(row_ref[i] * rows, rows), rows)
        cut = pl.ds(pl.multiple_of(column_ref[i] * columns, columns), columns)
        return at, cut

    def arrivals(i):
        at, cut = place_of(i)
        return (
            pltpu.make_async_copy(table.at[at, cut], held.at[0, i], in_sem.at[0, i]),
            pltpu.make_async_copy(first.at[at, cut], held.at[1, i], in_sem.at[1, i]),
        )

    def returns(i):
        at, cut = place_of(i)
        return (
            pltpu.make_async_copy(held.at[0, i], out_table.at[at, cut], out_sem.at[0, i]),
            pltpu.make_async_copy(held.at[1, i], out_first.at[at, cut], out_sem.at[1, i]),
        )

    for i in range(count):
        for copy in arrivals(i):
            copy.start()
    out_second[...] = before[...]
    begin = 0
    for i in range(count):
        mine = parts[begin : begin + groups[i]]
        begin += groups[i]
        block = row_ref[i]
        for copy in arrivals(i):
            copy.wait()
        old = second[pl.ds(block * lines, lines), :]
        tail = mine[-1].shape[0] - EXTRA
        squares = mine[-1][tail : tail + lines, :]
        fresh = beta_two * old + (1.0 - beta_two) * (squares / full_width)
        out_second[pl.ds(block * lines, lines), :] = fresh
        scaled = jnp.sqrt(fresh / (1.0 - beta_two**8)) + eps_value
        rates = (learn_rate / (1.0 - beta_one**8)) / scaled
        at = 0
        for part in mine:
            for top in range(0, part.shape[0] - LANES + 1, LANES):
                line = at // LANES
                rate = jnp.broadcast_to(rates[line : line + 1, :], (LANES, LANES)).T
                span = slice(at, at + LANES)
                gradient = part[top : top + LANES, :]
                moment = beta_one * held[1, i, span, :] + (1.0 - beta_one) * gradient
                held[1, i, span, :] = moment
                held[0, i, span, :] = held[0, i, span, :] - moment * rate
                at += LANES
        for copy in returns(i):
            copy.start()
    for i in range(count):
        for copy in returns(i):
            copy.wait()


def adam_blocks(rows_at, columns_at, parts, shape, full_width, common, before, held=None):
    groups = tuple(len(p) for p in parts)
    flat = [ref for p in parts for ref in p]
    table, first, second = common
    rows, columns = table.shape
    count = len(groups)
    aliased = 0 if held is None else 2
    n_in = 6 + len(flat)
    size = shape[0] * shape[1]
    return pl.pallas_call(
        lambda *refs: adam_kernel(groups, full_width, aliased, *refs),
        out_shape=(
            jax.ShapeDtypeStruct((rows, columns), jnp.float32),
            jax.ShapeDtypeStruct((rows, columns), jnp.float32),
            jax.ShapeDtypeStruct(second.shape, jnp.float32),
        ),
        in_specs=[SMEM] * 2 + [VMEM] * len(flat) + [ANY, ANY, VMEM, VMEM] + [HBM] * aliased,
        out_specs=[HBM, HBM, VMEM],
        scratch_shapes=[
            pltpu.VMEM((2, count) + shape, jnp.float32),
            pltpu.SemaphoreType.DMA((2, count)),
            pltpu.SemaphoreType.DMA((2, count)),
        ],
        input_output_aliases={n_in: 0, n_in + 1: 1} if aliased else {},
        compiler_params=pltpu.CompilerParams(vmem_limit_bytes=12 << 20),
        cost_estimate=pl.CostEstimate(
            flops=8 * count * size, bytes_accessed=20 * count * size, transcendentals=0
        ),
        name="adam_blocks",
    )(rows_at, columns_at, *flat, table, first, second, before, *(held or ()))


def local_targets(unique_rows, row_counts, hot_slices, rows_dev):
    n_table, n_hots = hot_slices.shape
    cap = unique_rows.shape[1]
    partner = (jnp.arange(n_table) + n_table // 2) % n_table
    partner_hot = jnp.concatenate([hot_slices[n_table // 2 :], hot_slices[: n_table // 2]], axis=0)
    local_row = unique_rows % rows_dev
    from_partner = unique_rows // rows_dev == partner[:, None]
    target = local_row
    for k in range(n_hots):
        moved = from_partner & (local_row // SLICE == partner_hot[:, k : k + 1])
        target = jnp.where(moved, hot_slices[:, k : k + 1] * SLICE + local_row % SLICE, target)
    valid = jnp.arange(cap)[None, :] < row_counts[:, None]
    return jnp.where(valid, target, rows_dev)


def on_device(
    table_weights,
    moment_first,
    moment_second,
    hot_slices,
    upstream_grad,
    dedup_map,
    unique_rows,
    row_counts,
):
    n_table = lax.axis_size("table")
    n_far, n_pair = lax.axis_size("far"), lax.axis_size("pair")
    n_dp = n_far * n_pair
    position = lax.axis_index("table")
    far_at, pair_at = lax.axis_index("far"), lax.axis_index("pair")
    rows_dev, col_width = table_weights.shape
    full_width = col_width * lax.axis_size("col")
    block, share = rows_dev // n_far, col_width // n_pair
    half = block // 2

    targets = local_targets(unique_rows[0], row_counts[0], hot_slices, rows_dev)
    slots = dedup_map.reshape(-1, GROUP * dedup_map.shape[1])
    slot_grad = slot_sums(slots, upstream_grad.T, targets.astype(jnp.float32), n_pair)
    got = lax.all_to_all(slot_grad, ("table", "pair"), split_axis=0, concat_axis=0, tiled=True)

    own_hot = hot_slices[position]
    n_hots = own_hot.shape[0]
    starts = [own_hot[k] * SLICE for k in range(n_hots)]
    leaving = [lax.dynamic_slice_in_dim(table_weights, s, SLICE, 0) for s in starts]
    leaving += [lax.dynamic_slice_in_dim(moment_first, s, SLICE, 0) for s in starts]
    leaving_second = [lax.dynamic_slice_in_dim(moment_second, s, SLICE, 0) for s in starts]
    lead = jnp.concatenate(leaving_second)[None, :]
    lead = jnp.broadcast_to(jnp.pad(lead, ((0, 0), (0, col_width - n_hots * SLICE))), (EXTRA, col_width))
    swap = [(t, (t + n_table // 2) % n_table) for t in range(n_table)]
    swapped = lax.ppermute(jnp.concatenate(leaving + [lead], axis=0), "table", swap)
    size = n_hots * SLICE

    def place(old, new):
        slices = old.reshape((-1, SLICE) + old.shape[1:])
        new = new.reshape((n_hots, SLICE) + old.shape[1:])
        at = jnp.arange(slices.shape[0]).reshape((-1,) + (1,) * old.ndim)
        for k in range(n_hots):
            slices = jnp.where(at == own_hot[k], new[k], slices)
        return slices.reshape(old.shape)

    placed_weights = place(table_weights, swapped[:size])
    placed_first = place(moment_first, swapped[size : 2 * size])
    placed_second = place(moment_second, swapped[2 * size, :size]).reshape(-1, LANES)
    got, placed_weights, placed_first, placed_second = lax.optimization_barrier(
        (got, placed_weights, placed_first, placed_second)
    )

    def begin_at(*offsets):
        return jnp.stack([(far_at + o + n_far) % n_far * block for o in offsets]).astype(jnp.int32)

    def send(value, axes, count, step):
        return lax.ppermute(value, axes, [(i, (i + step) % count) for i in range(count)])

    pieces, aims, other = place_first(got, begin_at(2), block)
    rise = send(other[:half], "far", n_far, 1)
    fall = send(other[half:], "far", n_far, -1)
    plus, minus = place_next(pieces, aims, begin_at(1, -1), block)
    rise = jnp.concatenate([plus[:half] + rise, plus[half:]], axis=0)
    fall = jnp.concatenate([minus[:half], minus[half:] + fall], axis=0)
    rise, fall = send(rise, "far", n_far, 1), send(fall, "far", n_far, -1)
    (mine,) = place_next(pieces, aims, begin_at(0), block)
    mine = mine + rise + fall
    squares = lax.psum(jnp.sum(mine * mine, axis=1), ("pair", "col")).reshape(-1, share)
    squares = jnp.pad(squares, ((0, EXTRA - squares.shape[0]), (0, 0)))
    own = jnp.concatenate([mine, squares], axis=0)

    ring = ("far", "pair")
    me = far_at * n_pair + pair_at
    common = (placed_weights, placed_first, placed_second)

    def update(arrived, second, held=None):
        at = jnp.stack([(me + o + n_dp) % n_dp for o, _ in arrived]).astype(jnp.int32)
        parts = [p for _, p in arrived]
        return adam_blocks(
            at // n_pair, at % n_pair, parts, (block, share), full_width, common, second, held
        )

    rise, fall = send(own, ring, n_dp, 1), send(own, ring, n_dp, -1)
    arrived = [(0, [own]), (-1, [rise]), (1, [fall])]
    rise, fall = send(rise, ring, n_dp, 1), send(fall, ring, n_dp, -1)
    weights, first, second = update(arrived, placed_second)
    rise, fall, second = lax.optimization_barrier((rise, fall, second))
    arrived = [(-2, [rise]), (2, [fall])]
    rise, fall = send(rise, ring, n_dp, 1), send(fall, ring, n_dp, -1)
    arrived += [(-3, [rise]), (3, [fall])]
    rise, fall = send(rise[:half], ring, n_dp, 1), send(fall[half:], ring, n_dp, -1)
    weights, first, second = update(arrived, second, (weights, first))
    weights, first, second = update([(4, [rise, fall])], second, (weights, first))
    return (weights, first, second.reshape(-1))


def solution(mesh):
    n_table, n_dp, n_col = (mesh.shape[a] for a in ("table", "dp", "col"))
    inner = Mesh(mesh.devices.reshape(n_table, n_dp // 2, 2, n_col), ("table", "far", "pair", "col"))
    samples = ("table", "far", "pair")
    placed = (
        P("table", "col"),
        P("table", "col"),
        P("table"),
        P(),
        P(samples, "col"),
        P(samples, None),
        P(samples, None, None),
        P(samples, None),
    )
    return jax.shard_map(
        on_device,
        mesh=inner,
        in_specs=placed,
        out_specs=(P("table", "col"), P("table", "col"), P("table")),
        check_vma=False,
    )
```

```python
import jax
import jax.numpy as jnp
from jax import lax
from jax.experimental import pallas as pl
from jax.experimental.pallas import tpu as pltpu
from jax.sharding import Mesh
from jax.sharding import PartitionSpec as P

SLICE = 64
CAP = 256
LOW = 128
GROUP = 8
EXTRA = 8
LANES = 128

beta_one = 0.9
beta_two = 0.99
learn_rate = 0.1
eps_value = 1e-08

NT = (((1,), (1,)), ((), ()))
VMEM = pl.BlockSpec(memory_space=pltpu.VMEM)
SMEM = pl.BlockSpec(memory_space=pltpu.SMEM)
HBM = pl.BlockSpec(memory_space=pltpu.HBM)
ANY = pl.BlockSpec(memory_space=pl.ANY)


def digits(values):
    return values.astype(jnp.float32).astype(jnp.bfloat16)


def counting(shape):
    return digits(lax.broadcasted_iota(jnp.int32, shape, 0))


def one_hot(positions, wanted):
    return jnp.where(positions == wanted, jnp.bfloat16(1), jnp.bfloat16(0))


def target_row(owner, hot_ref, count_ref, rows, rows_dev):
    owners, n_hots = hot_ref.shape
    partner = (owner + owners // 2) % owners
    local_row = rows % rows_dev
    from_partner = rows // rows_dev == partner
    target = local_row
    for k in range(n_hots):
        moved = from_partner & (local_row // SLICE == hot_ref[partner, k])
        target = jnp.where(moved, hot_ref[owner, k] * SLICE + local_row % SLICE, target)
    used = lax.broadcasted_iota(jnp.int32, rows.shape, 1) < count_ref[0, owner]
    return jnp.where(used, target, rows_dev)


def slot_kernel(rows_dev, map_ref, grad_ref, hot_ref, count_ref, rows_ref, out_ref, tally, held, sems):
    groups, span = map_ref.shape
    owners, _, cap = tally.shape
    per_owner = cap // LOW
    highs = owners * per_owner
    sample = lax.broadcasted_iota(jnp.int32, (1, span), 1) // (span // GROUP)
    left_at = counting((highs * GROUP, span))
    right_at = counting((LOW, span))
    batch = 16

    def count(step, carry):
        first = pl.multiple_of(step * batch, batch)
        slots = map_ref[pl.ds(first, batch), :]
        lefts = digits((slots // LOW) * GROUP + sample)
        rights = digits(slots % LOW)
        for pair in range(batch // 2):
            halves = []
            for at in (2 * pair, 2 * pair + 1):
                left = one_hot(left_at, lefts[at : at + 1, :])
                right = one_hot(right_at, rights[at : at + 1, :])
                part = lax.dot_general(left, right, NT, preferred_element_type=jnp.float32)
                halves.append(part.reshape(highs, GROUP, LOW))
            both = jnp.concatenate(halves, axis=1).astype(jnp.bfloat16)
            both = both.reshape(owners, per_owner, 2 * GROUP, LOW)
            begin = pl.multiple_of(first * GROUP + pair * 2 * GROUP, 2 * GROUP)
            for k in range(per_owner):
                tally[:, pl.ds(begin, 2 * GROUP), k * LOW : (k + 1) * LOW] = both[:, k]
        return carry

    lax.fori_loop(0, groups // batch, count, 0)
    depth, shares, height, _ = held.shape
    columns = height - EXTRA

    def leave(owner):
        slot = owner % depth
        at = pl.ds(owner * shares, shares)
        return pltpu.make_async_copy(held.at[slot], out_ref.at[at], sems.at[slot])

    for owner in range(owners):
        if owner >= depth:
            leave(owner - depth).wait()
        slot = owner % depth
        total = jnp.dot(grad_ref[...], tally[owner], preferred_element_type=jnp.float32)
        aim = target_row(owner, hot_ref, count_ref, rows_ref[0, owner : owner + 1, :], rows_dev)
        aim = jnp.broadcast_to(aim.astype(jnp.float32), (EXTRA, cap))
        for share in range(shares):
            held[slot, share, :columns, :] = total[share * columns : (share + 1) * columns, :]
            held[slot, share, columns:, :] = aim
        leave(owner).start()
    for owner in range(owners - depth, owners):
        leave(owner).wait()


def slot_sums(slots, grad_t, hot_slices, row_counts, unique_rows, shares, rows_dev):
    _, owners, cap = unique_rows.shape
    columns, samples = grad_t.shape
    height = columns // shares + EXTRA
    depth = 4
    return pl.pallas_call(
        lambda *refs: slot_kernel(rows_dev, *refs),
        out_shape=jax.ShapeDtypeStruct((owners * shares, height, cap), jnp.float32),
        in_specs=[VMEM, VMEM, SMEM, SMEM, VMEM],
        out_specs=HBM,
        scratch_shapes=[
            pltpu.VMEM((owners, samples, cap), jnp.bfloat16),
            pltpu.VMEM((depth, shares, height, cap), jnp.float32),
            pltpu.SemaphoreType.DMA((depth,)),
        ],
        compiler_params=pltpu.CompilerParams(vmem_limit_bytes=50 << 20),
        name="slot_sums",
    )(slots, grad_t, hot_slices, row_counts, unique_rows)


def add_block(pieces, aims, start, out_ref, select):
    part, width = select.shape
    columns = out_ref.shape[1]
    place = counting((part, CAP))
    for top in range(0, out_ref.shape[0], part):
        for at in range(0, width, CAP):
            row = aims[:1, at : at + CAP] - (start + top)
            row = digits(jnp.where((row >= 0) & (row < part), row, -1))
            select[:, at : at + CAP] = one_hot(place, row)
        both = lax.dot_general(select[...], pieces[...], NT, preferred_element_type=jnp.float32)
        out_ref[top : top + part, :] = both[:, :columns] + both[:, columns:]


def place_first_kernel(start_ref, got_ref, pieces, aims, out_ref, select, held, sems):
    sources, height, cap = got_ref.shape
    columns = height - EXTRA
    batch = sources // sems.shape[0]

    def fetch(k):
        at = pl.ds(k * batch, batch)
        return pltpu.make_async_copy(got_ref.at[at], held.at[at], sems.at[k])

    for k in range(sems.shape[0]):
        fetch(k).start()
    for source in range(sources):
        if source % batch == 0:
            fetch(source // batch).wait()
        value = held[source, :columns, :]
        upper = value.astype(jnp.bfloat16)
        lower = (value - upper.astype(jnp.float32)).astype(jnp.bfloat16)
        at = source * cap
        pieces[:columns, at : at + cap] = upper
        pieces[columns:, at : at + cap] = lower
        aims[:, at : at + cap] = held[source, columns:, :].astype(jnp.int32)
    add_block(pieces, aims, start_ref[0], out_ref, select)


def place_next_kernel(start_ref, pieces, aims, *refs):
    outs, select = refs[:-1], refs[-1]
    for k, out_ref in enumerate(outs):
        add_block(pieces, aims, start_ref[k], out_ref, select)


def place_cost(blocks, block, width, columns):
    flops = 4 * blocks * block * width * columns
    return pl.CostEstimate(flops=flops, bytes_accessed=8 << 20, transcendentals=0)


def place_first(got, start, block):
    sources, height, cap = got.shape
    columns = height - EXTRA
    width = sources * cap
    return pl.pallas_call(
        place_first_kernel,
        out_shape=(
            jax.ShapeDtypeStruct((2 * columns, width), jnp.bfloat16),
            jax.ShapeDtypeStruct((EXTRA, width), jnp.int32),
            jax.ShapeDtypeStruct((block, columns), jnp.float32),
        ),
        in_specs=[SMEM, HBM],
        out_specs=[VMEM] * 3,
        scratch_shapes=[
            pltpu.VMEM((CAP, width), jnp.bfloat16),
            pltpu.VMEM(got.shape, jnp.float32),
            pltpu.SemaphoreType.DMA((8,)),
        ],
        compiler_params=pltpu.CompilerParams(vmem_limit_bytes=46 << 20),
        cost_estimate=place_cost(1, block, width, columns),
        name="place_first",
    )(start, got)


def place_next(pieces, aims, starts, block):
    columns, width = pieces.shape[0] // 2, pieces.shape[1]
    count = starts.shape[0]
    return pl.pallas_call(
        place_next_kernel,
        out_shape=tuple(jax.ShapeDtypeStruct((block, columns), jnp.float32) for _ in range(count)),
        in_specs=[SMEM, VMEM, VMEM],
        out_specs=[VMEM] * count,
        scratch_shapes=[pltpu.VMEM((CAP, width), jnp.bfloat16)],
        compiler_params=pltpu.CompilerParams(vmem_limit_bytes=18 << 20),
        cost_estimate=place_cost(count, block, width, columns),
        name="place_next",
    )(starts, pieces, aims)


def adam_kernel(groups, full_width, aliased, *refs):
    count = len(groups)
    row_ref, column_ref, hot_ref = refs[:3]
    parts = refs[3 : 3 + sum(groups)]
    swapped, table, first, second, before = refs[3 + sum(groups) : 8 + sum(groups)]
    rest = refs[8 + sum(groups) + aliased :]
    placed_second = rest[-1]
    rest = rest[:-1]
    out_table, out_first, out_second, held, in_sem, out_sem = rest
    rows, columns = held.shape[2:]
    lines = rows // LANES

    def place_of(i):
        at = pl.ds(pl.multiple_of(row_ref[i] * rows, rows), rows)
        cut = pl.ds(pl.multiple_of(column_ref[i] * columns, columns), columns)
        return at, cut

    def arrivals(i):
        at, cut = place_of(i)
        return (
            pltpu.make_async_copy(table.at[at, cut], held.at[0, i], in_sem.at[0, i]),
            pltpu.make_async_copy(first.at[at, cut], held.at[1, i], in_sem.at[1, i]),
        )

    def returns(i):
        at, cut = place_of(i)
        return (
            pltpu.make_async_copy(held.at[0, i], out_table.at[at, cut], out_sem.at[0, i]),
            pltpu.make_async_copy(held.at[1, i], out_first.at[at, cut], out_sem.at[1, i]),
        )

    for i in range(count):
        for copy in arrivals(i):
            copy.start()
    out_second[...] = before[...]
    placed = second[...]
    lead = swapped[4 * SLICE : 4 * SLICE + 1, :LANES]
    line_at = lax.broadcasted_iota(jnp.int32, placed.shape, 0)
    side_at = lax.broadcasted_iota(jnp.int32, placed.shape, 1) // SLICE
    for k in range(2):
        hot = hot_ref[k]
        here = (line_at == hot // 2) & (side_at == hot % 2)
        placed = jnp.where(here, turned(lead, hot % 2 != k), placed)
    placed_second[...] = placed
    per_block = rows // SLICE
    begin = 0
    for i in range(count):
        mine = parts[begin : begin + groups[i]]
        begin += groups[i]
        block = row_ref[i]
        for copy in arrivals(i):
            copy.wait()
        for k in range(2):
            hot = hot_ref[k]

            @pl.when(hot // per_block == block)
            def _():
                at = pl.ds(pl.multiple_of((hot % per_block) * SLICE, SLICE), SLICE)
                for which in range(2):
                    begin_at = (2 * which + k) * SLICE
                    held[which, i, at, :] = swapped[begin_at : begin_at + SLICE, place_of(i)[1]]

        old = placed_second[pl.ds(block * lines, lines), :]
        tail = mine[-1].shape[0] - EXTRA
        squares = mine[-1][tail : tail + lines, :]
        fresh = beta_two * old + (1.0 - beta_two) * (squares / full_width)
        out_second[pl.ds(block * lines, lines), :] = fresh
        scaled = jnp.sqrt(fresh / (1.0 - beta_two**8)) + eps_value
        rates = (learn_rate / (1.0 - beta_one**8)) / scaled
        at = 0
        for part in mine:
            for top in range(0, part.shape[0] - LANES + 1, LANES):
                line = at // LANES
                rate = jnp.broadcast_to(rates[line : line + 1, :], (LANES, LANES)).T
                span = slice(at, at + LANES)
                gradient = part[top : top + LANES, :]
                moment = beta_one * held[1, i, span, :] + (1.0 - beta_one) * gradient
                held[1, i, span, :] = moment
                held[0, i, span, :] = held[0, i, span, :] - moment * rate
                at += LANES
        for copy in returns(i):
            copy.start()
    for i in range(count):
        for copy in returns(i):
            copy.wait()


def adam_blocks(rows_at, columns_at, parts, shape, full_width, common, before, held=None):
    groups = tuple(len(p) for p in parts)
    flat = [ref for p in parts for ref in p]
    own_hot, swapped, table, first, second = common
    rows, columns = table.shape
    count = len(groups)
    aliased = 0 if held is None else 2
    n_in = 8 + len(flat)
    size = shape[0] * shape[1]
    return pl.pallas_call(
        lambda *refs: adam_kernel(groups, full_width, aliased, *refs),
        out_shape=(
            jax.ShapeDtypeStruct((rows, columns), jnp.float32),
            jax.ShapeDtypeStruct((rows, columns), jnp.float32),
            jax.ShapeDtypeStruct(second.shape, jnp.float32),
        ),
        in_specs=[SMEM] * 3 + [VMEM] * (len(flat) + 1) + [ANY, ANY, VMEM, VMEM] + [HBM] * aliased,
        out_specs=[HBM, HBM, VMEM],
        scratch_shapes=[
            pltpu.VMEM((2, count) + shape, jnp.float32),
            pltpu.SemaphoreType.DMA((2, count)),
            pltpu.SemaphoreType.DMA((2, count)),
            pltpu.VMEM(second.shape, jnp.float32),
        ],
        input_output_aliases={n_in: 0, n_in + 1: 1} if aliased else {},
        compiler_params=pltpu.CompilerParams(vmem_limit_bytes=52 << 20),
        cost_estimate=pl.CostEstimate(
            flops=8 * count * size, bytes_accessed=20 * count * size, transcendentals=0
        ),
        name="adam_blocks",
    )(rows_at, columns_at, own_hot, *flat, swapped, table, first, second, before, *(held or ()))


def turned(row, wanted):
    return jnp.where(wanted, pltpu.roll(row, SLICE, 1), row)


def parcel_kernel(hot_ref, table, first, second, out_ref, sems):
    copies = []
    for which, source in enumerate((table, first)):
        for k in range(2):
            at = pl.ds(pl.multiple_of(hot_ref[k] * SLICE, SLICE), SLICE)
            to = pl.ds((2 * which + k) * SLICE, SLICE)
            copies.append(pltpu.make_async_copy(source.at[at, :], out_ref.at[to, :], sems.at[which, k]))
    for copy in copies:
        copy.start()
    left, right = (second[pl.ds(hot_ref[k] // 2, 1), :] for k in range(2))
    lane = lax.broadcasted_iota(jnp.int32, left.shape, 1)
    row = jnp.where(
        lane < SLICE, turned(left, hot_ref[0] % 2 == 1), turned(right, hot_ref[1] % 2 == 0)
    )
    out_ref[4 * SLICE :, :] = jnp.broadcast_to(
        jnp.concatenate([row, row], axis=1), (EXTRA, out_ref.shape[1])
    )
    for copy in copies:
        copy.wait()


def parcel_of(own_hot, table, first, second):
    return pl.pallas_call(
        parcel_kernel,
        out_shape=jax.ShapeDtypeStruct((4 * SLICE + EXTRA, table.shape[1]), jnp.float32),
        in_specs=[SMEM, ANY, ANY, VMEM],
        out_specs=VMEM,
        scratch_shapes=[pltpu.SemaphoreType.DMA((2, 2))],
        compiler_params=pltpu.CompilerParams(vmem_limit_bytes=52 << 20),
        name="parcel",
    )(own_hot, table, first, second)


def on_device(
    table_weights,
    moment_first,
    moment_second,
    hot_slices,
    upstream_grad,
    dedup_map,
    unique_rows,
    row_counts,
):
    n_table = lax.axis_size("table")
    n_far, n_pair = lax.axis_size("far"), lax.axis_size("pair")
    n_dp = n_far * n_pair
    position = lax.axis_index("table")
    far_at, pair_at = lax.axis_index("far"), lax.axis_index("pair")
    rows_dev, col_width = table_weights.shape
    full_width = col_width * lax.axis_size("col")
    block, share = rows_dev // n_far, col_width // n_pair
    half = block // 2

    own_hot = hot_slices[position]
    second_lines = moment_second.reshape(-1, LANES)
    parcel = parcel_of(own_hot, table_weights, moment_first, second_lines)
    swap = [(t, (t + n_table // 2) % n_table) for t in range(n_table)]
    swapped = lax.ppermute(parcel, "table", swap)
    slots = dedup_map.reshape(-1, GROUP * dedup_map.shape[1])
    slot_grad = slot_sums(
        slots, upstream_grad.T, hot_slices, row_counts, unique_rows, n_pair, rows_dev
    )
    slot_grad, swapped, own_hot, second_lines, far_at, pair_at = lax.optimization_barrier(
        (slot_grad, swapped, own_hot, second_lines, far_at, pair_at)
    )
    got = lax.all_to_all(slot_grad, ("table", "pair"), split_axis=0, concat_axis=0, tiled=True)
    got, swapped, own_hot, second_lines, far_at, pair_at = lax.optimization_barrier(
        (got, swapped, own_hot, second_lines, far_at, pair_at)
    )

    def begin_at(*offsets):
        return jnp.stack([(far_at + o + n_far) % n_far * block for o in offsets]).astype(jnp.int32)

    def send(value, axes, count, step):
        return lax.ppermute(value, axes, [(i, (i + step) % count) for i in range(count)])

    pieces, aims, other = place_first(got, begin_at(2), block)
    rise = send(other[:half], "far", n_far, 1)
    fall = send(other[half:], "far", n_far, -1)
    plus, minus = place_next(pieces, aims, begin_at(1, -1), block)
    rise = jnp.concatenate([plus[:half] + rise, plus[half:]], axis=0)
    fall = jnp.concatenate([minus[:half], minus[half:] + fall], axis=0)
    rise, fall = send(rise, "far", n_far, 1), send(fall, "far", n_far, -1)
    (mine,) = place_next(pieces, aims, begin_at(0), block)
    mine = mine + rise + fall
    squares = lax.psum(jnp.sum(mine * mine, axis=1), ("pair", "col")).reshape(-1, share)
    squares = jnp.pad(squares, ((0, EXTRA - squares.shape[0]), (0, 0)))
    own = jnp.concatenate([mine, squares], axis=0)

    ring = ("far", "pair")
    me = far_at * n_pair + pair_at
    common = (own_hot, swapped, table_weights, moment_first, second_lines)

    def update(arrived, second, held=None):
        at = jnp.stack([(me + o + n_dp) % n_dp for o, _ in arrived]).astype(jnp.int32)
        parts = [p for _, p in arrived]
        return adam_blocks(
            at // n_pair, at % n_pair, parts, (block, share), full_width, common, second, held
        )

    rise, fall = send(own, ring, n_dp, 1), send(own, ring, n_dp, -1)
    arrived = [(0, [own]), (-1, [rise]), (1, [fall])]
    rise, fall = send(rise, ring, n_dp, 1), send(fall, ring, n_dp, -1)
    weights, first, second = update(arrived, second_lines)
    rise, fall, second = lax.optimization_barrier((rise, fall, second))
    arrived = [(-2, [rise]), (2, [fall])]
    rise, fall = send(rise, ring, n_dp, 1), send(fall, ring, n_dp, -1)
    arrived += [(-3, [rise]), (3, [fall])]
    rise, fall = send(rise[:half], ring, n_dp, 1), send(fall[half:], ring, n_dp, -1)
    weights, first, second = update(arrived, second, (weights, first))
    weights, first, second = update([(4, [rise, fall])], second, (weights, first))
    return (weights, first, second.reshape(-1))


def solution(mesh):
    n_table, n_dp, n_col = (mesh.shape[a] for a in ("table", "dp", "col"))
    inner = Mesh(mesh.devices.reshape(n_table, n_dp // 2, 2, n_col), ("table", "far", "pair", "col"))
    samples = ("table", "far", "pair")
    placed = (
        P("table", "col"),
        P("table", "col"),
        P("table"),
        P(),
        P(samples, "col"),
        P(samples, None),
        P(samples, None, None),
        P(samples, None),
    )
    return jax.shard_map(
        on_device,
        mesh=inner,
        in_specs=placed,
        out_specs=(P("table", "col"), P("table", "col"), P("table")),
        check_vma=False,
    )
```

```python
import jax
import jax.numpy as jnp
from jax import lax
from jax.experimental import pallas as pl
from jax.experimental.pallas import tpu as pltpu
from jax.sharding import Mesh
from jax.sharding import PartitionSpec as P

SLICE = 64
CAP = 256
LOW = 128
GROUP = 8
EXTRA = 8
LANES = 128

beta_one = 0.9
beta_two = 0.99
learn_rate = 0.1
eps_value = 1e-08

NT = (((1,), (1,)), ((), ()))
VMEM = pl.BlockSpec(memory_space=pltpu.VMEM)
SMEM = pl.BlockSpec(memory_space=pltpu.SMEM)
HBM = pl.BlockSpec(memory_space=pltpu.HBM)
ANY = pl.BlockSpec(memory_space=pl.ANY)


def digits(values):
    return values.astype(jnp.float32).astype(jnp.bfloat16)


def counting(shape):
    return digits(lax.broadcasted_iota(jnp.int32, shape, 0))


def one_hot(positions, wanted):
    return jnp.where(positions == wanted, jnp.bfloat16(1), jnp.bfloat16(0))


def target_row(owner, hot_ref, count_ref, rows, rows_dev):
    owners, n_hots = hot_ref.shape
    partner = (owner + owners // 2) % owners
    local_row = rows % rows_dev
    from_partner = rows // rows_dev == partner
    target = local_row
    for k in range(n_hots):
        moved = from_partner & (local_row // SLICE == hot_ref[partner, k])
        target = jnp.where(moved, hot_ref[owner, k] * SLICE + local_row % SLICE, target)
    used = lax.broadcasted_iota(jnp.int32, rows.shape, 1) < count_ref[0, owner]
    return jnp.where(used, target, rows_dev)


def slot_kernel(rows_dev, map_ref, grad_ref, hot_ref, count_ref, rows_ref, out_ref, tally, held, sems):
    groups, span = map_ref.shape
    owners, _, cap = tally.shape
    per_owner = cap // LOW
    highs = owners * per_owner
    sample = lax.broadcasted_iota(jnp.int32, (1, span), 1) // (span // GROUP)
    left_at = counting((highs * GROUP, span))
    right_at = counting((LOW, span))
    batch = 16

    def count(step, carry):
        first = pl.multiple_of(step * batch, batch)
        slots = map_ref[pl.ds(first, batch), :]
        lefts = digits((slots // LOW) * GROUP + sample)
        rights = digits(slots % LOW)
        for pair in range(batch // 2):
            halves = []
            for at in (2 * pair, 2 * pair + 1):
                left = one_hot(left_at, lefts[at : at + 1, :])
                right = one_hot(right_at, rights[at : at + 1, :])
                part = lax.dot_general(left, right, NT, preferred_element_type=jnp.float32)
                halves.append(part.reshape(highs, GROUP, LOW))
            both = jnp.concatenate(halves, axis=1).astype(jnp.bfloat16)
            both = both.reshape(owners, per_owner, 2 * GROUP, LOW)
            begin = pl.multiple_of(first * GROUP + pair * 2 * GROUP, 2 * GROUP)
            for k in range(per_owner):
                tally[:, pl.ds(begin, 2 * GROUP), k * LOW : (k + 1) * LOW] = both[:, k]
        return carry

    lax.fori_loop(0, groups // batch, count, 0)
    depth, shares, height, lanes = held.shape
    columns = (height - EXTRA) * lanes // cap

    def leave(owner):
        slot = owner % depth
        at = pl.ds(owner * shares, shares)
        return pltpu.make_async_copy(held.at[slot], out_ref.at[at], sems.at[slot])

    for owner in range(owners):
        if owner >= depth:
            leave(owner - depth).wait()
        slot = owner % depth
        total = jnp.dot(grad_ref[...], tally[owner], preferred_element_type=jnp.float32)
        aim = target_row(owner, hot_ref, count_ref, rows_ref[0, owner : owner + 1, :], rows_dev)
        aim = jnp.broadcast_to(aim.astype(jnp.float32), (EXTRA, cap))
        for side in range(cap // lanes):
            cut = slice(side * lanes, (side + 1) * lanes)
            aim_at = height - EXTRA + side * EXTRA * lanes // cap
            for share in range(shares):
                part = total[share * columns : (share + 1) * columns, cut]
                held[slot, share, side * columns : (side + 1) * columns, :] = part
                held[slot, share, aim_at : aim_at + EXTRA * lanes // cap, :] = aim[: EXTRA * lanes // cap, cut]
        leave(owner).start()
    for owner in range(owners - depth, owners):
        leave(owner).wait()


def slot_sums(slots, grad_t, hot_slices, row_counts, unique_rows, shares, rows_dev):
    _, owners, cap = unique_rows.shape
    columns, samples = grad_t.shape
    height = columns // shares * cap // LANES + EXTRA
    depth = 4
    return pl.pallas_call(
        lambda *refs: slot_kernel(rows_dev, *refs),
        out_shape=jax.ShapeDtypeStruct((owners * shares, height, LANES), jnp.float32),
        in_specs=[VMEM, VMEM, SMEM, SMEM, VMEM],
        out_specs=HBM,
        scratch_shapes=[
            pltpu.VMEM((owners, samples, cap), jnp.bfloat16),
            pltpu.VMEM((depth, shares, height, LANES), jnp.float32),
            pltpu.SemaphoreType.DMA((depth,)),
        ],
        compiler_params=pltpu.CompilerParams(vmem_limit_bytes=50 << 20),
        name="slot_sums",
    )(slots, grad_t, hot_slices, row_counts, unique_rows)


def add_block(pieces, aims, start, out_ref, select):
    part, width = select.shape
    columns = out_ref.shape[1]
    place = counting((part, CAP))
    for top in range(0, out_ref.shape[0], part):
        for at in range(0, width, CAP):
            row = aims[:1, at : at + CAP] - (start + top)
            row = digits(jnp.where((row >= 0) & (row < part), row, -1))
            select[:, at : at + CAP] = one_hot(place, row)
        both = lax.dot_general(select[...], pieces[...], NT, preferred_element_type=jnp.float32)
        out_ref[top : top + part, :] = both[:, :columns] + both[:, columns:]


def place_first_kernel(start_ref, got_ref, pieces, aims, out_ref, select, held, sems):
    sources, height, lanes = got_ref.shape
    columns = (height - EXTRA) * lanes // CAP
    batch = sources // sems.shape[0]

    def fetch(k):
        at = pl.ds(k * batch, batch)
        return pltpu.make_async_copy(got_ref.at[at], held.at[at], sems.at[k])

    for k in range(sems.shape[0]):
        fetch(k).start()
    for source in range(sources):
        if source % batch == 0:
            fetch(source // batch).wait()
        for side in range(CAP // lanes):
            value = held[source, side * columns : (side + 1) * columns, :]
            upper = value.astype(jnp.bfloat16)
            lower = (value - upper.astype(jnp.float32)).astype(jnp.bfloat16)
            at = source * CAP + side * lanes
            pieces[:columns, at : at + lanes] = upper
            pieces[columns:, at : at + lanes] = lower
            aim_at = height - EXTRA + side * EXTRA * lanes // CAP
            aim = held[source, aim_at : aim_at + 1, :].astype(jnp.int32)
            aims[:, at : at + lanes] = jnp.broadcast_to(aim, (EXTRA, lanes))
    add_block(pieces, aims, start_ref[0], out_ref, select)


def place_next_kernel(start_ref, pieces, aims, *refs):
    outs, select = refs[:-1], refs[-1]
    for k, out_ref in enumerate(outs):
        add_block(pieces, aims, start_ref[k], out_ref, select)


def place_cost(blocks, block, width, columns):
    flops = 4 * blocks * block * width * columns
    return pl.CostEstimate(flops=flops, bytes_accessed=8 << 20, transcendentals=0)


def place_first(got, start, block):
    sources, height, lanes = got.shape
    columns = (height - EXTRA) * lanes // CAP
    width = sources * CAP
    return pl.pallas_call(
        place_first_kernel,
        out_shape=(
            jax.ShapeDtypeStruct((2 * columns, width), jnp.bfloat16),
            jax.ShapeDtypeStruct((EXTRA, width), jnp.int32),
            jax.ShapeDtypeStruct((block, columns), jnp.float32),
        ),
        in_specs=[SMEM, HBM],
        out_specs=[VMEM] * 3,
        scratch_shapes=[
            pltpu.VMEM((CAP, width), jnp.bfloat16),
            pltpu.VMEM(got.shape, jnp.float32),
            pltpu.SemaphoreType.DMA((8,)),
        ],
        compiler_params=pltpu.CompilerParams(vmem_limit_bytes=46 << 20),
        cost_estimate=place_cost(1, block, width, columns),
        name="place_first",
    )(start, got)


def place_next(pieces, aims, starts, block):
    columns, width = pieces.shape[0] // 2, pieces.shape[1]
    count = starts.shape[0]
    return pl.pallas_call(
        place_next_kernel,
        out_shape=tuple(jax.ShapeDtypeStruct((block, columns), jnp.float32) for _ in range(count)),
        in_specs=[SMEM, VMEM, VMEM],
        out_specs=[VMEM] * count,
        scratch_shapes=[pltpu.VMEM((CAP, width), jnp.bfloat16)],
        compiler_params=pltpu.CompilerParams(vmem_limit_bytes=18 << 20),
        cost_estimate=place_cost(count, block, width, columns),
        name="place_next",
    )(starts, pieces, aims)


def block_copies(table, first, held, sems, rows_at, columns_at, i, back):
    rows, columns = held.shape[2:]
    at = pl.ds(pl.multiple_of(rows_at * rows, rows), rows)
    cut = pl.ds(pl.multiple_of(columns_at * columns, columns), columns)
    pairs = [(source.at[at, cut], held.at[which, i]) for which, source in enumerate((table, first))]
    if back:
        pairs = [(here, there) for there, here in pairs]
    return [pltpu.make_async_copy(a, b, sems.at[which, i]) for which, (a, b) in enumerate(pairs)]


def put_swapped(where_ref, hots, swapped, held, rows_at, columns_at, i):
    rows, columns = held.shape[2:]
    per_block = rows // SLICE
    for k in range(2):
        hot = hots[where_ref[0], k]

        @pl.when(hot // per_block == rows_at)
        def _():
            at = pl.ds(pl.multiple_of((hot % per_block) * SLICE, SLICE), SLICE)
            cut = pl.ds(pl.multiple_of(columns_at * columns, columns), columns)
            for which in range(2):
                begin = (2 * which + k) * SLICE
                held[which, i, at, :] = swapped[begin : begin + SLICE, cut]


def fetch_kernel(row_ref, column_ref, where_ref, hots, swapped, table, first, held, sems):
    for copy in block_copies(table, first, held, sems, row_ref[0], column_ref[0], 0, False):
        copy.start()
    for copy in block_copies(table, first, held, sems, row_ref[0], column_ref[0], 0, False):
        copy.wait()
    put_swapped(where_ref, hots, swapped, held, row_ref[0], column_ref[0], 0)


def fetch_block(rows_at, columns_at, shape, common):
    where, hots, swapped, _, table, first, _ = common
    return pl.pallas_call(
        fetch_kernel,
        out_shape=jax.ShapeDtypeStruct((2, 1) + shape, jnp.float32),
        in_specs=[SMEM] * 4 + [VMEM, ANY, ANY],
        out_specs=VMEM,
        scratch_shapes=[pltpu.SemaphoreType.DMA((2, 1))],
        compiler_params=pltpu.CompilerParams(vmem_limit_bytes=52 << 20),
        name="fetch_block",
    )(rows_at, columns_at, where, hots, swapped, table, first)


def adam_kernel(groups, full_width, fetched, *refs):
    count = len(groups)
    row_ref, column_ref, where_ref, hots = refs[:4]
    parts = refs[4 : 4 + sum(groups)]
    swapped, squares, table, first, second, before = refs[4 + sum(groups) : 10 + sum(groups)]
    out_table, out_first, out_second, held, in_sem, out_sem, placed_second = refs[-7:]
    rows, columns = held.shape[2:]
    lines = rows // LANES
    source = refs[10 + sum(groups)] if fetched else held

    def arrivals(i):
        return block_copies(table, first, held, in_sem, row_ref[i], column_ref[i], i, False)

    def returns(i):
        return block_copies(out_table, out_first, held, out_sem, row_ref[i], column_ref[i], i, True)

    if not fetched:
        for i in range(count):
            for copy in arrivals(i):
                copy.start()
    out_second[...] = before[...]
    placed = second[...]
    lead = swapped[4 * SLICE : 4 * SLICE + 1, :LANES]
    line_at = lax.broadcasted_iota(jnp.int32, placed.shape, 0)
    side_at = lax.broadcasted_iota(jnp.int32, placed.shape, 1) // SLICE
    for k in range(2):
        hot = hots[where_ref[0], k]
        here = (line_at == hot // 2) & (side_at == hot % 2)
        placed = jnp.where(here, turned(lead, hot % 2 != k), placed)
    placed_second[...] = placed
    blocks = second.shape[0] // lines
    sharers = squares.shape[0] // blocks
    begin = 0
    for i in range(count):
        mine = parts[begin : begin + groups[i]]
        begin += groups[i]
        block = row_ref[i]
        total = jnp.sum(squares[pl.ds(block * sharers, sharers)], axis=0)[:lines]
        old = placed_second[pl.ds(block * lines, lines), :]
        fresh = beta_two * old + (1.0 - beta_two) * (total / full_width)
        out_second[pl.ds(block * lines, lines), :] = fresh
        scaled = jnp.sqrt(fresh / (1.0 - beta_two**8)) + eps_value
        rates = (learn_rate / (1.0 - beta_one**8)) / scaled
        if not fetched:
            for copy in arrivals(i):
                copy.wait()
            put_swapped(where_ref, hots, swapped, held, block, column_ref[i], i)
        at = 0
        for part in mine:
            for top in range(0, part.shape[0], LANES):
                line = at // LANES
                rate = jnp.broadcast_to(rates[line : line + 1, :], (LANES, LANES)).T
                span = slice(at, at + LANES)
                gradient = part[top : top + LANES, :]
                moment = beta_one * source[1, i, span, :] + (1.0 - beta_one) * gradient
                weight = source[0, i, span, :] - moment * rate
                held[1, i, span, :] = moment
                held[0, i, span, :] = weight
                at += LANES
        for copy in returns(i):
            copy.start()
    for i in range(count):
        for copy in returns(i):
            copy.wait()


def adam_blocks(rows_at, columns_at, parts, shape, full_width, common, before, held=None, fetched=None):
    groups = tuple(len(p) for p in parts)
    flat = [ref for p in parts for ref in p]
    where, hots, swapped, squares, table, first, second = common
    count = len(groups)
    more = [] if fetched is None else [fetched]
    n_in = 10 + len(flat) + len(more)
    size = shape[0] * shape[1]
    kept = [] if held is None else list(held)
    return pl.pallas_call(
        lambda *refs: adam_kernel(groups, full_width, fetched is not None, *refs),
        out_shape=(
            jax.ShapeDtypeStruct(table.shape, jnp.float32),
            jax.ShapeDtypeStruct(table.shape, jnp.float32),
            jax.ShapeDtypeStruct(second.shape, jnp.float32),
        ),
        in_specs=[SMEM] * 4
        + [VMEM] * (len(flat) + 2)
        + [ANY, ANY, VMEM, VMEM]
        + [VMEM] * len(more)
        + [HBM] * len(kept),
        out_specs=[HBM, HBM, VMEM],
        scratch_shapes=[
            pltpu.VMEM((2, count) + shape, jnp.float32),
            pltpu.SemaphoreType.DMA((2, count)),
            pltpu.SemaphoreType.DMA((2, count)),
            pltpu.VMEM(second.shape, jnp.float32),
        ],
        input_output_aliases={n_in: 0, n_in + 1: 1} if kept else {},
        compiler_params=pltpu.CompilerParams(vmem_limit_bytes=52 << 20),
        cost_estimate=pl.CostEstimate(
            flops=8 * count * size, bytes_accessed=20 * count * size, transcendentals=0
        ),
        name="adam_blocks",
    )(
        rows_at, columns_at, where, hots, *flat, swapped, squares, table, first, second, before,
        *more, *kept,
    )


def turned(row, wanted):
    return jnp.where(wanted, pltpu.roll(row, SLICE, 1), row)


def parcel_kernel(where_ref, hots, table, first, second, out_ref, sems):
    hot_ref = [hots[where_ref[0], k] for k in range(2)]
    copies = []
    for which, source in enumerate((table, first)):
        for k in range(2):
            at = pl.ds(pl.multiple_of(hot_ref[k] * SLICE, SLICE), SLICE)
            to = pl.ds((2 * which + k) * SLICE, SLICE)
            copies.append(pltpu.make_async_copy(source.at[at, :], out_ref.at[to, :], sems.at[which, k]))
    for copy in copies:
        copy.start()
    left, right = (second[pl.ds(hot_ref[k] // 2, 1), :] for k in range(2))
    lane = lax.broadcasted_iota(jnp.int32, left.shape, 1)
    row = jnp.where(
        lane < SLICE, turned(left, hot_ref[0] % 2 == 1), turned(right, hot_ref[1] % 2 == 0)
    )
    out_ref[4 * SLICE :, :] = jnp.broadcast_to(
        jnp.concatenate([row, row], axis=1), (EXTRA, out_ref.shape[1])
    )
    for copy in copies:
        copy.wait()


def parcel_of(where, hots, table, first, second):
    return pl.pallas_call(
        parcel_kernel,
        out_shape=jax.ShapeDtypeStruct((4 * SLICE + EXTRA, table.shape[1]), jnp.float32),
        in_specs=[SMEM, SMEM, ANY, ANY, VMEM],
        out_specs=VMEM,
        scratch_shapes=[pltpu.SemaphoreType.DMA((2, 2))],
        compiler_params=pltpu.CompilerParams(vmem_limit_bytes=52 << 20),
        name="parcel",
    )(where, hots, table, first, second)


def on_device(
    table_weights,
    moment_first,
    moment_second,
    hot_slices,
    upstream_grad,
    dedup_map,
    unique_rows,
    row_counts,
):
    n_table = lax.axis_size("table")
    n_far, n_pair = lax.axis_size("far"), lax.axis_size("pair")
    n_dp = n_far * n_pair
    position = lax.axis_index("table")
    far_at, pair_at = lax.axis_index("far"), lax.axis_index("pair")
    rows_dev, col_width = table_weights.shape
    full_width = col_width * lax.axis_size("col")
    block, share = rows_dev // n_far, col_width // n_pair
    half = block // 2

    second_lines = moment_second.reshape(-1, LANES)
    slots = dedup_map.reshape(-1, GROUP * dedup_map.shape[1])
    slot_grad = slot_sums(
        slots, upstream_grad.T, hot_slices, row_counts, unique_rows, n_pair, rows_dev
    )
    slot_grad, position, far_at, pair_at = lax.optimization_barrier(
        (slot_grad, position, far_at, pair_at)
    )
    got = lax.all_to_all(slot_grad, ("table", "pair"), split_axis=0, concat_axis=0, tiled=True)
    got, position, far_at, pair_at, second_lines = lax.optimization_barrier(
        (got, position, far_at, pair_at, second_lines)
    )

    def begin_at(*offsets):
        return jnp.stack([(far_at + o + n_far) % n_far * block for o in offsets]).astype(jnp.int32)

    def send(value, axes, count, step):
        return lax.ppermute(value, axes, [(i, (i + step) % count) for i in range(count)])

    pieces, aims, other = place_first(got, begin_at(2), block)
    rise = send(other[:half], "far", n_far, 1)
    fall = send(other[half:], "far", n_far, -1)
    plus, minus = place_next(pieces, aims, begin_at(1, -1), block)
    rise = jnp.concatenate([plus[:half] + rise, plus[half:]], axis=0)
    fall = jnp.concatenate([minus[:half], minus[half:] + fall], axis=0)
    where = position.reshape(1)
    rise, fall, where, second_lines = lax.optimization_barrier((rise, fall, where, second_lines))
    rise, fall = send(rise, "far", n_far, 1), send(fall, "far", n_far, -1)
    parcel = parcel_of(where, hot_slices, table_weights, moment_first, second_lines)
    swapped = send(parcel, "table", n_table, n_table // 2)
    (mine,) = place_next(pieces, aims, begin_at(0), block)
    mine = mine + rise + fall
    mine, swapped = lax.optimization_barrier((mine, swapped))

    ring = ("far", "pair")
    me = far_at * n_pair + pair_at
    n_all = n_dp * lax.axis_size("col")
    own_squares = jnp.sum(mine * mine, axis=1).reshape(-1, LANES)
    own_squares = jnp.pad(own_squares, ((0, EXTRA - own_squares.shape[0]), (0, 0)))
    squares = lax.all_to_all(
        jnp.broadcast_to(own_squares[None], (n_all,) + own_squares.shape),
        ("far", "pair", "col"),
        split_axis=0,
        concat_axis=0,
        tiled=True,
    )
    common = (where, hot_slices, swapped, squares, table_weights, moment_first, second_lines)
    shape = (block, share)

    def at_ring(offsets):
        at = jnp.stack([(me + o + n_dp) % n_dp for o in offsets]).astype(jnp.int32)
        return at // n_pair, at % n_pair

    def update(offsets, parts, second, held=None, fetched=None):
        return adam_blocks(*at_ring(offsets), parts, shape, full_width, common, second, held, fetched)

    rise, fall = send(mine, ring, n_dp, 1), send(mine, ring, n_dp, -1)
    parts = [[mine], [rise], [fall]]
    rise, fall = send(rise, ring, n_dp, 1), send(fall, ring, n_dp, -1)
    weights, first, second = update((0, -1, 1), parts, second_lines)
    rise, fall, second = lax.optimization_barrier((rise, fall, second))
    parts = [[rise], [fall]]
    rise, fall = send(rise, ring, n_dp, 1), send(fall, ring, n_dp, -1)
    fetched = fetch_block(*at_ring((4,)), shape, common)
    weights, first, second = update((-2, 2), parts, second, (weights, first))
    rise, fall, second, fetched = lax.optimization_barrier((rise, fall, second, fetched))
    parts = [[rise], [fall]]
    rise, fall = send(rise[:half], ring, n_dp, 1), send(fall[half:], ring, n_dp, -1)
    weights, first, second = update((-3, 3), parts, second, (weights, first))
    weights, first, second = update((4,), [[rise, fall]], second, (weights, first), fetched)
    return (weights, first, second.reshape(-1))


def solution(mesh):
    n_table, n_dp, n_col = (mesh.shape[a] for a in ("table", "dp", "col"))
    inner = Mesh(mesh.devices.reshape(n_table, n_dp // 2, 2, n_col), ("table", "far", "pair", "col"))
    samples = ("table", "far", "pair")
    placed = (
        P("table", "col"),
        P("table", "col"),
        P("table"),
        P(),
        P(samples, "col"),
        P(samples, None),
        P(samples, None, None),
        P(samples, None),
    )
    return jax.shard_map(
        on_device,
        mesh=inner,
        in_specs=placed,
        out_specs=(P("table", "col"), P("table", "col"), P("table")),
        check_vma=False,
    )
```

```python
import jax
import jax.numpy as jnp
from jax import lax
from jax.experimental import pallas as pl
from jax.experimental.pallas import tpu as pltpu
from jax.sharding import Mesh
from jax.sharding import PartitionSpec as P

SLICE = 64
CAP = 256
LOW = 128
GROUP = 8
EXTRA = 8
LANES = 128

beta_one = 0.9
beta_two = 0.99
learn_rate = 0.1
eps_value = 1e-08

NT = (((1,), (1,)), ((), ()))
VMEM = pl.BlockSpec(memory_space=pltpu.VMEM)
SMEM = pl.BlockSpec(memory_space=pltpu.SMEM)
HBM = pl.BlockSpec(memory_space=pltpu.HBM)
ANY = pl.BlockSpec(memory_space=pl.ANY)


def digits(values):
    return values.astype(jnp.float32).astype(jnp.bfloat16)


def counting(shape):
    return digits(lax.broadcasted_iota(jnp.int32, shape, 0))


def one_hot(positions, wanted):
    return jnp.where(positions == wanted, jnp.bfloat16(1), jnp.bfloat16(0))


def target_row(owner, hot_ref, count_ref, rows, rows_dev):
    n_hots, owners = hot_ref.shape
    partner = (owner + owners // 2) % owners
    local_row = rows % rows_dev
    from_partner = rows // rows_dev == partner
    target = local_row
    for k in range(n_hots):
        moved = from_partner & (local_row // SLICE == hot_ref[k, partner])
        target = jnp.where(moved, hot_ref[k, owner] * SLICE + local_row % SLICE, target)
    used = lax.broadcasted_iota(jnp.int32, rows.shape, 1) < count_ref[0, owner]
    return jnp.where(used, target, rows_dev)


def slot_kernel(rows_dev, map_ref, grad_ref, hot_ref, count_ref, rows_ref, out_ref, tally, held, sems):
    groups, span = map_ref.shape
    owners, _, cap = tally.shape
    per_owner = cap // LOW
    highs = owners * per_owner
    sample = lax.broadcasted_iota(jnp.int32, (1, span), 1) // (span // GROUP)
    left_at = counting((highs * GROUP, span))
    right_at = counting((LOW, span))
    batch = 32

    def count(step, carry):
        first = pl.multiple_of(step * batch, batch)
        slots = map_ref[pl.ds(first, batch), :]
        lefts = digits((slots // LOW) * GROUP + sample)
        rights = digits(slots % LOW)
        for pair in range(batch // 2):
            halves = []
            for at in (2 * pair, 2 * pair + 1):
                left = one_hot(left_at, lefts[at : at + 1, :])
                right = one_hot(right_at, rights[at : at + 1, :])
                part = lax.dot_general(left, right, NT, preferred_element_type=jnp.float32)
                halves.append(part.reshape(highs, GROUP, LOW))
            both = jnp.concatenate(halves, axis=1).astype(jnp.bfloat16)
            both = both.reshape(owners, per_owner, 2 * GROUP, LOW)
            begin = pl.multiple_of(first * GROUP + pair * 2 * GROUP, 2 * GROUP)
            for k in range(per_owner):
                tally[:, pl.ds(begin, 2 * GROUP), k * LOW : (k + 1) * LOW] = both[:, k]
        return carry

    lax.fori_loop(0, groups // batch, count, 0)
    depth, shares, height, lanes = held.shape
    columns = (height - EXTRA) * lanes // cap

    def leave(owner):
        slot = owner % depth
        at = pl.ds(owner * shares, shares)
        return pltpu.make_async_copy(held.at[slot], out_ref.at[at], sems.at[slot])

    for owner in range(owners):
        if owner >= depth:
            leave(owner - depth).wait()
        slot = owner % depth
        total = jnp.dot(grad_ref[...], tally[owner], preferred_element_type=jnp.float32)
        aim = target_row(owner, hot_ref, count_ref, rows_ref[0, owner : owner + 1, :], rows_dev)
        aim = jnp.broadcast_to(aim.astype(jnp.float32), (EXTRA, cap))
        for side in range(cap // lanes):
            cut = slice(side * lanes, (side + 1) * lanes)
            aim_at = height - EXTRA + side * EXTRA * lanes // cap
            for share in range(shares):
                part = total[share * columns : (share + 1) * columns, cut]
                held[slot, share, side * columns : (side + 1) * columns, :] = part
                held[slot, share, aim_at : aim_at + EXTRA * lanes // cap, :] = aim[: EXTRA * lanes // cap, cut]
        leave(owner).start()
    for owner in range(owners - depth, owners):
        leave(owner).wait()


def slot_sums(slots, grad_t, hot_slices, row_counts, unique_rows, shares, rows_dev):
    _, owners, cap = unique_rows.shape
    columns, samples = grad_t.shape
    height = columns // shares * cap // LANES + EXTRA
    depth = 4
    return pl.pallas_call(
        lambda *refs: slot_kernel(rows_dev, *refs),
        out_shape=jax.ShapeDtypeStruct((owners * shares, height, LANES), jnp.float32),
        in_specs=[VMEM, VMEM, SMEM, SMEM, VMEM],
        out_specs=HBM,
        scratch_shapes=[
            pltpu.VMEM((owners, samples, cap), jnp.bfloat16),
            pltpu.VMEM((depth, shares, height, LANES), jnp.float32),
            pltpu.SemaphoreType.DMA((depth,)),
        ],
        compiler_params=pltpu.CompilerParams(vmem_limit_bytes=50 << 20),
        name="slot_sums",
    )(slots, grad_t, hot_slices, row_counts, unique_rows)


def add_block(pieces, aims, start, out_ref, select):
    part, width = select.shape
    columns = out_ref.shape[1]
    place = counting((part, CAP))
    for top in range(0, out_ref.shape[0], part):
        for at in range(0, width, CAP):
            row = aims[:1, at : at + CAP] - (start + top)
            row = digits(jnp.where((row >= 0) & (row < part), row, -1))
            select[:, at : at + CAP] = one_hot(place, row)
        both = lax.dot_general(select[...], pieces[...], NT, preferred_element_type=jnp.float32)
        out_ref[top : top + part, :] = both[:, :columns] + both[:, columns:]


def place_first_kernel(start_ref, got_ref, pieces, aims, out_ref, select, held, sems):
    sources, height, lanes = got_ref.shape
    columns = (height - EXTRA) * lanes // CAP
    batch = sources // sems.shape[0]

    def fetch(k):
        at = pl.ds(k * batch, batch)
        return pltpu.make_async_copy(got_ref.at[at], held.at[at], sems.at[k])

    for k in range(sems.shape[0]):
        fetch(k).start()
    rows = out_ref.shape[0]
    place = counting((CAP, CAP))
    span = batch * CAP
    sums = [jnp.zeros((CAP, 2 * columns), jnp.float32) for _ in range(rows // CAP)]
    for k in range(sems.shape[0]):
        fetch(k).wait()
        for source in range(k * batch, (k + 1) * batch):
            for side in range(CAP // lanes):
                value = held[source, side * columns : (side + 1) * columns, :]
                upper = value.astype(jnp.bfloat16)
                lower = (value - upper.astype(jnp.float32)).astype(jnp.bfloat16)
                at = source * CAP + side * lanes
                pieces[:columns, at : at + lanes] = upper
                pieces[columns:, at : at + lanes] = lower
                aim_at = height - EXTRA + side * EXTRA * lanes // CAP
                aim = held[source, aim_at : aim_at + 1, :].astype(jnp.int32)
                aims[:, at : at + lanes] = jnp.broadcast_to(aim, (EXTRA, lanes))
        for part in range(rows // CAP):
            for at in range(k * span, (k + 1) * span, CAP):
                row = aims[:1, at : at + CAP] - (start_ref[0] + part * CAP)
                row = digits(jnp.where((row >= 0) & (row < CAP), row, -1))
                select[part * CAP : (part + 1) * CAP, at - k * span : at - k * span + CAP] = one_hot(
                    place, row
                )
            sums[part] += lax.dot_general(
                select[part * CAP : (part + 1) * CAP, :span],
                pieces[:, k * span : (k + 1) * span],
                NT,
                preferred_element_type=jnp.float32,
            )
    for part in range(rows // CAP):
        both = sums[part]
        out_ref[part * CAP : (part + 1) * CAP, :] = both[:, :columns] + both[:, columns:]


def place_next_kernel(start_ref, pieces, aims, *refs):
    outs, select = refs[:-1], refs[-1]
    for k, out_ref in enumerate(outs):
        add_block(pieces, aims, start_ref[k], out_ref, select)


def place_cost(blocks, block, width, columns):
    flops = 4 * blocks * block * width * columns
    return pl.CostEstimate(flops=flops, bytes_accessed=8 << 20, transcendentals=0)


def place_first(got, start, block):
    sources, height, lanes = got.shape
    columns = (height - EXTRA) * lanes // CAP
    width = sources * CAP
    return pl.pallas_call(
        place_first_kernel,
        out_shape=(
            jax.ShapeDtypeStruct((2 * columns, width), jnp.bfloat16),
            jax.ShapeDtypeStruct((EXTRA, width), jnp.int32),
            jax.ShapeDtypeStruct((block, columns), jnp.float32),
        ),
        in_specs=[SMEM, HBM],
        out_specs=[VMEM] * 3,
        scratch_shapes=[
            pltpu.VMEM((block, width // 8), jnp.bfloat16),
            pltpu.VMEM(got.shape, jnp.float32),
            pltpu.SemaphoreType.DMA((8,)),
        ],
        compiler_params=pltpu.CompilerParams(vmem_limit_bytes=46 << 20),
        cost_estimate=place_cost(1, block, width, columns),
        name="place_first",
    )(start, got)


def place_next(pieces, aims, starts, block):
    columns, width = pieces.shape[0] // 2, pieces.shape[1]
    count = starts.shape[0]
    return pl.pallas_call(
        place_next_kernel,
        out_shape=tuple(jax.ShapeDtypeStruct((block, columns), jnp.float32) for _ in range(count)),
        in_specs=[SMEM, VMEM, VMEM],
        out_specs=[VMEM] * count,
        scratch_shapes=[pltpu.VMEM((CAP, width), jnp.bfloat16)],
        compiler_params=pltpu.CompilerParams(vmem_limit_bytes=18 << 20),
        cost_estimate=place_cost(count, block, width, columns),
        name="place_next",
    )(starts, pieces, aims)


def block_copies(table, first, held, sems, rows_at, columns_at, i, back):
    rows, columns = held.shape[2:]
    at = pl.ds(pl.multiple_of(rows_at * rows, rows), rows)
    cut = pl.ds(pl.multiple_of(columns_at * columns, columns), columns)
    pairs = [(source.at[at, cut], held.at[which, i]) for which, source in enumerate((table, first))]
    if back:
        pairs = [(here, there) for there, here in pairs]
    return [pltpu.make_async_copy(a, b, sems.at[which, i]) for which, (a, b) in enumerate(pairs)]


def put_swapped(where_ref, hots, swapped, held, rows_at, columns_at, i):
    rows, columns = held.shape[2:]
    per_block = rows // SLICE
    for k in range(2):
        hot = hots[k, where_ref[0]]

        @pl.when(hot // per_block == rows_at)
        def _():
            at = pl.ds(pl.multiple_of((hot % per_block) * SLICE, SLICE), SLICE)
            cut = pl.ds(pl.multiple_of(columns_at * columns, columns), columns)
            for which in range(2):
                begin = (2 * which + k) * SLICE
                held[which, i, at, :] = swapped[begin : begin + SLICE, cut]


def fetch_kernel(row_ref, column_ref, where_ref, hots, swapped, table, first, held, sems):
    count = held.shape[1]
    copies = [
        block_copies(table, first, held, sems, row_ref[0], column_ref[i], i, False)
        for i in range(count)
    ]
    for i in range(count):
        for copy in copies[i]:
            copy.start()
    for i in range(count):
        for copy in copies[i]:
            copy.wait()
        put_swapped(where_ref, hots, swapped, held, row_ref[0], column_ref[i], i)


def fetch_blocks(rows_at, columns_at, shape, common):
    where, hots, swapped, table, first, _ = common
    count = columns_at.shape[0]
    return pl.pallas_call(
        fetch_kernel,
        out_shape=jax.ShapeDtypeStruct((2, count) + shape, jnp.float32),
        in_specs=[SMEM] * 4 + [VMEM, ANY, ANY],
        out_specs=VMEM,
        scratch_shapes=[pltpu.SemaphoreType.DMA((2, count))],
        compiler_params=pltpu.CompilerParams(vmem_limit_bytes=52 << 20),
        name="fetch_blocks",
    )(rows_at, columns_at, where, hots, swapped, table, first)


def adam_kernel(layout, n_parts, full_width, fetched, *refs):
    count = len(layout)
    row_ref, column_ref, flip_ref, where_ref, hots = refs[:5]
    parts = refs[5 : 5 + n_parts]
    swapped, table, first, second, before = refs[5 + n_parts : 10 + n_parts]
    out_table, out_first, out_second, held, in_sem, out_sem, placed_second = refs[-7:]
    rows, columns = held.shape[2:]
    lines = rows // LANES
    source = refs[10 + n_parts] if fetched else held
    block = row_ref[0]

    def arrivals(i):
        return block_copies(table, first, held, in_sem, block, column_ref[i], i, False)

    def returns(i):
        return block_copies(out_table, out_first, held, out_sem, block, column_ref[i], i, True)

    def read(piece, begin, end):
        here, there = (parts[k] for k in piece)
        if here is there:
            return here[begin:end, :]
        return jnp.where(flip_ref[0] == 0, here[begin:end, :], there[begin:end, :])

    if not fetched:
        for i in range(count):
            for copy in arrivals(i):
                copy.start()
    out_second[...] = before[...]
    placed = second[...]
    lead = swapped[4 * SLICE : 4 * SLICE + 1, :LANES]
    line_at = lax.broadcasted_iota(jnp.int32, placed.shape, 0)
    side_at = lax.broadcasted_iota(jnp.int32, placed.shape, 1) // SLICE
    for k in range(2):
        hot = hots[k, where_ref[0]]
        here = (line_at == hot // 2) & (side_at == hot % 2)
        placed = jnp.where(here, turned(lead, hot % 2 != k), placed)
    placed_second[...] = placed
    total = jnp.zeros((lines, LANES), jnp.float32)
    for pieces in layout:
        tail = parts[pieces[-1][0]].shape[0] - EXTRA
        total += read(pieces[-1], tail, tail + lines)
    old = placed_second[pl.ds(block * lines, lines), :]
    fresh = beta_two * old + (1.0 - beta_two) * (total / full_width)
    out_second[pl.ds(block * lines, lines), :] = fresh
    scaled = jnp.sqrt(fresh / (1.0 - beta_two**8)) + eps_value
    rates = (learn_rate / (1.0 - beta_one**8)) / scaled
    rates = [jnp.broadcast_to(rates[k : k + 1, :], (LANES, LANES)).T for k in range(lines)]
    for i in range(count):
        if not fetched:
            for copy in arrivals(i):
                copy.wait()
            put_swapped(where_ref, hots, swapped, held, block, column_ref[i], i)
        at = 0
        for piece in layout[i]:
            for top in range(0, parts[piece[0]].shape[0] - LANES + 1, LANES):
                span = slice(at, at + LANES)
                gradient = read(piece, top, top + LANES)
                moment = beta_one * source[1, i, span, :] + (1.0 - beta_one) * gradient
                weight = source[0, i, span, :] - moment * rates[at // LANES]
                held[1, i, span, :] = moment
                held[0, i, span, :] = weight
                at += LANES
        for copy in returns(i):
            copy.start()
    for i in range(count):
        for copy in returns(i):
            copy.wait()


def adam_block(rows_at, columns_at, flip, layout, parts, full_width, common, before, held=None, fetched=None):
    where, hots, swapped, table, first, second = common
    count = len(layout)
    shape = (parts[0].shape[0] - EXTRA, parts[0].shape[1])
    more = [] if fetched is None else [fetched]
    kept = [] if held is None else list(held)
    n_in = 10 + len(parts) + len(more)
    size = shape[0] * shape[1]
    return pl.pallas_call(
        lambda *refs: adam_kernel(layout, len(parts), full_width, fetched is not None, *refs),
        out_shape=(
            jax.ShapeDtypeStruct(table.shape, jnp.float32),
            jax.ShapeDtypeStruct(table.shape, jnp.float32),
            jax.ShapeDtypeStruct(second.shape, jnp.float32),
        ),
        in_specs=[SMEM] * 5
        + [VMEM] * (len(parts) + 1)
        + [ANY, ANY, VMEM, VMEM]
        + [VMEM] * len(more)
        + [HBM] * len(kept),
        out_specs=[HBM, HBM, VMEM],
        scratch_shapes=[
            pltpu.VMEM((2, count) + shape, jnp.float32),
            pltpu.SemaphoreType.DMA((2, count)),
            pltpu.SemaphoreType.DMA((2, count)),
            pltpu.VMEM(second.shape, jnp.float32),
        ],
        input_output_aliases={n_in: 0, n_in + 1: 1} if kept else {},
        compiler_params=pltpu.CompilerParams(vmem_limit_bytes=51 << 20),
        cost_estimate=pl.CostEstimate(
            flops=8 * count * size, bytes_accessed=20 * count * size, transcendentals=0
        ),
        name="adam_block",
    )(
        rows_at, columns_at, flip, where, hots, *parts, swapped, table, first, second, before,
        *more, *kept,
    )


def turned(row, wanted):
    return jnp.where(wanted, pltpu.roll(row, SLICE, 1), row)


def parcel_kernel(where_ref, hots, table, first, second, out_ref, sems):
    hot_ref = [hots[k, where_ref[0]] for k in range(2)]
    copies = []
    for which, source in enumerate((table, first)):
        for k in range(2):
            at = pl.ds(pl.multiple_of(hot_ref[k] * SLICE, SLICE), SLICE)
            to = pl.ds((2 * which + k) * SLICE, SLICE)
            copies.append(pltpu.make_async_copy(source.at[at, :], out_ref.at[to, :], sems.at[which, k]))
    for copy in copies:
        copy.start()
    left, right = (second[pl.ds(hot_ref[k] // 2, 1), :] for k in range(2))
    lane = lax.broadcasted_iota(jnp.int32, left.shape, 1)
    row = jnp.where(
        lane < SLICE, turned(left, hot_ref[0] % 2 == 1), turned(right, hot_ref[1] % 2 == 0)
    )
    out_ref[4 * SLICE :, :] = jnp.broadcast_to(
        jnp.concatenate([row, row], axis=1), (EXTRA, out_ref.shape[1])
    )
    for copy in copies:
        copy.wait()


def parcel_of(where, hots, table, first, second):
    return pl.pallas_call(
        parcel_kernel,
        out_shape=jax.ShapeDtypeStruct((4 * SLICE + EXTRA, table.shape[1]), jnp.float32),
        in_specs=[SMEM, SMEM, ANY, ANY, VMEM],
        out_specs=VMEM,
        scratch_shapes=[pltpu.SemaphoreType.DMA((2, 2))],
        compiler_params=pltpu.CompilerParams(vmem_limit_bytes=52 << 20),
        name="parcel",
    )(where, hots, table, first, second)


def on_device(
    table_weights,
    moment_first,
    moment_second,
    hot_slices,
    upstream_grad,
    dedup_map,
    unique_rows,
    row_counts,
):
    n_table = lax.axis_size("table")
    n_far, n_pair = lax.axis_size("far"), lax.axis_size("pair")
    n_dp = n_far * n_pair
    position = lax.axis_index("table")
    far_at, pair_at = lax.axis_index("far"), lax.axis_index("pair")
    rows_dev, col_width = table_weights.shape
    full_width = col_width * lax.axis_size("col")
    block, share = rows_dev // n_far, col_width // n_pair
    half = block // 2

    hots = hot_slices.T
    second_lines = moment_second.reshape(-1, LANES)
    slots = dedup_map.reshape(-1, GROUP * dedup_map.shape[1])
    slot_grad = slot_sums(
        slots, upstream_grad.T, hots, row_counts, unique_rows, n_pair, rows_dev
    )
    slot_grad, position, far_at, pair_at = lax.optimization_barrier(
        (slot_grad, position, far_at, pair_at)
    )
    got = lax.all_to_all(slot_grad, ("table", "pair"), split_axis=0, concat_axis=0, tiled=True)
    got, position, far_at, pair_at, second_lines = lax.optimization_barrier(
        (got, position, far_at, pair_at, second_lines)
    )

    def begin_at(*offsets):
        return jnp.stack([(far_at + o + n_far) % n_far * block for o in offsets]).astype(jnp.int32)

    def send(value, axes, count, step):
        return lax.ppermute(value, axes, [(i, (i + step) % count) for i in range(count)])

    pieces, aims, other = place_first(got, begin_at(2), block)
    rise = send(other[:half], "far", n_far, 1)
    fall = send(other[half:], "far", n_far, -1)
    plus, minus = place_next(pieces, aims, begin_at(1, -1), block)
    rise = jnp.concatenate([plus[:half] + rise, plus[half:]], axis=0)
    fall = jnp.concatenate([minus[:half], minus[half:] + fall], axis=0)
    where = position.reshape(1)
    rise, fall, where, second_lines = lax.optimization_barrier((rise, fall, where, second_lines))
    rise, fall = send(rise, "far", n_far, 1), send(fall, "far", n_far, -1)
    parcel = parcel_of(where, hots, table_weights, moment_first, second_lines)
    swapped = send(parcel, "table", n_table, n_table // 2)
    (mine,) = place_next(pieces, aims, begin_at(0), block)
    mine = mine + rise + fall
    mine, swapped = lax.optimization_barrier((mine, swapped))

    ring = ("far", "pair")
    squares = lax.psum(jnp.sum(mine * mine, axis=1).reshape(-1, LANES), "col")
    squares = jnp.pad(squares, ((0, EXTRA - squares.shape[0]), (0, 0)))
    own = jnp.concatenate([mine, squares], axis=0)
    common = (where, hots, swapped, table_weights, moment_first, second_lines)
    flip = pair_at.reshape(1)
    away = 2 * pair_at - 1
    straight = jnp.stack([pair_at, 1 - pair_at])
    crossed = jnp.stack([1 - pair_at, pair_at])

    def row_at(offset):
        return ((far_at + offset + n_far) % n_far).reshape(1)

    def update(offset, columns_at, layout, parts, second, held=None, fetched=None):
        at = row_at(offset)
        return adam_block(at, columns_at, flip, layout, parts, full_width, common, second, held, fetched)

    rise_1, fall_1 = send(own, ring, n_dp, 1), send(own, ring, n_dp, -1)
    rise_2, fall_2 = send(rise_1, ring, n_dp, 1), send(fall_1, ring, n_dp, -1)
    layout = (((0, 0),), ((2, 1),))
    weights, first, second = update(0, straight, layout, [own, rise_1, fall_1], second_lines)
    rise_2, fall_2, second = lax.optimization_barrier((rise_2, fall_2, second))
    rise_3, fall_3 = send(rise_2, ring, n_dp, 1), send(fall_2, ring, n_dp, -1)
    parts = [rise_1, fall_1, rise_2, fall_2]
    fetched = fetch_blocks(row_at(2), crossed, (block, share), common)
    weights, first, second = update(
        away, crossed, (((0, 1),), ((2, 3),)), parts, second, (weights, first)
    )
    rise_3, fall_3, second, fetched = lax.optimization_barrier((rise_3, fall_3, second, fetched))
    rise_4, fall_4 = send(rise_3[:half], ring, n_dp, 1), send(fall_3[half:], ring, n_dp, -1)
    parts = [rise_2, fall_2, rise_3, fall_3]
    weights, first, second = update(
        -away, straight, (((1, 0),), ((3, 2),)), parts, second, (weights, first)
    )
    parts = [rise_3, fall_3, rise_4, fall_4]
    weights, first, second = update(
        2, crossed, (((0, 1),), ((2, 2), (3, 3))), parts, second, (weights, first), fetched
    )
    return (weights, first, second.reshape(-1))


def solution(mesh):
    n_table, n_dp, n_col = (mesh.shape[a] for a in ("table", "dp", "col"))
    inner = Mesh(mesh.devices.reshape(n_table, n_dp // 2, 2, n_col), ("table", "far", "pair", "col"))
    samples = ("table", "far", "pair")
    placed = (
        P("table", "col"),
        P("table", "col"),
        P("table"),
        P(),
        P(samples, "col"),
        P(samples, None),
        P(samples, None, None),
        P(samples, None),
    )
    return jax.shard_map(
        on_device,
        mesh=inner,
        in_specs=placed,
        out_specs=(P("table", "col"), P("table", "col"), P("table")),
        check_vma=False,
    )
```

```python
import jax
import jax.numpy as jnp
from jax import lax
from jax.experimental import pallas as pl
from jax.experimental.pallas import tpu as pltpu
from jax.sharding import Mesh
from jax.sharding import PartitionSpec as P

SLICE = 64
CAP = 256
LOW = 128
GROUP = 8
EXTRA = 8
LANES = 128

beta_one = 0.9
beta_two = 0.99
learn_rate = 0.1
eps_value = 1e-08

NT = (((1,), (1,)), ((), ()))
VMEM = pl.BlockSpec(memory_space=pltpu.VMEM)
SMEM = pl.BlockSpec(memory_space=pltpu.SMEM)
HBM = pl.BlockSpec(memory_space=pltpu.HBM)
ANY = pl.BlockSpec(memory_space=pl.ANY)


def digits(values):
    return values.astype(jnp.float32).astype(jnp.bfloat16)


def counting(shape):
    return digits(lax.broadcasted_iota(jnp.int32, shape, 0))


def one_hot(positions, wanted):
    return jnp.where(positions == wanted, jnp.bfloat16(1), jnp.bfloat16(0))


def target_row(owner, hot_ref, count_ref, rows, rows_dev):
    n_hots, owners = hot_ref.shape
    partner = (owner + owners // 2) % owners
    local_row = rows % rows_dev
    from_partner = rows // rows_dev == partner
    target = local_row
    for k in range(n_hots):
        moved = from_partner & (local_row // SLICE == hot_ref[k, partner])
        target = jnp.where(moved, hot_ref[k, owner] * SLICE + local_row % SLICE, target)
    used = lax.broadcasted_iota(jnp.int32, rows.shape, 1) < count_ref[0, owner]
    return jnp.where(used, target, rows_dev)


def slot_kernel(
    rows_dev, map_ref, grad, hot_ref, count_ref, rows_ref, out_ref, tally, held, natural, grad_ref, sems, sem
):
    load = pltpu.make_async_copy(grad, natural, sem)
    load.start()
    groups, span = map_ref.shape
    owners, _, cap = tally.shape
    per_owner = cap // LOW
    highs = owners * per_owner
    sample = lax.broadcasted_iota(jnp.int32, (1, span), 1) // (span // GROUP)
    left_at = counting((highs * GROUP, span))
    right_at = counting((LOW, span))
    batch = 32

    def count(step, carry):
        first = pl.multiple_of(step * batch, batch)
        slots = map_ref[pl.ds(first, batch), :]
        lefts = digits((slots // LOW) * GROUP + sample)
        rights = digits(slots % LOW)
        for pair in range(batch // 2):
            halves = []
            for at in (2 * pair, 2 * pair + 1):
                left = one_hot(left_at, lefts[at : at + 1, :])
                right = one_hot(right_at, rights[at : at + 1, :])
                part = lax.dot_general(left, right, NT, preferred_element_type=jnp.float32)
                halves.append(part.reshape(highs, GROUP, LOW))
            both = jnp.concatenate(halves, axis=1).astype(jnp.bfloat16)
            both = both.reshape(owners, per_owner, 2 * GROUP, LOW)
            begin = pl.multiple_of(first * GROUP + pair * 2 * GROUP, 2 * GROUP)
            for k in range(per_owner):
                tally[:, pl.ds(begin, 2 * GROUP), k * LOW : (k + 1) * LOW] = both[:, k]
        return carry

    lax.fori_loop(0, groups // batch, count, 0)
    load.wait()
    grad_ref[...] = natural[...].T
    depth, shares, height, lanes = held.shape
    columns = (height - EXTRA) * lanes // cap

    def leave(owner):
        slot = owner % depth
        at = pl.ds(owner * shares, shares)
        return pltpu.make_async_copy(held.at[slot], out_ref.at[at], sems.at[slot])

    for owner in range(owners):
        if owner >= depth:
            leave(owner - depth).wait()
        slot = owner % depth
        total = jnp.dot(grad_ref[...], tally[owner], preferred_element_type=jnp.float32)
        aim = target_row(owner, hot_ref, count_ref, rows_ref[0, owner : owner + 1, :], rows_dev)
        aim = jnp.broadcast_to(aim.astype(jnp.float32), (EXTRA, cap))
        for side in range(cap // lanes):
            cut = slice(side * lanes, (side + 1) * lanes)
            aim_at = height - EXTRA + side * EXTRA * lanes // cap
            for share in range(shares):
                part = total[share * columns : (share + 1) * columns, cut]
                held[slot, share, side * columns : (side + 1) * columns, :] = part
                held[slot, share, aim_at : aim_at + EXTRA * lanes // cap, :] = aim[: EXTRA * lanes // cap, cut]
        leave(owner).start()
    for owner in range(owners - depth, owners):
        leave(owner).wait()


def slot_sums(slots, grad, hot_slices, row_counts, unique_rows, shares, rows_dev):
    _, owners, cap = unique_rows.shape
    samples, columns = grad.shape
    height = columns // shares * cap // LANES + EXTRA
    depth = 4
    return pl.pallas_call(
        lambda *refs: slot_kernel(rows_dev, *refs),
        out_shape=jax.ShapeDtypeStruct((owners * shares, height, LANES), jnp.float32),
        in_specs=[VMEM, ANY, SMEM, SMEM, VMEM],
        out_specs=HBM,
        scratch_shapes=[
            pltpu.VMEM((owners, samples, cap), jnp.bfloat16),
            pltpu.VMEM((depth, shares, height, LANES), jnp.float32),
            pltpu.VMEM(grad.shape, grad.dtype),
            pltpu.VMEM((columns, samples), grad.dtype),
            pltpu.SemaphoreType.DMA((depth,)),
            pltpu.SemaphoreType.DMA,
        ],
        compiler_params=pltpu.CompilerParams(vmem_limit_bytes=50 << 20),
        name="slot_sums",
    )(slots, grad, hot_slices, row_counts, unique_rows)


def add_block(pieces, aims, start, out_ref, select):
    part, width = select.shape
    columns = out_ref.shape[1]
    place = counting((part, CAP))
    for top in range(0, out_ref.shape[0], part):
        for at in range(0, width, CAP):
            row = aims[:1, at : at + CAP] - (start + top)
            row = digits(jnp.where((row >= 0) & (row < part), row, -1))
            select[:, at : at + CAP] = one_hot(place, row)
        both = lax.dot_general(select[...], pieces[...], NT, preferred_element_type=jnp.float32)
        out_ref[top : top + part, :] = both[:, :columns] + both[:, columns:]


def place_first_kernel(start_ref, got_ref, pieces, aims, out_ref, select, held, sems):
    sources, height, lanes = got_ref.shape
    columns = (height - EXTRA) * lanes // CAP
    batch = sources // sems.shape[0]

    def fetch(k):
        at = pl.ds(k * batch, batch)
        return pltpu.make_async_copy(got_ref.at[at], held.at[at], sems.at[k])

    for k in range(sems.shape[0]):
        fetch(k).start()
    rows = out_ref.shape[0]
    place = counting((CAP, CAP))
    span = batch * CAP
    sums = [jnp.zeros((CAP, 2 * columns), jnp.float32) for _ in range(rows // CAP)]
    for k in range(sems.shape[0]):
        fetch(k).wait()
        for source in range(k * batch, (k + 1) * batch):
            for side in range(CAP // lanes):
                value = held[source, side * columns : (side + 1) * columns, :]
                upper = value.astype(jnp.bfloat16)
                lower = (value - upper.astype(jnp.float32)).astype(jnp.bfloat16)
                at = source * CAP + side * lanes
                pieces[:columns, at : at + lanes] = upper
                pieces[columns:, at : at + lanes] = lower
                aim_at = height - EXTRA + side * EXTRA * lanes // CAP
                aim = held[source, aim_at : aim_at + 1, :].astype(jnp.int32)
                aims[:, at : at + lanes] = jnp.broadcast_to(aim, (EXTRA, lanes))
        for part in range(rows // CAP):
            for at in range(k * span, (k + 1) * span, CAP):
                row = aims[:1, at : at + CAP] - (start_ref[0] + part * CAP)
                row = digits(jnp.where((row >= 0) & (row < CAP), row, -1))
                select[part * CAP : (part + 1) * CAP, at - k * span : at - k * span + CAP] = one_hot(
                    place, row
                )
            sums[part] += lax.dot_general(
                select[part * CAP : (part + 1) * CAP, :span],
                pieces[:, k * span : (k + 1) * span],
                NT,
                preferred_element_type=jnp.float32,
            )
    for part in range(rows // CAP):
        both = sums[part]
        out_ref[part * CAP : (part + 1) * CAP, :] = both[:, :columns] + both[:, columns:]


def place_next_kernel(start_ref, pieces, aims, *refs):
    outs, select = refs[:-1], refs[-1]
    for k, out_ref in enumerate(outs):
        add_block(pieces, aims, start_ref[k], out_ref, select)


def place_cost(blocks, block, width, columns):
    flops = 4 * blocks * block * width * columns
    return pl.CostEstimate(flops=flops, bytes_accessed=8 << 20, transcendentals=0)


def place_first(got, start, block):
    sources, height, lanes = got.shape
    columns = (height - EXTRA) * lanes // CAP
    width = sources * CAP
    return pl.pallas_call(
        place_first_kernel,
        out_shape=(
            jax.ShapeDtypeStruct((2 * columns, width), jnp.bfloat16),
            jax.ShapeDtypeStruct((EXTRA, width), jnp.int32),
            jax.ShapeDtypeStruct((block, columns), jnp.float32),
        ),
        in_specs=[SMEM, HBM],
        out_specs=[VMEM] * 3,
        scratch_shapes=[
            pltpu.VMEM((block, width // 8), jnp.bfloat16),
            pltpu.VMEM(got.shape, jnp.float32),
            pltpu.SemaphoreType.DMA((8,)),
        ],
        compiler_params=pltpu.CompilerParams(vmem_limit_bytes=46 << 20),
        cost_estimate=place_cost(1, block, width, columns),
        name="place_first",
    )(start, got)


def place_next(pieces, aims, starts, block):
    columns, width = pieces.shape[0] // 2, pieces.shape[1]
    count = starts.shape[0]
    return pl.pallas_call(
        place_next_kernel,
        out_shape=tuple(jax.ShapeDtypeStruct((block, columns), jnp.float32) for _ in range(count)),
        in_specs=[SMEM, VMEM, VMEM],
        out_specs=[VMEM] * count,
        scratch_shapes=[pltpu.VMEM((CAP, width), jnp.bfloat16)],
        compiler_params=pltpu.CompilerParams(vmem_limit_bytes=18 << 20),
        cost_estimate=place_cost(count, block, width, columns),
        name="place_next",
    )(starts, pieces, aims)


def block_copies(table, first, held, sems, rows_at, columns_at, i, back):
    rows, columns = held.shape[2:]
    at = pl.ds(pl.multiple_of(rows_at * rows, rows), rows)
    cut = pl.ds(pl.multiple_of(columns_at * columns, columns), columns)
    pairs = [(source.at[at, cut], held.at[which, i]) for which, source in enumerate((table, first))]
    if back:
        pairs = [(here, there) for there, here in pairs]
    return [pltpu.make_async_copy(a, b, sems.at[which, i]) for which, (a, b) in enumerate(pairs)]


def put_swapped(where_ref, hots, swapped, held, rows_at, columns_at, i):
    rows, columns = held.shape[2:]
    per_block = rows // SLICE
    for k in range(2):
        hot = hots[k, where_ref[0]]

        @pl.when(hot // per_block == rows_at)
        def _():
            at = pl.ds(pl.multiple_of((hot % per_block) * SLICE, SLICE), SLICE)
            cut = pl.ds(pl.multiple_of(columns_at * columns, columns), columns)
            for which in range(2):
                begin = (2 * which + k) * SLICE
                held[which, i, at, :] = swapped[begin : begin + SLICE, cut]


def fetch_kernel(row_ref, column_ref, where_ref, hots, swapped, table, first, held, sems):
    for copy in block_copies(table, first, held, sems, row_ref[0], column_ref[0], 0, False):
        copy.start()
    for copy in block_copies(table, first, held, sems, row_ref[0], column_ref[0], 0, False):
        copy.wait()
    put_swapped(where_ref, hots, swapped, held, row_ref[0], column_ref[0], 0)


def fetch_block(rows_at, columns_at, shape, common):
    where, hots, swapped, _, table, first, _ = common
    return pl.pallas_call(
        fetch_kernel,
        out_shape=jax.ShapeDtypeStruct((2, 1) + shape, jnp.float32),
        in_specs=[SMEM] * 4 + [VMEM, ANY, ANY],
        out_specs=VMEM,
        scratch_shapes=[pltpu.SemaphoreType.DMA((2, 1))],
        compiler_params=pltpu.CompilerParams(vmem_limit_bytes=52 << 20),
        name="fetch_block",
    )(rows_at, columns_at, where, hots, swapped, table, first)


def adam_kernel(groups, full_width, fetched, *refs):
    count = len(groups)
    row_ref, column_ref, where_ref, hots = refs[:4]
    parts = refs[4 : 4 + sum(groups)]
    swapped, squares, table, first, second, before = refs[4 + sum(groups) : 10 + sum(groups)]
    out_table, out_first, out_second, held, in_sem, out_sem, placed_second = refs[-7:]
    rows, columns = held.shape[2:]
    lines = rows // LANES
    source = refs[10 + sum(groups)] if fetched else held

    def arrivals(i):
        return block_copies(table, first, held, in_sem, row_ref[i], column_ref[i], i, False)

    def returns(i):
        return block_copies(out_table, out_first, held, out_sem, row_ref[i], column_ref[i], i, True)

    if not fetched:
        for i in range(count):
            for copy in arrivals(i):
                copy.start()
    out_second[...] = before[...]
    placed = second[...]
    lead = swapped[4 * SLICE : 4 * SLICE + 1, :LANES]
    line_at = lax.broadcasted_iota(jnp.int32, placed.shape, 0)
    side_at = lax.broadcasted_iota(jnp.int32, placed.shape, 1) // SLICE
    for k in range(2):
        hot = hots[k, where_ref[0]]
        here = (line_at == hot // 2) & (side_at == hot % 2)
        placed = jnp.where(here, turned(lead, hot % 2 != k), placed)
    placed_second[...] = placed
    blocks = second.shape[0] // lines
    sharers = squares.shape[0] // blocks
    begin = 0
    for i in range(count):
        mine = parts[begin : begin + groups[i]]
        begin += groups[i]
        block = row_ref[i]
        total = jnp.sum(squares[pl.ds(block * sharers, sharers)], axis=0)[:lines]
        old = placed_second[pl.ds(block * lines, lines), :]
        fresh = beta_two * old + (1.0 - beta_two) * (total / full_width)
        out_second[pl.ds(block * lines, lines), :] = fresh
        scaled = jnp.sqrt(fresh / (1.0 - beta_two**8)) + eps_value
        rates = (learn_rate / (1.0 - beta_one**8)) / scaled
        if not fetched:
            for copy in arrivals(i):
                copy.wait()
            put_swapped(where_ref, hots, swapped, held, block, column_ref[i], i)
        at = 0
        for part in mine:
            for top in range(0, part.shape[0], LANES):
                line = at // LANES
                rate = jnp.broadcast_to(rates[line : line + 1, :], (LANES, LANES)).T
                span = slice(at, at + LANES)
                gradient = part[top : top + LANES, :]
                moment = beta_one * source[1, i, span, :] + (1.0 - beta_one) * gradient
                weight = source[0, i, span, :] - moment * rate
                held[1, i, span, :] = moment
                held[0, i, span, :] = weight
                at += LANES
        for copy in returns(i):
            copy.start()
    for i in range(count):
        for copy in returns(i):
            copy.wait()


def adam_blocks(rows_at, columns_at, parts, shape, full_width, common, before, held=None, fetched=None):
    groups = tuple(len(p) for p in parts)
    flat = [ref for p in parts for ref in p]
    where, hots, swapped, squares, table, first, second = common
    count = len(groups)
    more = [] if fetched is None else [fetched]
    n_in = 10 + len(flat) + len(more)
    size = shape[0] * shape[1]
    kept = [] if held is None else list(held)
    return pl.pallas_call(
        lambda *refs: adam_kernel(groups, full_width, fetched is not None, *refs),
        out_shape=(
            jax.ShapeDtypeStruct(table.shape, jnp.float32),
            jax.ShapeDtypeStruct(table.shape, jnp.float32),
            jax.ShapeDtypeStruct(second.shape, jnp.float32),
        ),
        in_specs=[SMEM] * 4
        + [VMEM] * (len(flat) + 2)
        + [ANY, ANY, VMEM, VMEM]
        + [VMEM] * len(more)
        + [HBM] * len(kept),
        out_specs=[HBM, HBM, VMEM],
        scratch_shapes=[
            pltpu.VMEM((2, count) + shape, jnp.float32),
            pltpu.SemaphoreType.DMA((2, count)),
            pltpu.SemaphoreType.DMA((2, count)),
            pltpu.VMEM(second.shape, jnp.float32),
        ],
        input_output_aliases={n_in: 0, n_in + 1: 1} if kept else {},
        compiler_params=pltpu.CompilerParams(vmem_limit_bytes=52 << 20),
        cost_estimate=pl.CostEstimate(
            flops=8 * count * size, bytes_accessed=20 * count * size, transcendentals=0
        ),
        name="adam_blocks",
    )(
        rows_at, columns_at, where, hots, *flat, swapped, squares, table, first, second, before,
        *more, *kept,
    )


def turned(row, wanted):
    return jnp.where(wanted, pltpu.roll(row, SLICE, 1), row)


def parcel_kernel(where_ref, hots, table, first, second, out_ref, sems):
    hot_ref = [hots[k, where_ref[0]] for k in range(2)]
    copies = []
    for which, source in enumerate((table, first)):
        for k in range(2):
            at = pl.ds(pl.multiple_of(hot_ref[k] * SLICE, SLICE), SLICE)
            to = pl.ds((2 * which + k) * SLICE, SLICE)
            copies.append(pltpu.make_async_copy(source.at[at, :], out_ref.at[to, :], sems.at[which, k]))
    for copy in copies:
        copy.start()
    left, right = (second[pl.ds(hot_ref[k] // 2, 1), :] for k in range(2))
    lane = lax.broadcasted_iota(jnp.int32, left.shape, 1)
    row = jnp.where(
        lane < SLICE, turned(left, hot_ref[0] % 2 == 1), turned(right, hot_ref[1] % 2 == 0)
    )
    out_ref[4 * SLICE :, :] = jnp.broadcast_to(
        jnp.concatenate([row, row], axis=1), (EXTRA, out_ref.shape[1])
    )
    for copy in copies:
        copy.wait()


def parcel_of(where, hots, table, first, second):
    return pl.pallas_call(
        parcel_kernel,
        out_shape=jax.ShapeDtypeStruct((4 * SLICE + EXTRA, table.shape[1]), jnp.float32),
        in_specs=[SMEM, SMEM, ANY, ANY, VMEM],
        out_specs=VMEM,
        scratch_shapes=[pltpu.SemaphoreType.DMA((2, 2))],
        compiler_params=pltpu.CompilerParams(vmem_limit_bytes=52 << 20),
        name="parcel",
    )(where, hots, table, first, second)


def on_device(
    table_weights,
    moment_first,
    moment_second,
    hot_slices,
    upstream_grad,
    dedup_map,
    unique_rows,
    row_counts,
):
    n_table = lax.axis_size("table")
    n_far, n_pair = lax.axis_size("far"), lax.axis_size("pair")
    n_dp = n_far * n_pair
    position = lax.axis_index("table")
    far_at, pair_at = lax.axis_index("far"), lax.axis_index("pair")
    rows_dev, col_width = table_weights.shape
    full_width = col_width * lax.axis_size("col")
    block, share = rows_dev // n_far, col_width // n_pair
    half = block // 2

    hots = hot_slices.T
    second_lines = moment_second.reshape(-1, LANES)
    slots = dedup_map.reshape(-1, GROUP * dedup_map.shape[1])
    slot_grad = slot_sums(
        slots, upstream_grad, hots, row_counts, unique_rows, n_pair, rows_dev
    )
    slot_grad, position, far_at, pair_at = lax.optimization_barrier(
        (slot_grad, position, far_at, pair_at)
    )
    got = lax.all_to_all(slot_grad, ("table", "pair"), split_axis=0, concat_axis=0, tiled=True)
    got, position, far_at, pair_at, second_lines = lax.optimization_barrier(
        (got, position, far_at, pair_at, second_lines)
    )

    def begin_at(*offsets):
        return jnp.stack([(far_at + o + n_far) % n_far * block for o in offsets]).astype(jnp.int32)

    def send(value, axes, count, step):
        return lax.ppermute(value, axes, [(i, (i + step) % count) for i in range(count)])

    pieces, aims, other = place_first(got, begin_at(2), block)
    rise = send(other[:half], "far", n_far, 1)
    fall = send(other[half:], "far", n_far, -1)
    plus, minus = place_next(pieces, aims, begin_at(1, -1), block)
    rise = jnp.concatenate([plus[:half] + rise, plus[half:]], axis=0)
    fall = jnp.concatenate([minus[:half], minus[half:] + fall], axis=0)
    where = position.reshape(1)
    rise, fall, where, second_lines = lax.optimization_barrier((rise, fall, where, second_lines))
    rise, fall = send(rise, "far", n_far, 1), send(fall, "far", n_far, -1)
    parcel = parcel_of(where, hots, table_weights, moment_first, second_lines)
    swapped = send(parcel, "table", n_table, n_table // 2)
    (mine,) = place_next(pieces, aims, begin_at(0), block)
    mine = mine + rise + fall
    mine, swapped = lax.optimization_barrier((mine, swapped))

    ring = ("far", "pair")
    me = far_at * n_pair + pair_at
    n_all = n_dp * lax.axis_size("col")
    own_squares = jnp.sum(mine * mine, axis=1).reshape(-1, LANES)
    own_squares = jnp.pad(own_squares, ((0, EXTRA - own_squares.shape[0]), (0, 0)))
    squares = lax.all_to_all(
        jnp.broadcast_to(own_squares[None], (n_all,) + own_squares.shape),
        ("far", "pair", "col"),
        split_axis=0,
        concat_axis=0,
        tiled=True,
    )
    common = (where, hots, swapped, squares, table_weights, moment_first, second_lines)
    shape = (block, share)

    def at_ring(offsets):
        at = jnp.stack([(me + o + n_dp) % n_dp for o in offsets]).astype(jnp.int32)
        return at // n_pair, at % n_pair

    def update(offsets, parts, second, held=None, fetched=None):
        return adam_blocks(*at_ring(offsets), parts, shape, full_width, common, second, held, fetched)

    rise, fall = send(mine, ring, n_dp, 1), send(mine, ring, n_dp, -1)
    parts = [[mine], [rise], [fall]]
    rise, fall = send(rise, ring, n_dp, 1), send(fall, ring, n_dp, -1)
    weights, first, second = update((0, -1, 1), parts, second_lines)
    rise, fall, second = lax.optimization_barrier((rise, fall, second))
    parts = [[rise], [fall]]
    rise, fall = send(rise, ring, n_dp, 1), send(fall, ring, n_dp, -1)
    fetched = fetch_block(*at_ring((4,)), shape, common)
    weights, first, second = update((-2, 2), parts, second, (weights, first))
    rise, fall, second, fetched = lax.optimization_barrier((rise, fall, second, fetched))
    parts = [[rise], [fall]]
    rise, fall = send(rise[:half], ring, n_dp, 1), send(fall[half:], ring, n_dp, -1)
    weights, first, second = update((-3, 3), parts, second, (weights, first))
    weights, first, second = update((4,), [[rise, fall]], second, (weights, first), fetched)
    return (weights, first, second.reshape(-1))


def solution(mesh):
    n_table, n_dp, n_col = (mesh.shape[a] for a in ("table", "dp", "col"))
    inner = Mesh(mesh.devices.reshape(n_table, n_dp // 2, 2, n_col), ("table", "far", "pair", "col"))
    samples = ("table", "far", "pair")
    placed = (
        P("table", "col"),
        P("table", "col"),
        P("table"),
        P(),
        P(samples, "col"),
        P(samples, None),
        P(samples, None, None),
        P(samples, None),
    )
    return jax.shard_map(
        on_device,
        mesh=inner,
        in_specs=placed,
        out_specs=(P("table", "col"), P("table", "col"), P("table")),
        check_vma=False,
    )
```

```python
import jax
import jax.numpy as jnp
from jax import lax
from jax.experimental import pallas as pl
from jax.experimental.pallas import tpu as pltpu
from jax.sharding import Mesh
from jax.sharding import PartitionSpec as P

SLICE = 64
CAP = 256
LOW = 128
GROUP = 8
EXTRA = 8
LANES = 128

beta_one = 0.9
beta_two = 0.99
learn_rate = 0.1
eps_value = 1e-08

NT = (((1,), (1,)), ((), ()))
VMEM = pl.BlockSpec(memory_space=pltpu.VMEM)
SMEM = pl.BlockSpec(memory_space=pltpu.SMEM)
HBM = pl.BlockSpec(memory_space=pltpu.HBM)
ANY = pl.BlockSpec(memory_space=pl.ANY)


def digits(values):
    return values.astype(jnp.float32).astype(jnp.bfloat16)


def counting(shape):
    return digits(lax.broadcasted_iota(jnp.int32, shape, 0))


def one_hot(positions, wanted):
    return jnp.where(positions == wanted, jnp.bfloat16(1), jnp.bfloat16(0))


def target_row(owner, hot_ref, count_ref, rows, rows_dev):
    n_hots, owners = hot_ref.shape
    partner = (owner + owners // 2) % owners
    local_row = rows % rows_dev
    from_partner = rows // rows_dev == partner
    target = local_row
    for k in range(n_hots):
        moved = from_partner & (local_row // SLICE == hot_ref[k, partner])
        target = jnp.where(moved, hot_ref[k, owner] * SLICE + local_row % SLICE, target)
    used = lax.broadcasted_iota(jnp.int32, rows.shape, 1) < count_ref[0, owner]
    return jnp.where(used, target, rows_dev)


def slot_kernel(rows_dev, map_ref, grad_ref, hot_ref, count_ref, rows_ref, out_ref, tally, held, sems):
    groups, span = map_ref.shape
    owners, _, cap = tally.shape
    per_owner = cap // LOW
    highs = owners * per_owner
    sample = lax.broadcasted_iota(jnp.int32, (1, span), 1) // (span // GROUP)
    left_at = counting((highs * GROUP, span))
    right_at = counting((LOW, span))
    batch = 32

    def count(step, carry):
        first = pl.multiple_of(step * batch, batch)
        slots = map_ref[pl.ds(first, batch), :]
        lefts = digits((slots // LOW) * GROUP + sample)
        rights = digits(slots % LOW)
        for pair in range(batch // 2):
            halves = []
            for at in (2 * pair, 2 * pair + 1):
                left = one_hot(left_at, lefts[at : at + 1, :])
                right = one_hot(right_at, rights[at : at + 1, :])
                part = lax.dot_general(left, right, NT, preferred_element_type=jnp.float32)
                halves.append(part.reshape(highs, GROUP, LOW))
            both = jnp.concatenate(halves, axis=1).astype(jnp.bfloat16)
            both = both.reshape(owners, per_owner, 2 * GROUP, LOW)
            begin = pl.multiple_of(first * GROUP + pair * 2 * GROUP, 2 * GROUP)
            for k in range(per_owner):
                tally[:, pl.ds(begin, 2 * GROUP), k * LOW : (k + 1) * LOW] = both[:, k]
        return carry

    lax.fori_loop(0, groups // batch, count, 0)
    depth, shares, height, lanes = held.shape
    columns = (height - EXTRA) * lanes // cap

    def leave(owner):
        slot = owner % depth
        at = pl.ds(owner * shares, shares)
        return pltpu.make_async_copy(held.at[slot], out_ref.at[at], sems.at[slot])

    for owner in range(owners):
        if owner >= depth:
            leave(owner - depth).wait()
        slot = owner % depth
        total = jnp.dot(grad_ref[...], tally[owner], preferred_element_type=jnp.float32)
        aim = target_row(owner, hot_ref, count_ref, rows_ref[0, owner : owner + 1, :], rows_dev)
        aim = jnp.broadcast_to(aim.astype(jnp.float32), (EXTRA, cap))
        for side in range(cap // lanes):
            cut = slice(side * lanes, (side + 1) * lanes)
            aim_at = height - EXTRA + side * EXTRA * lanes // cap
            for share in range(shares):
                part = total[share * columns : (share + 1) * columns, cut]
                held[slot, share, side * columns : (side + 1) * columns, :] = part
                held[slot, share, aim_at : aim_at + EXTRA * lanes // cap, :] = aim[: EXTRA * lanes // cap, cut]
        leave(owner).start()
    for owner in range(owners - depth, owners):
        leave(owner).wait()


def slot_sums(slots, grad_t, hot_slices, row_counts, unique_rows, shares, rows_dev):
    _, owners, cap = unique_rows.shape
    columns, samples = grad_t.shape
    height = columns // shares * cap // LANES + EXTRA
    depth = 4
    return pl.pallas_call(
        lambda *refs: slot_kernel(rows_dev, *refs),
        out_shape=jax.ShapeDtypeStruct((owners * shares, height, LANES), jnp.float32),
        in_specs=[VMEM, VMEM, SMEM, SMEM, VMEM],
        out_specs=HBM,
        scratch_shapes=[
            pltpu.VMEM((owners, samples, cap), jnp.bfloat16),
            pltpu.VMEM((depth, shares, height, LANES), jnp.float32),
            pltpu.SemaphoreType.DMA((depth,)),
        ],
        compiler_params=pltpu.CompilerParams(vmem_limit_bytes=50 << 20),
        name="slot_sums",
    )(slots, grad_t, hot_slices, row_counts, unique_rows)


def add_block(pieces, aims, start, out_ref, select):
    part, width = select.shape
    columns = out_ref.shape[1]
    place = counting((part, CAP))
    for top in range(0, out_ref.shape[0], part):
        for at in range(0, width, CAP):
            row = aims[:1, at : at + CAP] - (start + top)
            row = digits(jnp.where((row >= 0) & (row < part), row, -1))
            select[:, at : at + CAP] = one_hot(place, row)
        both = lax.dot_general(select[...], pieces[...], NT, preferred_element_type=jnp.float32)
        out_ref[top : top + part, :] = both[:, :columns] + both[:, columns:]


def place_first_kernel(start_ref, got_ref, pieces, aims, out_ref, select, held, sems):
    sources, height, lanes = got_ref.shape
    columns = (height - EXTRA) * lanes // CAP
    batch = sources // sems.shape[0]

    def fetch(k):
        at = pl.ds(k * batch, batch)
        return pltpu.make_async_copy(got_ref.at[at], held.at[at], sems.at[k])

    for k in range(sems.shape[0]):
        fetch(k).start()
    rows = out_ref.shape[0]
    place = counting((CAP, CAP))
    span = batch * CAP
    sums = [jnp.zeros((CAP, 2 * columns), jnp.float32) for _ in range(rows // CAP)]
    for k in range(sems.shape[0]):
        fetch(k).wait()
        for source in range(k * batch, (k + 1) * batch):
            for side in range(CAP // lanes):
                value = held[source, side * columns : (side + 1) * columns, :]
                upper = value.astype(jnp.bfloat16)
                lower = (value - upper.astype(jnp.float32)).astype(jnp.bfloat16)
                at = source * CAP + side * lanes
                pieces[:columns, at : at + lanes] = upper
                pieces[columns:, at : at + lanes] = lower
                aim_at = height - EXTRA + side * EXTRA * lanes // CAP
                aim = held[source, aim_at : aim_at + 1, :].astype(jnp.int32)
                aims[:, at : at + lanes] = jnp.broadcast_to(aim, (EXTRA, lanes))
        for part in range(rows // CAP):
            for at in range(k * span, (k + 1) * span, CAP):
                row = aims[:1, at : at + CAP] - (start_ref[0] + part * CAP)
                row = digits(jnp.where((row >= 0) & (row < CAP), row, -1))
                select[part * CAP : (part + 1) * CAP, at - k * span : at - k * span + CAP] = one_hot(
                    place, row
                )
            sums[part] += lax.dot_general(
                select[part * CAP : (part + 1) * CAP, :span],
                pieces[:, k * span : (k + 1) * span],
                NT,
                preferred_element_type=jnp.float32,
            )
    for part in range(rows // CAP):
        both = sums[part]
        out_ref[part * CAP : (part + 1) * CAP, :] = both[:, :columns] + both[:, columns:]


def place_next_kernel(start_ref, pieces, aims, *refs):
    outs, select = refs[:-1], refs[-1]
    for k, out_ref in enumerate(outs):
        add_block(pieces, aims, start_ref[k], out_ref, select)


def place_cost(blocks, block, width, columns):
    flops = 4 * blocks * block * width * columns
    return pl.CostEstimate(flops=flops, bytes_accessed=8 << 20, transcendentals=0)


def place_first(got, start, block):
    sources, height, lanes = got.shape
    columns = (height - EXTRA) * lanes // CAP
    width = sources * CAP
    return pl.pallas_call(
        place_first_kernel,
        out_shape=(
            jax.ShapeDtypeStruct((2 * columns, width), jnp.bfloat16),
            jax.ShapeDtypeStruct((EXTRA, width), jnp.int32),
            jax.ShapeDtypeStruct((block, columns), jnp.float32),
        ),
        in_specs=[SMEM, HBM],
        out_specs=[VMEM] * 3,
        scratch_shapes=[
            pltpu.VMEM((block, width // 8), jnp.bfloat16),
            pltpu.VMEM(got.shape, jnp.float32),
            pltpu.SemaphoreType.DMA((8,)),
        ],
        compiler_params=pltpu.CompilerParams(vmem_limit_bytes=46 << 20),
        cost_estimate=place_cost(1, block, width, columns),
        name="place_first",
    )(start, got)


def place_next(pieces, aims, starts, block):
    columns, width = pieces.shape[0] // 2, pieces.shape[1]
    count = starts.shape[0]
    return pl.pallas_call(
        place_next_kernel,
        out_shape=tuple(jax.ShapeDtypeStruct((block, columns), jnp.float32) for _ in range(count)),
        in_specs=[SMEM, VMEM, VMEM],
        out_specs=[VMEM] * count,
        scratch_shapes=[pltpu.VMEM((CAP, width), jnp.bfloat16)],
        compiler_params=pltpu.CompilerParams(vmem_limit_bytes=18 << 20),
        cost_estimate=place_cost(count, block, width, columns),
        name="place_next",
    )(starts, pieces, aims)


def block_copies(table, first, held, sems, rows_at, columns_at, i, back):
    rows, columns = held.shape[2:]
    at = pl.ds(pl.multiple_of(rows_at * rows, rows), rows)
    cut = pl.ds(pl.multiple_of(columns_at * columns, columns), columns)
    pairs = [(source.at[at, cut], held.at[which, i]) for which, source in enumerate((table, first))]
    if back:
        pairs = [(here, there) for there, here in pairs]
    return [pltpu.make_async_copy(a, b, sems.at[which, i]) for which, (a, b) in enumerate(pairs)]


def put_swapped(where_ref, hots, swapped, held, rows_at, columns_at, i):
    rows, columns = held.shape[2:]
    per_block = rows // SLICE
    for k in range(2):
        hot = hots[k, where_ref[0]]

        @pl.when(hot // per_block == rows_at)
        def _():
            at = pl.ds(pl.multiple_of((hot % per_block) * SLICE, SLICE), SLICE)
            cut = pl.ds(pl.multiple_of(columns_at * columns, columns), columns)
            for which in range(2):
                begin = (2 * which + k) * SLICE
                held[which, i, at, :] = swapped[begin : begin + SLICE, cut]


def fetch_kernel(row_ref, column_ref, where_ref, hots, swapped, table, first, held, sems):
    for copy in block_copies(table, first, held, sems, row_ref[0], column_ref[0], 0, False):
        copy.start()
    for copy in block_copies(table, first, held, sems, row_ref[0], column_ref[0], 0, False):
        copy.wait()
    put_swapped(where_ref, hots, swapped, held, row_ref[0], column_ref[0], 0)


def fetch_block(rows_at, columns_at, shape, common):
    where, hots, swapped, _, table, first, _ = common
    return pl.pallas_call(
        fetch_kernel,
        out_shape=jax.ShapeDtypeStruct((2, 1) + shape, jnp.float32),
        in_specs=[SMEM] * 4 + [VMEM, ANY, ANY],
        out_specs=VMEM,
        scratch_shapes=[pltpu.SemaphoreType.DMA((2, 1))],
        compiler_params=pltpu.CompilerParams(vmem_limit_bytes=52 << 20),
        name="fetch_block",
    )(rows_at, columns_at, where, hots, swapped, table, first)


def adam_kernel(groups, full_width, fetched, *refs):
    count = len(groups)
    row_ref, column_ref, where_ref, hots = refs[:4]
    parts = refs[4 : 4 + sum(groups)]
    swapped, squares, table, first, second, before = refs[4 + sum(groups) : 10 + sum(groups)]
    out_table, out_first, out_second, held, in_sem, out_sem, placed_second = refs[-7:]
    rows, columns = held.shape[2:]
    lines = rows // LANES
    source = refs[10 + sum(groups)] if fetched else held

    def arrivals(i):
        return block_copies(table, first, held, in_sem, row_ref[i], column_ref[i], i, False)

    def returns(i):
        return block_copies(out_table, out_first, held, out_sem, row_ref[i], column_ref[i], i, True)

    if not fetched:
        for i in range(count):
            for copy in arrivals(i):
                copy.start()
    out_second[...] = before[...]
    placed = second[...]
    lead = swapped[4 * SLICE : 4 * SLICE + 1, :LANES]
    line_at = lax.broadcasted_iota(jnp.int32, placed.shape, 0)
    side_at = lax.broadcasted_iota(jnp.int32, placed.shape, 1) // SLICE
    for k in range(2):
        hot = hots[k, where_ref[0]]
        here = (line_at == hot // 2) & (side_at == hot % 2)
        placed = jnp.where(here, turned(lead, hot % 2 != k), placed)
    placed_second[...] = placed
    blocks = second.shape[0] // lines
    sharers = squares.shape[0] // blocks
    begin = 0
    for i in range(count):
        mine = parts[begin : begin + groups[i]]
        begin += groups[i]
        block = row_ref[i]
        total = jnp.sum(squares[pl.ds(block * sharers, sharers)], axis=0)[:lines]
        old = placed_second[pl.ds(block * lines, lines), :]
        fresh = beta_two * old + (1.0 - beta_two) * (total / full_width)
        out_second[pl.ds(block * lines, lines), :] = fresh
        scaled = jnp.sqrt(fresh / (1.0 - beta_two**8)) + eps_value
        rates = (learn_rate / (1.0 - beta_one**8)) / scaled
        if not fetched:
            for copy in arrivals(i):
                copy.wait()
            put_swapped(where_ref, hots, swapped, held, block, column_ref[i], i)
        at = 0
        for part in mine:
            for top in range(0, part.shape[0], LANES):
                line = at // LANES
                rate = jnp.broadcast_to(rates[line : line + 1, :], (LANES, LANES)).T
                span = slice(at, at + LANES)
                gradient = part[top : top + LANES, :]
                moment = beta_one * source[1, i, span, :] + (1.0 - beta_one) * gradient
                weight = source[0, i, span, :] - moment * rate
                held[1, i, span, :] = moment
                held[0, i, span, :] = weight
                at += LANES
        for copy in returns(i):
            copy.start()
    for i in range(count):
        for copy in returns(i):
            copy.wait()


def adam_blocks(rows_at, columns_at, parts, shape, full_width, common, before, held=None, fetched=None):
    groups = tuple(len(p) for p in parts)
    flat = [ref for p in parts for ref in p]
    where, hots, swapped, squares, table, first, second = common
    count = len(groups)
    more = [] if fetched is None else [fetched]
    n_in = 10 + len(flat) + len(more)
    size = shape[0] * shape[1]
    kept = [] if held is None else list(held)
    return pl.pallas_call(
        lambda *refs: adam_kernel(groups, full_width, fetched is not None, *refs),
        out_shape=(
            jax.ShapeDtypeStruct(table.shape, jnp.float32),
            jax.ShapeDtypeStruct(table.shape, jnp.float32),
            jax.ShapeDtypeStruct(second.shape, jnp.float32),
        ),
        in_specs=[SMEM] * 4
        + [VMEM] * (len(flat) + 2)
        + [ANY, ANY, VMEM, VMEM]
        + [VMEM] * len(more)
        + [HBM] * len(kept),
        out_specs=[HBM, HBM, VMEM],
        scratch_shapes=[
            pltpu.VMEM((2, count) + shape, jnp.float32),
            pltpu.SemaphoreType.DMA((2, count)),
            pltpu.SemaphoreType.DMA((2, count)),
            pltpu.VMEM(second.shape, jnp.float32),
        ],
        input_output_aliases={n_in: 0, n_in + 1: 1} if kept else {},
        compiler_params=pltpu.CompilerParams(vmem_limit_bytes=52 << 20),
        cost_estimate=pl.CostEstimate(
            flops=8 * count * size, bytes_accessed=20 * count * size, transcendentals=0
        ),
        name="adam_blocks",
    )(
        rows_at, columns_at, where, hots, *flat, swapped, squares, table, first, second, before,
        *more, *kept,
    )


def turned(row, wanted):
    return jnp.where(wanted, pltpu.roll(row, SLICE, 1), row)


def parcel_kernel(where_ref, hots, table, first, second, out_ref, sems):
    hot_ref = [hots[k, where_ref[0]] for k in range(2)]
    copies = []
    for which, source in enumerate((table, first)):
        for k in range(2):
            at = pl.ds(pl.multiple_of(hot_ref[k] * SLICE, SLICE), SLICE)
            to = pl.ds((2 * which + k) * SLICE, SLICE)
            copies.append(pltpu.make_async_copy(source.at[at, :], out_ref.at[to, :], sems.at[which, k]))
    for copy in copies:
        copy.start()
    left, right = (second[pl.ds(hot_ref[k] // 2, 1), :] for k in range(2))
    lane = lax.broadcasted_iota(jnp.int32, left.shape, 1)
    row = jnp.where(
        lane < SLICE, turned(left, hot_ref[0] % 2 == 1), turned(right, hot_ref[1] % 2 == 0)
    )
    out_ref[4 * SLICE :, :] = jnp.broadcast_to(
        jnp.concatenate([row, row], axis=1), (EXTRA, out_ref.shape[1])
    )
    for copy in copies:
        copy.wait()


def parcel_of(where, hots, table, first, second):
    return pl.pallas_call(
        parcel_kernel,
        out_shape=jax.ShapeDtypeStruct((4 * SLICE + EXTRA, table.shape[1]), jnp.float32),
        in_specs=[SMEM, SMEM, ANY, ANY, VMEM],
        out_specs=VMEM,
        scratch_shapes=[pltpu.SemaphoreType.DMA((2, 2))],
        compiler_params=pltpu.CompilerParams(vmem_limit_bytes=52 << 20),
        name="parcel",
    )(where, hots, table, first, second)


def on_device(
    table_weights,
    moment_first,
    moment_second,
    hot_slices,
    upstream_grad,
    dedup_map,
    unique_rows,
    row_counts,
):
    n_table = lax.axis_size("table")
    n_far, n_pair = lax.axis_size("far"), lax.axis_size("pair")
    n_dp = n_far * n_pair
    position = lax.axis_index("table")
    far_at, pair_at = lax.axis_index("far"), lax.axis_index("pair")
    rows_dev, col_width = table_weights.shape
    full_width = col_width * lax.axis_size("col")
    block, share = rows_dev // n_far, col_width // n_pair
    half = block // 2

    hots = hot_slices.T
    second_lines = moment_second.reshape(-1, LANES)
    slots = dedup_map.reshape(-1, GROUP * dedup_map.shape[1])
    slot_grad = slot_sums(
        slots, upstream_grad.T, hots, row_counts, unique_rows, n_pair, rows_dev
    )
    slot_grad, position, far_at, pair_at = lax.optimization_barrier(
        (slot_grad, position, far_at, pair_at)
    )
    got = lax.all_to_all(slot_grad, ("table", "pair"), split_axis=0, concat_axis=0, tiled=True)
    got, position, far_at, pair_at, second_lines = lax.optimization_barrier(
        (got, position, far_at, pair_at, second_lines)
    )

    def begin_at(*offsets):
        return jnp.stack([(far_at + o + n_far) % n_far * block for o in offsets]).astype(jnp.int32)

    def send(value, axes, count, step):
        return lax.ppermute(value, axes, [(i, (i + step) % count) for i in range(count)])

    pieces, aims, other = place_first(got, begin_at(2), block)
    rise = send(other[:half], "far", n_far, 1)
    fall = send(other[half:], "far", n_far, -1)
    plus, minus = place_next(pieces, aims, begin_at(1, -1), block)
    rise = jnp.concatenate([plus[:half] + rise, plus[half:]], axis=0)
    fall = jnp.concatenate([minus[:half], minus[half:] + fall], axis=0)
    where = position.reshape(1)
    rise, fall, where, second_lines = lax.optimization_barrier((rise, fall, where, second_lines))
    rise, fall = send(rise, "far", n_far, 1), send(fall, "far", n_far, -1)
    parcel = parcel_of(where, hots, table_weights, moment_first, second_lines)
    swapped = send(parcel, "table", n_table, n_table // 2)
    (mine,) = place_next(pieces, aims, begin_at(0), block)
    mine = mine + rise + fall
    mine, swapped = lax.optimization_barrier((mine, swapped))

    ring = ("far", "pair")
    me = far_at * n_pair + pair_at
    n_all = n_dp * lax.axis_size("col")
    own_squares = jnp.sum(mine * mine, axis=1).reshape(-1, LANES)
    own_squares = jnp.pad(own_squares, ((0, EXTRA - own_squares.shape[0]), (0, 0)))
    squares = lax.all_to_all(
        jnp.broadcast_to(own_squares[None], (n_all,) + own_squares.shape),
        ("far", "pair", "col"),
        split_axis=0,
        concat_axis=0,
        tiled=True,
    )
    common = (where, hots, swapped, squares, table_weights, moment_first, second_lines)
    shape = (block, share)

    def at_ring(offsets):
        at = jnp.stack([(me + o + n_dp) % n_dp for o in offsets]).astype(jnp.int32)
        return at // n_pair, at % n_pair

    def update(offsets, parts, second, held=None, fetched=None):
        return adam_blocks(*at_ring(offsets), parts, shape, full_width, common, second, held, fetched)

    def hop(pieces, step):
        return [send(piece, ring, n_dp, step) for piece in pieces]

    own = [mine[:half], mine[half:]]
    rise, fall = hop(own, 1), hop(own, -1)
    parts = [own, rise, fall]
    rise, fall = hop(rise, 1), hop(fall, -1)
    weights, first, second = update((0, -1, 1), parts, second_lines)
    rise[1], fall[1], second = lax.optimization_barrier((rise[1], fall[1], second))
    parts = [rise, fall]
    rise, fall = hop(rise, 1), hop(fall, -1)
    fetched = fetch_block(*at_ring((4,)), shape, common)
    weights, first, second = update((-2, 2), parts, second, (weights, first))
    rise[1], fall[1], second, fetched = lax.optimization_barrier((rise[1], fall[1], second, fetched))
    parts = [rise, fall]
    last = [send(rise[0], ring, n_dp, 1), send(fall[1], ring, n_dp, -1)]
    weights, first, second = update((-3, 3), parts, second, (weights, first))
    weights, first, second = update((4,), [last], second, (weights, first), fetched)
    return (weights, first, second.reshape(-1))


def solution(mesh):
    n_table, n_dp, n_col = (mesh.shape[a] for a in ("table", "dp", "col"))
    inner = Mesh(mesh.devices.reshape(n_table, n_dp // 2, 2, n_col), ("table", "far", "pair", "col"))
    samples = ("table", "far", "pair")
    placed = (
        P("table", "col"),
        P("table", "col"),
        P("table"),
        P(),
        P(samples, "col"),
        P(samples, None),
        P(samples, None, None),
        P(samples, None),
    )
    return jax.shard_map(
        on_device,
        mesh=inner,
        in_specs=placed,
        out_specs=(P("table", "col"), P("table", "col"), P("table")),
        check_vma=False,
    )
```

```python
import jax
import jax.numpy as jnp
from jax import lax
from jax.experimental import pallas as pl
from jax.experimental.pallas import tpu as pltpu
from jax.sharding import Mesh
from jax.sharding import PartitionSpec as P

SLICE = 64
CAP = 256
LOW = 128
GROUP = 8
EXTRA = 8
LANES = 128

beta_one = 0.9
beta_two = 0.99
learn_rate = 0.1
eps_value = 1e-08

NT = (((1,), (1,)), ((), ()))
VMEM = pl.BlockSpec(memory_space=pltpu.VMEM)
SMEM = pl.BlockSpec(memory_space=pltpu.SMEM)
HBM = pl.BlockSpec(memory_space=pltpu.HBM)
ANY = pl.BlockSpec(memory_space=pl.ANY)


def digits(values):
    return values.astype(jnp.float32).astype(jnp.bfloat16)


def counting(shape):
    return digits(lax.broadcasted_iota(jnp.int32, shape, 0))


def one_hot(positions, wanted):
    return jnp.where(positions == wanted, jnp.bfloat16(1), jnp.bfloat16(0))


def target_row(owner, hot_ref, count_ref, rows, rows_dev):
    n_hots, owners = hot_ref.shape
    partner = (owner + owners // 2) % owners
    local_row = rows % rows_dev
    from_partner = rows // rows_dev == partner
    target = local_row
    for k in range(n_hots):
        moved = from_partner & (local_row // SLICE == hot_ref[k, partner])
        target = jnp.where(moved, hot_ref[k, owner] * SLICE + local_row % SLICE, target)
    used = lax.broadcasted_iota(jnp.int32, rows.shape, 1) < count_ref[0, owner]
    return jnp.where(used, target, rows_dev)


def slot_kernel(rows_dev, map_ref, grad_ref, hot_ref, count_ref, rows_ref, out_ref, tally, held, sems):
    groups, span = map_ref.shape
    owners, _, cap = tally.shape
    per_owner = cap // LOW
    highs = owners * per_owner
    sample = lax.broadcasted_iota(jnp.int32, (1, span), 1) // (span // GROUP)
    left_at = counting((highs * GROUP, span))
    right_at = counting((LOW, span))
    batch = 32

    def count(step, carry):
        first = pl.multiple_of(step * batch, batch)
        slots = map_ref[pl.ds(first, batch), :]
        lefts = digits((slots // LOW) * GROUP + sample)
        rights = digits(slots % LOW)
        for pair in range(batch // 2):
            halves = []
            for at in (2 * pair, 2 * pair + 1):
                left = one_hot(left_at, lefts[at : at + 1, :])
                right = one_hot(right_at, rights[at : at + 1, :])
                part = lax.dot_general(left, right, NT, preferred_element_type=jnp.float32)
                halves.append(part.reshape(highs, GROUP, LOW))
            both = jnp.concatenate(halves, axis=1).astype(jnp.bfloat16)
            both = both.reshape(owners, per_owner, 2 * GROUP, LOW)
            begin = pl.multiple_of(first * GROUP + pair * 2 * GROUP, 2 * GROUP)
            for k in range(per_owner):
                tally[:, pl.ds(begin, 2 * GROUP), k * LOW : (k + 1) * LOW] = both[:, k]
        return carry

    lax.fori_loop(0, groups // batch, count, 0)
    depth, shares, height, lanes = held.shape
    columns = (height - EXTRA) * lanes // cap

    def leave(owner):
        slot = owner % depth
        at = pl.ds(owner * shares, shares)
        return pltpu.make_async_copy(held.at[slot], out_ref.at[at], sems.at[slot])

    for owner in range(owners):
        if owner >= depth:
            leave(owner - depth).wait()
        slot = owner % depth
        total = jnp.dot(grad_ref[...], tally[owner], preferred_element_type=jnp.float32)
        aim = target_row(owner, hot_ref, count_ref, rows_ref[0, owner : owner + 1, :], rows_dev)
        aim = jnp.broadcast_to(aim.astype(jnp.float32), (EXTRA, cap))
        for side in range(cap // lanes):
            cut = slice(side * lanes, (side + 1) * lanes)
            aim_at = height - EXTRA + side * EXTRA * lanes // cap
            for share in range(shares):
                part = total[share * columns : (share + 1) * columns, cut]
                held[slot, share, side * columns : (side + 1) * columns, :] = part
                held[slot, share, aim_at : aim_at + EXTRA * lanes // cap, :] = aim[: EXTRA * lanes // cap, cut]
        leave(owner).start()
    for owner in range(owners - depth, owners):
        leave(owner).wait()


def slot_sums(slots, grad_t, hot_slices, row_counts, unique_rows, shares, rows_dev):
    _, owners, cap = unique_rows.shape
    columns, samples = grad_t.shape
    height = columns // shares * cap // LANES + EXTRA
    depth = 4
    return pl.pallas_call(
        lambda *refs: slot_kernel(rows_dev, *refs),
        out_shape=jax.ShapeDtypeStruct((owners * shares, height, LANES), jnp.float32),
        in_specs=[VMEM, VMEM, SMEM, SMEM, VMEM],
        out_specs=HBM,
        scratch_shapes=[
            pltpu.VMEM((owners, samples, cap), jnp.bfloat16),
            pltpu.VMEM((depth, shares, height, LANES), jnp.float32),
            pltpu.SemaphoreType.DMA((depth,)),
        ],
        compiler_params=pltpu.CompilerParams(vmem_limit_bytes=50 << 20),
        name="slot_sums",
    )(slots, grad_t, hot_slices, row_counts, unique_rows)


def add_block(pieces, aims, start, out_ref, select):
    part, width = select.shape
    columns = out_ref.shape[1]
    place = counting((part, CAP))
    for top in range(0, out_ref.shape[0], part):
        for at in range(0, width, CAP):
            row = aims[:1, at : at + CAP] - (start + top)
            row = digits(jnp.where((row >= 0) & (row < part), row, -1))
            select[:, at : at + CAP] = one_hot(place, row)
        both = lax.dot_general(select[...], pieces[...], NT, preferred_element_type=jnp.float32)
        out_ref[top : top + part, :] = both[:, :columns] + both[:, columns:]


def place_first_kernel(start_ref, got_ref, pieces, aims, out_ref, select, held, sems):
    sources, height, lanes = got_ref.shape
    columns = (height - EXTRA) * lanes // CAP
    batch = sources // sems.shape[0]

    def fetch(k):
        at = pl.ds(k * batch, batch)
        return pltpu.make_async_copy(got_ref.at[at], held.at[at], sems.at[k])

    for k in range(sems.shape[0]):
        fetch(k).start()
    rows = out_ref.shape[0]
    place = counting((CAP, CAP))
    span = batch * CAP
    sums = [jnp.zeros((CAP, 2 * columns), jnp.float32) for _ in range(rows // CAP)]
    for k in range(sems.shape[0]):
        fetch(k).wait()
        for source in range(k * batch, (k + 1) * batch):
            for side in range(CAP // lanes):
                value = held[source, side * columns : (side + 1) * columns, :]
                upper = value.astype(jnp.bfloat16)
                lower = (value - upper.astype(jnp.float32)).astype(jnp.bfloat16)
                at = source * CAP + side * lanes
                pieces[:columns, at : at + lanes] = upper
                pieces[columns:, at : at + lanes] = lower
                aim_at = height - EXTRA + side * EXTRA * lanes // CAP
                aim = held[source, aim_at : aim_at + 1, :].astype(jnp.int32)
                aims[:, at : at + lanes] = jnp.broadcast_to(aim, (EXTRA, lanes))
        for part in range(rows // CAP):
            for at in range(k * span, (k + 1) * span, CAP):
                row = aims[:1, at : at + CAP] - (start_ref[0] + part * CAP)
                row = digits(jnp.where((row >= 0) & (row < CAP), row, -1))
                select[part * CAP : (part + 1) * CAP, at - k * span : at - k * span + CAP] = one_hot(
                    place, row
                )
            sums[part] += lax.dot_general(
                select[part * CAP : (part + 1) * CAP, :span],
                pieces[:, k * span : (k + 1) * span],
                NT,
                preferred_element_type=jnp.float32,
            )
    for part in range(rows // CAP):
        both = sums[part]
        out_ref[part * CAP : (part + 1) * CAP, :] = both[:, :columns] + both[:, columns:]


def place_next_kernel(start_ref, pieces, aims, *refs):
    outs, select = refs[:-1], refs[-1]
    for k, out_ref in enumerate(outs):
        add_block(pieces, aims, start_ref[k], out_ref, select)


def place_cost(blocks, block, width, columns):
    flops = 4 * blocks * block * width * columns
    return pl.CostEstimate(flops=flops, bytes_accessed=8 << 20, transcendentals=0)


def place_first(got, start, block):
    sources, height, lanes = got.shape
    columns = (height - EXTRA) * lanes // CAP
    width = sources * CAP
    return pl.pallas_call(
        place_first_kernel,
        out_shape=(
            jax.ShapeDtypeStruct((2 * columns, width), jnp.bfloat16),
            jax.ShapeDtypeStruct((EXTRA, width), jnp.int32),
            jax.ShapeDtypeStruct((block, columns), jnp.float32),
        ),
        in_specs=[SMEM, HBM],
        out_specs=[VMEM] * 3,
        scratch_shapes=[
            pltpu.VMEM((block, width // 8), jnp.bfloat16),
            pltpu.VMEM(got.shape, jnp.float32),
            pltpu.SemaphoreType.DMA((8,)),
        ],
        compiler_params=pltpu.CompilerParams(vmem_limit_bytes=46 << 20),
        cost_estimate=place_cost(1, block, width, columns),
        name="place_first",
    )(start, got)


def place_next(pieces, aims, starts, block):
    columns, width = pieces.shape[0] // 2, pieces.shape[1]
    count = starts.shape[0]
    return pl.pallas_call(
        place_next_kernel,
        out_shape=tuple(jax.ShapeDtypeStruct((block, columns), jnp.float32) for _ in range(count)),
        in_specs=[SMEM, VMEM, VMEM],
        out_specs=[VMEM] * count,
        scratch_shapes=[pltpu.VMEM((CAP, width), jnp.bfloat16)],
        compiler_params=pltpu.CompilerParams(vmem_limit_bytes=18 << 20),
        cost_estimate=place_cost(count, block, width, columns),
        name="place_next",
    )(starts, pieces, aims)


def block_copies(table, first, held, sems, rows_at, columns_at, i, back):
    rows, columns = held.shape[2:]
    at = pl.ds(pl.multiple_of(rows_at * rows, rows), rows)
    cut = pl.ds(pl.multiple_of(columns_at * columns, columns), columns)
    pairs = [(source.at[at, cut], held.at[which, i]) for which, source in enumerate((table, first))]
    if back:
        pairs = [(here, there) for there, here in pairs]
    return [pltpu.make_async_copy(a, b, sems.at[which, i]) for which, (a, b) in enumerate(pairs)]


def put_swapped(where_ref, hots, swapped, held, rows_at, columns_at, i):
    rows, columns = held.shape[2:]
    per_block = rows // SLICE
    for k in range(2):
        hot = hots[k, where_ref[0]]

        @pl.when(hot // per_block == rows_at)
        def _():
            at = pl.ds(pl.multiple_of((hot % per_block) * SLICE, SLICE), SLICE)
            cut = pl.ds(pl.multiple_of(columns_at * columns, columns), columns)
            for which in range(2):
                begin = (2 * which + k) * SLICE
                held[which, i, at, :] = swapped[begin : begin + SLICE, cut]


def fetch_kernel(row_ref, column_ref, where_ref, hots, swapped, table, first, held, sems):
    for copy in block_copies(table, first, held, sems, row_ref[0], column_ref[0], 0, False):
        copy.start()
    for copy in block_copies(table, first, held, sems, row_ref[0], column_ref[0], 0, False):
        copy.wait()
    put_swapped(where_ref, hots, swapped, held, row_ref[0], column_ref[0], 0)


def fetch_block(rows_at, columns_at, shape, common):
    where, hots, swapped, _, table, first, _ = common
    return pl.pallas_call(
        fetch_kernel,
        out_shape=jax.ShapeDtypeStruct((2, 1) + shape, jnp.float32),
        in_specs=[SMEM] * 4 + [VMEM, ANY, ANY],
        out_specs=VMEM,
        scratch_shapes=[pltpu.SemaphoreType.DMA((2, 1))],
        compiler_params=pltpu.CompilerParams(vmem_limit_bytes=52 << 20),
        name="fetch_block",
    )(rows_at, columns_at, where, hots, swapped, table, first)


def adam_kernel(groups, full_width, fetched, *refs):
    count = len(groups)
    row_ref, column_ref, where_ref, hots = refs[:4]
    parts = refs[4 : 4 + sum(groups)]
    swapped, squares, table, first, second, before = refs[4 + sum(groups) : 10 + sum(groups)]
    out_table, out_first, out_second, held, in_sem, out_sem, placed_second = refs[-7:]
    rows, columns = held.shape[2:]
    lines = rows // LANES
    source = refs[10 + sum(groups)] if fetched else held

    def arrivals(i):
        return block_copies(table, first, held, in_sem, row_ref[i], column_ref[i], i, False)

    def returns(i):
        return block_copies(out_table, out_first, held, out_sem, row_ref[i], column_ref[i], i, True)

    if not fetched:
        for i in range(count):
            for copy in arrivals(i):
                copy.start()
    out_second[...] = before[...]
    placed = second[...]
    lead = swapped[4 * SLICE : 4 * SLICE + 1, :LANES]
    line_at = lax.broadcasted_iota(jnp.int32, placed.shape, 0)
    side_at = lax.broadcasted_iota(jnp.int32, placed.shape, 1) // SLICE
    for k in range(2):
        hot = hots[k, where_ref[0]]
        here = (line_at == hot // 2) & (side_at == hot % 2)
        placed = jnp.where(here, turned(lead, hot % 2 != k), placed)
    placed_second[...] = placed
    blocks = second.shape[0] // lines
    sharers = squares.shape[0] // blocks
    begin = 0
    for i in range(count):
        mine = parts[begin : begin + groups[i]]
        begin += groups[i]
        block = row_ref[i]
        total = jnp.sum(squares[pl.ds(block * sharers, sharers)], axis=0)[:lines]
        old = placed_second[pl.ds(block * lines, lines), :]
        fresh = beta_two * old + (1.0 - beta_two) * (total / full_width)
        out_second[pl.ds(block * lines, lines), :] = fresh
        scaled = jnp.sqrt(fresh / (1.0 - beta_two**8)) + eps_value
        rates = (learn_rate / (1.0 - beta_one**8)) / scaled
        if not fetched:
            for copy in arrivals(i):
                copy.wait()
            put_swapped(where_ref, hots, swapped, held, block, column_ref[i], i)
        at = 0
        for part in mine:
            for top in range(0, part.shape[0], LANES):
                line = at // LANES
                rate = jnp.broadcast_to(rates[line : line + 1, :], (LANES, LANES)).T
                span = slice(at, at + LANES)
                gradient = part[top : top + LANES, :]
                moment = beta_one * source[1, i, span, :] + (1.0 - beta_one) * gradient
                weight = source[0, i, span, :] - moment * rate
                held[1, i, span, :] = moment
                held[0, i, span, :] = weight
                at += LANES
        for copy in returns(i):
            copy.start()
    for i in range(count):
        for copy in returns(i):
            copy.wait()


def adam_blocks(rows_at, columns_at, parts, shape, full_width, common, before, held=None, fetched=None):
    groups = tuple(len(p) for p in parts)
    flat = [ref for p in parts for ref in p]
    where, hots, swapped, squares, table, first, second = common
    count = len(groups)
    more = [] if fetched is None else [fetched]
    n_in = 10 + len(flat) + len(more)
    size = shape[0] * shape[1]
    kept = [] if held is None else list(held)
    return pl.pallas_call(
        lambda *refs: adam_kernel(groups, full_width, fetched is not None, *refs),
        out_shape=(
            jax.ShapeDtypeStruct(table.shape, jnp.float32),
            jax.ShapeDtypeStruct(table.shape, jnp.float32),
            jax.ShapeDtypeStruct(second.shape, jnp.float32),
        ),
        in_specs=[SMEM] * 4
        + [VMEM] * (len(flat) + 2)
        + [ANY, ANY, VMEM, VMEM]
        + [VMEM] * len(more)
        + [HBM] * len(kept),
        out_specs=[HBM, HBM, VMEM],
        scratch_shapes=[
            pltpu.VMEM((2, count) + shape, jnp.float32),
            pltpu.SemaphoreType.DMA((2, count)),
            pltpu.SemaphoreType.DMA((2, count)),
            pltpu.VMEM(second.shape, jnp.float32),
        ],
        input_output_aliases={n_in: 0, n_in + 1: 1} if kept else {},
        compiler_params=pltpu.CompilerParams(vmem_limit_bytes=52 << 20),
        cost_estimate=pl.CostEstimate(
            flops=8 * count * size, bytes_accessed=20 * count * size, transcendentals=0
        ),
        name="adam_blocks",
    )(
        rows_at, columns_at, where, hots, *flat, swapped, squares, table, first, second, before,
        *more, *kept,
    )


def turned(row, wanted):
    return jnp.where(wanted, pltpu.roll(row, SLICE, 1), row)


def parcel_kernel(where_ref, hots, table, first, second, out_ref, sems):
    hot_ref = [hots[k, where_ref[0]] for k in range(2)]
    copies = []
    for which, source in enumerate((table, first)):
        for k in range(2):
            at = pl.ds(pl.multiple_of(hot_ref[k] * SLICE, SLICE), SLICE)
            to = pl.ds((2 * which + k) * SLICE, SLICE)
            copies.append(pltpu.make_async_copy(source.at[at, :], out_ref.at[to, :], sems.at[which, k]))
    for copy in copies:
        copy.start()
    left, right = (second[pl.ds(hot_ref[k] // 2, 1), :] for k in range(2))
    lane = lax.broadcasted_iota(jnp.int32, left.shape, 1)
    row = jnp.where(
        lane < SLICE, turned(left, hot_ref[0] % 2 == 1), turned(right, hot_ref[1] % 2 == 0)
    )
    out_ref[4 * SLICE :, :] = jnp.broadcast_to(
        jnp.concatenate([row, row], axis=1), (EXTRA, out_ref.shape[1])
    )
    for copy in copies:
        copy.wait()


def parcel_of(where, hots, table, first, second):
    return pl.pallas_call(
        parcel_kernel,
        out_shape=jax.ShapeDtypeStruct((4 * SLICE + EXTRA, table.shape[1]), jnp.float32),
        in_specs=[SMEM, SMEM, ANY, ANY, VMEM],
        out_specs=VMEM,
        scratch_shapes=[pltpu.SemaphoreType.DMA((2, 2))],
        compiler_params=pltpu.CompilerParams(vmem_limit_bytes=52 << 20),
        name="parcel",
    )(where, hots, table, first, second)


def on_device(
    table_weights,
    moment_first,
    moment_second,
    hot_slices,
    upstream_grad,
    dedup_map,
    unique_rows,
    row_counts,
):
    n_table = lax.axis_size("table")
    n_far, n_pair = lax.axis_size("far"), lax.axis_size("pair")
    n_dp = n_far * n_pair
    position = lax.axis_index("table")
    far_at, pair_at = lax.axis_index("far"), lax.axis_index("pair")
    rows_dev, col_width = table_weights.shape
    full_width = col_width * lax.axis_size("col")
    block, share = rows_dev // n_far, col_width // n_pair
    half = block // 2

    hots = hot_slices.T
    second_lines = moment_second.reshape(-1, LANES)
    slots = dedup_map.reshape(-1, GROUP * dedup_map.shape[1])
    slot_grad = slot_sums(
        slots, upstream_grad.T, hots, row_counts, unique_rows, n_pair, rows_dev
    )
    slot_grad, position, far_at, pair_at = lax.optimization_barrier(
        (slot_grad, position, far_at, pair_at)
    )
    got = lax.all_to_all(slot_grad, ("table", "pair"), split_axis=0, concat_axis=0, tiled=True)
    got, position, far_at, pair_at, second_lines = lax.optimization_barrier(
        (got, position, far_at, pair_at, second_lines)
    )

    def begin_at(*offsets):
        return jnp.stack([(far_at + o + n_far) % n_far * block for o in offsets]).astype(jnp.int32)

    def send(value, axes, count, step):
        return lax.ppermute(value, axes, [(i, (i + step) % count) for i in range(count)])

    pieces, aims, other = place_first(got, begin_at(2), block)
    rise = send(other[:half], "far", n_far, 1)
    fall = send(other[half:], "far", n_far, -1)
    plus, minus = place_next(pieces, aims, begin_at(1, -1), block)
    rise = jnp.concatenate([plus[:half] + rise, plus[half:]], axis=0)
    fall = jnp.concatenate([minus[:half], minus[half:] + fall], axis=0)
    where = position.reshape(1)
    rise, fall, where, second_lines = lax.optimization_barrier((rise, fall, where, second_lines))
    rise, fall = send(rise, "far", n_far, 1), send(fall, "far", n_far, -1)
    parcel = parcel_of(where, hots, table_weights, moment_first, second_lines)
    swapped = send(parcel, "table", n_table, n_table // 2)
    (mine,) = place_next(pieces, aims, begin_at(0), block)
    mine = mine + rise + fall
    mine, swapped = lax.optimization_barrier((mine, swapped))

    ring = ("far", "pair")
    me = far_at * n_pair + pair_at
    n_all = n_dp * lax.axis_size("col")
    own_squares = jnp.sum(mine * mine, axis=1).reshape(-1, LANES)
    own_squares = jnp.pad(own_squares, ((0, EXTRA - own_squares.shape[0]), (0, 0)))
    squares = lax.all_to_all(
        jnp.broadcast_to(own_squares[None], (n_all,) + own_squares.shape),
        ("far", "pair", "col"),
        split_axis=0,
        concat_axis=0,
        tiled=True,
    )
    common = (where, hots, swapped, squares, table_weights, moment_first, second_lines)
    shape = (block, share)

    def at_ring(offsets):
        at = jnp.stack([(me + o + n_dp) % n_dp for o in offsets]).astype(jnp.int32)
        return at // n_pair, at % n_pair

    def update(offsets, parts, second, held=None, fetched=None):
        return adam_blocks(*at_ring(offsets), parts, shape, full_width, common, second, held, fetched)

    rise, fall = send(mine, ring, n_dp, 1), send(mine, ring, n_dp, -1)
    parts = [[mine], [rise], [fall]]
    rise, fall = send(rise, ring, n_dp, 1), send(fall, ring, n_dp, -1)
    weights, first, second = update((0, -1, 1), parts, second_lines)
    rise, fall, second = lax.optimization_barrier((rise, fall, second))
    parts = [[rise], [fall]]
    rise, fall = send(rise, ring, n_dp, 1), send(fall, ring, n_dp, -1)
    fetched = fetch_block(*at_ring((4,)), shape, common)
    weights, first, second = update((-2, 2), parts, second, (weights, first))
    rise, fall, second, fetched = lax.optimization_barrier((rise, fall, second, fetched))
    parts = [[rise], [fall]]
    rise, fall = send(rise[:half], ring, n_dp, 1), send(fall[half:], ring, n_dp, -1)
    weights, first, second = update((-3, 3), parts, second, (weights, first))
    weights, first, second = update((4,), [[rise, fall]], second, (weights, first), fetched)
    return (weights, first, second.reshape(-1))


def solution(mesh):
    n_table, n_dp, n_col = (mesh.shape[a] for a in ("table", "dp", "col"))
    inner = Mesh(mesh.devices.reshape(n_table, n_dp // 2, 2, n_col), ("table", "far", "pair", "col"))
    samples = ("table", "far", "pair")
    placed = (
        P("table", "col"),
        P("table", "col"),
        P("table"),
        P(),
        P(samples, "col"),
        P(samples, None),
        P(samples, None, None),
        P(samples, None),
    )
    return jax.shard_map(
        on_device,
        mesh=inner,
        in_specs=placed,
        out_specs=(P("table", "col"), P("table", "col"), P("table")),
        check_vma=False,
    )
```

```python
import jax
import jax.numpy as jnp
from jax import lax
from jax.experimental import pallas as pl
from jax.experimental.pallas import tpu as pltpu
from jax.sharding import Mesh
from jax.sharding import PartitionSpec as P

SLICE = 64
CAP = 256
LOW = 128
GROUP = 8
EXTRA = 8
LANES = 128

beta_one = 0.9
beta_two = 0.99
learn_rate = 0.1
eps_value = 1e-08

NT = (((1,), (1,)), ((), ()))
VMEM = pl.BlockSpec(memory_space=pltpu.VMEM)
SMEM = pl.BlockSpec(memory_space=pltpu.SMEM)
HBM = pl.BlockSpec(memory_space=pltpu.HBM)
ANY = pl.BlockSpec(memory_space=pl.ANY)


def digits(values):
    return values.astype(jnp.float32).astype(jnp.bfloat16)


def counting(shape):
    return digits(lax.broadcasted_iota(jnp.int32, shape, 0))


def one_hot(positions, wanted):
    return jnp.where(positions == wanted, jnp.bfloat16(1), jnp.bfloat16(0))


def target_row(owner, hot_ref, count_ref, rows, rows_dev):
    n_hots, owners = hot_ref.shape
    partner = (owner + owners // 2) % owners
    local_row = rows % rows_dev
    from_partner = rows // rows_dev == partner
    target = local_row
    for k in range(n_hots):
        moved = from_partner & (local_row // SLICE == hot_ref[k, partner])
        target = jnp.where(moved, hot_ref[k, owner] * SLICE + local_row % SLICE, target)
    used = lax.broadcasted_iota(jnp.int32, rows.shape, 1) < count_ref[0, owner]
    return jnp.where(used, target, rows_dev)


def slot_kernel(rows_dev, map_ref, grad_ref, hot_ref, count_ref, rows_ref, out_ref, tally, held, sems):
    groups, span = map_ref.shape
    owners, _, cap = tally.shape
    per_owner = cap // LOW
    highs = owners * per_owner
    sample = lax.broadcasted_iota(jnp.int32, (1, span), 1) // (span // GROUP)
    left_at = counting((highs * GROUP, span))
    right_at = counting((LOW, span))
    batch = 32

    def count(step, carry):
        first = pl.multiple_of(step * batch, batch)
        slots = map_ref[pl.ds(first, batch), :]
        lefts = digits((slots // LOW) * GROUP + sample)
        rights = digits(slots % LOW)
        for pair in range(batch // 2):
            halves = []
            for at in (2 * pair, 2 * pair + 1):
                left = one_hot(left_at, lefts[at : at + 1, :])
                right = one_hot(right_at, rights[at : at + 1, :])
                part = lax.dot_general(left, right, NT, preferred_element_type=jnp.float32)
                halves.append(part.reshape(highs, GROUP, LOW))
            both = jnp.concatenate(halves, axis=1).astype(jnp.bfloat16)
            both = both.reshape(owners, per_owner, 2 * GROUP, LOW)
            begin = pl.multiple_of(first * GROUP + pair * 2 * GROUP, 2 * GROUP)
            for k in range(per_owner):
                tally[:, pl.ds(begin, 2 * GROUP), k * LOW : (k + 1) * LOW] = both[:, k]
        return carry

    lax.fori_loop(0, groups // batch, count, 0)
    depth, shares, height, lanes = held.shape
    columns = (height - EXTRA) * lanes // cap

    def leave(owner):
        slot = owner % depth
        at = pl.ds(owner * shares, shares)
        return pltpu.make_async_copy(held.at[slot], out_ref.at[at], sems.at[slot])

    for owner in range(owners):
        if owner >= depth:
            leave(owner - depth).wait()
        slot = owner % depth
        total = jnp.dot(grad_ref[...], tally[owner], preferred_element_type=jnp.float32)
        aim = target_row(owner, hot_ref, count_ref, rows_ref[0, owner : owner + 1, :], rows_dev)
        aim = jnp.broadcast_to(aim.astype(jnp.float32), (EXTRA, cap))
        for side in range(cap // lanes):
            cut = slice(side * lanes, (side + 1) * lanes)
            aim_at = height - EXTRA + side * EXTRA * lanes // cap
            for share in range(shares):
                part = total[share * columns : (share + 1) * columns, cut]
                held[slot, share, side * columns : (side + 1) * columns, :] = part
                held[slot, share, aim_at : aim_at + EXTRA * lanes // cap, :] = aim[: EXTRA * lanes // cap, cut]
        leave(owner).start()
    for owner in range(owners - depth, owners):
        leave(owner).wait()


def slot_sums(slots, grad_t, hot_slices, row_counts, unique_rows, shares, rows_dev):
    _, owners, cap = unique_rows.shape
    columns, samples = grad_t.shape
    height = columns // shares * cap // LANES + EXTRA
    depth = 4
    return pl.pallas_call(
        lambda *refs: slot_kernel(rows_dev, *refs),
        out_shape=jax.ShapeDtypeStruct((owners * shares, height, LANES), jnp.float32),
        in_specs=[VMEM, VMEM, SMEM, SMEM, VMEM],
        out_specs=HBM,
        scratch_shapes=[
            pltpu.VMEM((owners, samples, cap), jnp.bfloat16),
            pltpu.VMEM((depth, shares, height, LANES), jnp.float32),
            pltpu.SemaphoreType.DMA((depth,)),
        ],
        compiler_params=pltpu.CompilerParams(vmem_limit_bytes=50 << 20),
        name="slot_sums",
    )(slots, grad_t, hot_slices, row_counts, unique_rows)


def add_block(pieces, aims, start, out_ref, select):
    part, width = select.shape
    columns = out_ref.shape[1]
    place = counting((part, CAP))
    for top in range(0, out_ref.shape[0], part):
        for at in range(0, width, CAP):
            row = aims[:1, at : at + CAP] - (start + top)
            row = digits(jnp.where((row >= 0) & (row < part), row, -1))
            select[:, at : at + CAP] = one_hot(place, row)
        both = lax.dot_general(select[...], pieces[...], NT, preferred_element_type=jnp.float32)
        out_ref[top : top + part, :] = both[:, :columns] + both[:, columns:]


def place_first_kernel(start_ref, got_ref, pieces, aims, out_ref, select, held, sems):
    sources, height, lanes = got_ref.shape
    columns = (height - EXTRA) * lanes // CAP
    batch = sources // sems.shape[0]

    def fetch(k):
        at = pl.ds(k * batch, batch)
        return pltpu.make_async_copy(got_ref.at[at], held.at[at], sems.at[k])

    for k in range(sems.shape[0]):
        fetch(k).start()
    rows = out_ref.shape[0]
    place = counting((CAP, CAP))
    span = batch * CAP
    sums = [jnp.zeros((CAP, 2 * columns), jnp.float32) for _ in range(rows // CAP)]
    for k in range(sems.shape[0]):
        fetch(k).wait()
        for source in range(k * batch, (k + 1) * batch):
            for side in range(CAP // lanes):
                value = held[source, side * columns : (side + 1) * columns, :]
                upper = value.astype(jnp.bfloat16)
                lower = (value - upper.astype(jnp.float32)).astype(jnp.bfloat16)
                at = source * CAP + side * lanes
                pieces[:columns, at : at + lanes] = upper
                pieces[columns:, at : at + lanes] = lower
                aim_at = height - EXTRA + side * EXTRA * lanes // CAP
                aim = held[source, aim_at : aim_at + 1, :].astype(jnp.int32)
                aims[:, at : at + lanes] = jnp.broadcast_to(aim, (EXTRA, lanes))
        for part in range(rows // CAP):
            for at in range(k * span, (k + 1) * span, CAP):
                row = aims[:1, at : at + CAP] - (start_ref[0] + part * CAP)
                row = digits(jnp.where((row >= 0) & (row < CAP), row, -1))
                select[part * CAP : (part + 1) * CAP, at - k * span : at - k * span + CAP] = one_hot(
                    place, row
                )
            sums[part] += lax.dot_general(
                select[part * CAP : (part + 1) * CAP, :span],
                pieces[:, k * span : (k + 1) * span],
                NT,
                preferred_element_type=jnp.float32,
            )
    for part in range(rows // CAP):
        both = sums[part]
        out_ref[part * CAP : (part + 1) * CAP, :] = both[:, :columns] + both[:, columns:]


def place_next_kernel(start_ref, pieces, aims, *refs):
    outs, select = refs[:-1], refs[-1]
    for k, out_ref in enumerate(outs):
        add_block(pieces, aims, start_ref[k], out_ref, select)


def place_cost(blocks, block, width, columns):
    flops = 4 * blocks * block * width * columns
    return pl.CostEstimate(flops=flops, bytes_accessed=8 << 20, transcendentals=0)


def place_first(got, start, block):
    sources, height, lanes = got.shape
    columns = (height - EXTRA) * lanes // CAP
    width = sources * CAP
    return pl.pallas_call(
        place_first_kernel,
        out_shape=(
            jax.ShapeDtypeStruct((2 * columns, width), jnp.bfloat16),
            jax.ShapeDtypeStruct((EXTRA, width), jnp.int32),
            jax.ShapeDtypeStruct((block, columns), jnp.float32),
        ),
        in_specs=[SMEM, HBM],
        out_specs=[VMEM] * 3,
        scratch_shapes=[
            pltpu.VMEM((block, width // 8), jnp.bfloat16),
            pltpu.VMEM(got.shape, jnp.float32),
            pltpu.SemaphoreType.DMA((8,)),
        ],
        compiler_params=pltpu.CompilerParams(vmem_limit_bytes=46 << 20),
        cost_estimate=place_cost(1, block, width, columns),
        name="place_first",
    )(start, got)


def place_next(pieces, aims, starts, block):
    columns, width = pieces.shape[0] // 2, pieces.shape[1]
    count = starts.shape[0]
    return pl.pallas_call(
        place_next_kernel,
        out_shape=tuple(jax.ShapeDtypeStruct((block, columns), jnp.float32) for _ in range(count)),
        in_specs=[SMEM, VMEM, VMEM],
        out_specs=[VMEM] * count,
        scratch_shapes=[pltpu.VMEM((CAP, width), jnp.bfloat16)],
        compiler_params=pltpu.CompilerParams(vmem_limit_bytes=18 << 20),
        cost_estimate=place_cost(count, block, width, columns),
        name="place_next",
    )(starts, pieces, aims)


def block_copies(table, first, held, sems, rows_at, columns_at, i):
    rows, columns = held.shape[2:]
    at = pl.ds(pl.multiple_of(rows_at * rows, rows), rows)
    cut = pl.ds(pl.multiple_of(columns_at * columns, columns), columns)
    pairs = [(source.at[at, cut], held.at[which, i]) for which, source in enumerate((table, first))]
    return [pltpu.make_async_copy(a, b, sems.at[which, i]) for which, (a, b) in enumerate(pairs)]


def put_swapped(where_ref, hots, swapped, held, rows_at, columns_at, i):
    rows, columns = held.shape[2:]
    per_block = rows // SLICE
    for k in range(2):
        hot = hots[k, where_ref[0]]

        @pl.when(hot // per_block == rows_at)
        def _():
            at = pl.ds(pl.multiple_of((hot % per_block) * SLICE, SLICE), SLICE)
            cut = pl.ds(pl.multiple_of(columns_at * columns, columns), columns)
            for which in range(2):
                begin = (2 * which + k) * SLICE
                held[which, i, at, :] = swapped[begin : begin + SLICE, cut]


def fetch_kernel(row_ref, column_ref, where_ref, hots, swapped, table, first, held, sems):
    for copy in block_copies(table, first, held, sems, row_ref[0], column_ref[0], 0):
        copy.start()
    for copy in block_copies(table, first, held, sems, row_ref[0], column_ref[0], 0):
        copy.wait()
    put_swapped(where_ref, hots, swapped, held, row_ref[0], column_ref[0], 0)


def fetch_block(rows_at, columns_at, shape, common):
    where, hots, swapped, _, table, first, _ = common
    return pl.pallas_call(
        fetch_kernel,
        out_shape=jax.ShapeDtypeStruct((2, 1) + shape, jnp.float32),
        in_specs=[SMEM] * 4 + [VMEM, ANY, ANY],
        out_specs=VMEM,
        scratch_shapes=[pltpu.SemaphoreType.DMA((2, 1))],
        compiler_params=pltpu.CompilerParams(vmem_limit_bytes=52 << 20),
        name="fetch_block",
    )(rows_at, columns_at, where, hots, swapped, table, first)


def adam_kernel(groups, full_width, fetched, *refs):
    count = len(groups)
    row_ref, column_ref, where_ref, hots = refs[:4]
    parts = refs[4 : 4 + sum(groups)]
    swapped, squares, table, first, second, before = refs[4 + sum(groups) : 10 + sum(groups)]
    out_table, out_first, out_second, held, in_sem, out_sem, placed_second = refs[-7:]
    rows, columns = held.shape[2:]
    lines = rows // LANES
    source = refs[10 + sum(groups)] if fetched else held

    def arrivals(i):
        return block_copies(table, first, held, in_sem, row_ref[i], column_ref[i], i)

    def returns(i, line):
        at = pl.ds(pl.multiple_of(row_ref[i] * rows + line * LANES, LANES), LANES)
        cut = pl.ds(pl.multiple_of(column_ref[i] * columns, columns), columns)
        here = pl.ds(line * LANES, LANES)
        return [
            pltpu.make_async_copy(
                held.at[which, i, here], there.at[at, cut], out_sem.at[which, i * lines + line]
            )
            for which, there in enumerate((out_table, out_first))
        ]

    if not fetched:
        for i in range(count):
            for copy in arrivals(i):
                copy.start()
    out_second[...] = before[...]
    placed = second[...]
    lead = swapped[4 * SLICE : 4 * SLICE + 1, :LANES]
    line_at = lax.broadcasted_iota(jnp.int32, placed.shape, 0)
    side_at = lax.broadcasted_iota(jnp.int32, placed.shape, 1) // SLICE
    for k in range(2):
        hot = hots[k, where_ref[0]]
        here = (line_at == hot // 2) & (side_at == hot % 2)
        placed = jnp.where(here, turned(lead, hot % 2 != k), placed)
    placed_second[...] = placed
    blocks = second.shape[0] // lines
    sharers = squares.shape[0] // blocks
    begin = 0
    for i in range(count):
        mine = parts[begin : begin + groups[i]]
        begin += groups[i]
        block = row_ref[i]
        total = jnp.sum(squares[pl.ds(block * sharers, sharers)], axis=0)[:lines]
        old = placed_second[pl.ds(block * lines, lines), :]
        fresh = beta_two * old + (1.0 - beta_two) * (total / full_width)
        out_second[pl.ds(block * lines, lines), :] = fresh
        scaled = jnp.sqrt(fresh / (1.0 - beta_two**8)) + eps_value
        rates = (learn_rate / (1.0 - beta_one**8)) / scaled
        if not fetched:
            for copy in arrivals(i):
                copy.wait()
            put_swapped(where_ref, hots, swapped, held, block, column_ref[i], i)
        at = 0
        for part in mine:
            for top in range(0, part.shape[0], LANES):
                line = at // LANES
                rate = jnp.broadcast_to(rates[line : line + 1, :], (LANES, LANES)).T
                span = slice(at, at + LANES)
                gradient = part[top : top + LANES, :]
                moment = beta_one * source[1, i, span, :] + (1.0 - beta_one) * gradient
                weight = source[0, i, span, :] - moment * rate
                held[1, i, span, :] = moment
                held[0, i, span, :] = weight
                for copy in returns(i, line):
                    copy.start()
                at += LANES
    for i in range(count):
        for line in range(lines):
            for copy in returns(i, line):
                copy.wait()


def adam_blocks(rows_at, columns_at, parts, shape, full_width, common, before, held=None, fetched=None):
    groups = tuple(len(p) for p in parts)
    flat = [ref for p in parts for ref in p]
    where, hots, swapped, squares, table, first, second = common
    count = len(groups)
    more = [] if fetched is None else [fetched]
    n_in = 10 + len(flat) + len(more)
    size = shape[0] * shape[1]
    kept = [] if held is None else list(held)
    return pl.pallas_call(
        lambda *refs: adam_kernel(groups, full_width, fetched is not None, *refs),
        out_shape=(
            jax.ShapeDtypeStruct(table.shape, jnp.float32),
            jax.ShapeDtypeStruct(table.shape, jnp.float32),
            jax.ShapeDtypeStruct(second.shape, jnp.float32),
        ),
        in_specs=[SMEM] * 4
        + [VMEM] * (len(flat) + 2)
        + [ANY, ANY, VMEM, VMEM]
        + [VMEM] * len(more)
        + [HBM] * len(kept),
        out_specs=[HBM, HBM, VMEM],
        scratch_shapes=[
            pltpu.VMEM((2, count) + shape, jnp.float32),
            pltpu.SemaphoreType.DMA((2, count)),
            pltpu.SemaphoreType.DMA((2, count * shape[0] // LANES)),
            pltpu.VMEM(second.shape, jnp.float32),
        ],
        input_output_aliases={n_in: 0, n_in + 1: 1} if kept else {},
        compiler_params=pltpu.CompilerParams(vmem_limit_bytes=52 << 20),
        cost_estimate=pl.CostEstimate(
            flops=8 * count * size, bytes_accessed=20 * count * size, transcendentals=0
        ),
        name="adam_blocks",
    )(
        rows_at, columns_at, where, hots, *flat, swapped, squares, table, first, second, before,
        *more, *kept,
    )


def turned(row, wanted):
    return jnp.where(wanted, pltpu.roll(row, SLICE, 1), row)


def parcel_kernel(where_ref, hots, table, first, second, out_ref, sems):
    hot_ref = [hots[k, where_ref[0]] for k in range(2)]
    copies = []
    for which, source in enumerate((table, first)):
        for k in range(2):
            at = pl.ds(pl.multiple_of(hot_ref[k] * SLICE, SLICE), SLICE)
            to = pl.ds((2 * which + k) * SLICE, SLICE)
            copies.append(pltpu.make_async_copy(source.at[at, :], out_ref.at[to, :], sems.at[which, k]))
    for copy in copies:
        copy.start()
    left, right = (second[pl.ds(hot_ref[k] // 2, 1), :] for k in range(2))
    lane = lax.broadcasted_iota(jnp.int32, left.shape, 1)
    row = jnp.where(
        lane < SLICE, turned(left, hot_ref[0] % 2 == 1), turned(right, hot_ref[1] % 2 == 0)
    )
    out_ref[4 * SLICE :, :] = jnp.broadcast_to(
        jnp.concatenate([row, row], axis=1), (EXTRA, out_ref.shape[1])
    )
    for copy in copies:
        copy.wait()


def parcel_of(where, hots, table, first, second):
    return pl.pallas_call(
        parcel_kernel,
        out_shape=jax.ShapeDtypeStruct((4 * SLICE + EXTRA, table.shape[1]), jnp.float32),
        in_specs=[SMEM, SMEM, ANY, ANY, VMEM],
        out_specs=VMEM,
        scratch_shapes=[pltpu.SemaphoreType.DMA((2, 2))],
        compiler_params=pltpu.CompilerParams(vmem_limit_bytes=52 << 20),
        name="parcel",
    )(where, hots, table, first, second)


def on_device(
    table_weights,
    moment_first,
    moment_second,
    hot_slices,
    upstream_grad,
    dedup_map,
    unique_rows,
    row_counts,
):
    n_table = lax.axis_size("table")
    n_far, n_pair = lax.axis_size("far"), lax.axis_size("pair")
    n_dp = n_far * n_pair
    position = lax.axis_index("table")
    far_at, pair_at = lax.axis_index("far"), lax.axis_index("pair")
    rows_dev, col_width = table_weights.shape
    full_width = col_width * lax.axis_size("col")
    block, share = rows_dev // n_far, col_width // n_pair
    half = block // 2

    hots = hot_slices.T
    second_lines = moment_second.reshape(-1, LANES)
    slots = dedup_map.reshape(-1, GROUP * dedup_map.shape[1])
    slot_grad = slot_sums(
        slots, upstream_grad.T, hots, row_counts, unique_rows, n_pair, rows_dev
    )
    slot_grad, position, far_at, pair_at = lax.optimization_barrier(
        (slot_grad, position, far_at, pair_at)
    )
    got = lax.all_to_all(slot_grad, ("table", "pair"), split_axis=0, concat_axis=0, tiled=True)
    got, position, far_at, pair_at, second_lines = lax.optimization_barrier(
        (got, position, far_at, pair_at, second_lines)
    )

    def begin_at(*offsets):
        return jnp.stack([(far_at + o + n_far) % n_far * block for o in offsets]).astype(jnp.int32)

    def send(value, axes, count, step):
        return lax.ppermute(value, axes, [(i, (i + step) % count) for i in range(count)])

    pieces, aims, other = place_first(got, begin_at(2), block)
    rise = send(other[:half], "far", n_far, 1)
    fall = send(other[half:], "far", n_far, -1)
    plus, minus = place_next(pieces, aims, begin_at(1, -1), block)
    rise = jnp.concatenate([plus[:half] + rise, plus[half:]], axis=0)
    fall = jnp.concatenate([minus[:half], minus[half:] + fall], axis=0)
    where = position.reshape(1)
    rise, fall, where, second_lines = lax.optimization_barrier((rise, fall, where, second_lines))
    rise, fall = send(rise, "far", n_far, 1), send(fall, "far", n_far, -1)
    parcel = parcel_of(where, hots, table_weights, moment_first, second_lines)
    swapped = send(parcel, "table", n_table, n_table // 2)
    (mine,) = place_next(pieces, aims, begin_at(0), block)
    mine = mine + rise + fall
    mine, swapped = lax.optimization_barrier((mine, swapped))

    ring = ("far", "pair")
    me = far_at * n_pair + pair_at
    n_all = n_dp * lax.axis_size("col")
    own_squares = jnp.sum(mine * mine, axis=1).reshape(-1, LANES)
    own_squares = jnp.pad(own_squares, ((0, EXTRA - own_squares.shape[0]), (0, 0)))
    squares = lax.all_to_all(
        jnp.broadcast_to(own_squares[None], (n_all,) + own_squares.shape),
        ("far", "pair", "col"),
        split_axis=0,
        concat_axis=0,
        tiled=True,
    )
    common = (where, hots, swapped, squares, table_weights, moment_first, second_lines)
    shape = (block, share)

    def at_ring(offsets):
        at = jnp.stack([(me + o + n_dp) % n_dp for o in offsets]).astype(jnp.int32)
        return at // n_pair, at % n_pair

    def update(offsets, parts, second, held=None, fetched=None):
        return adam_blocks(*at_ring(offsets), parts, shape, full_width, common, second, held, fetched)

    rise, fall = send(mine, ring, n_dp, 1), send(mine, ring, n_dp, -1)
    parts = [[mine], [rise], [fall]]
    rise, fall = send(rise, ring, n_dp, 1), send(fall, ring, n_dp, -1)
    weights, first, second = update((0, -1, 1), parts, second_lines)
    rise, fall, second = lax.optimization_barrier((rise, fall, second))
    parts = [[rise], [fall]]
    rise, fall = send(rise, ring, n_dp, 1), send(fall, ring, n_dp, -1)
    fetched = fetch_block(*at_ring((4,)), shape, common)
    weights, first, second = update((-2, 2), parts, second, (weights, first))
    rise, fall, second, fetched = lax.optimization_barrier((rise, fall, second, fetched))
    parts = [[rise], [fall]]
    rise, fall = send(rise[:half], ring, n_dp, 1), send(fall[half:], ring, n_dp, -1)
    weights, first, second = update((-3, 3), parts, second, (weights, first))
    weights, first, second = update((4,), [[rise, fall]], second, (weights, first), fetched)
    return (weights, first, second.reshape(-1))


def solution(mesh):
    n_table, n_dp, n_col = (mesh.shape[a] for a in ("table", "dp", "col"))
    inner = Mesh(mesh.devices.reshape(n_table, n_dp // 2, 2, n_col), ("table", "far", "pair", "col"))
    samples = ("table", "far", "pair")
    placed = (
        P("table", "col"),
        P("table", "col"),
        P("table"),
        P(),
        P(samples, "col"),
        P(samples, None),
        P(samples, None, None),
        P(samples, None),
    )
    return jax.shard_map(
        on_device,
        mesh=inner,
        in_specs=placed,
        out_specs=(P("table", "col"), P("table", "col"), P("table")),
        check_vma=False,
    )
```
